32 devices in a mesh: dp: 8 (over y, x, core), tensor: 4 (over z).
Axes of the slice: x: 2, y: 2, z: 4, core: 2. Of those that a mesh axis runs over, the one named last changes fastest.
Arguments:
- hidden_in: bfloat16 [32768, 768], P('dp'), may hold values from -6 to 6
- lengths: int32 [8], P('dp'), may hold values from 1024 to 4096, as said below
- labels: int32 [8], P('dp'), may hold values from 0 to 13
- out_cotangent: bfloat16 [32768, 768], P('dp'), may hold values from -6 to 6
- w_query: bfloat16 [768, 768], P(None, 'tensor'), may hold values from -0.21875 to 0.21875
- b_query: float32 [768], P('tensor'), may hold values from -1.75 to 1.75
- w_key: bfloat16 [768, 768], P(None, 'tensor'), may hold values from -0.21875 to 0.21875
- w_value: bfloat16 [768, 768], P(None, 'tensor'), may hold values from -0.21875 to 0.21875
- b_value: float32 [768], P('tensor'), may hold values from -1.75 to 1.75
- w_out: bfloat16 [768, 768], P('tensor'), may hold values from -6 to 6
- b_out: float32 [768], replicated, may hold values from -1.75 to 1.75
- ln1_gain: float32 [768], replicated, may hold values from 0.5 to 1.5
- ln1_bias: float32 [768], replicated, may hold values from -1.75 to 1.75
- w_in: bfloat16 [768, 3072], P(None, 'tensor'), may hold values from -0.21875 to 0.21875
- b_in: bfloat16 [3072], P('tensor'), may hold values from -1.75 to 1.75
- w_down: bfloat16 [3072, 768], P('tensor'), may hold values from -0.109375 to 0.109375
- b_down: float32 [768], replicated, may hold values from -1.75 to 1.75
- ln2_gain: float32 [768], replicated, may hold values from 0.5 to 1.5
- ln2_bias: float32 [768], replicated, may hold values from -1.75 to 1.75
- w_student: bfloat16 [768, 128], P(None, 'tensor'), may hold values from -0.21875 to 0.21875
- b_student: bfloat16 [128], P('tensor'), may hold values from -1.75 to 1.75
- pool_query: float32 [128], replicated, may hold values from -8 to 8
- w_pool: float32 [128, 128], replicated, may hold values from -0.5 to 0.5
- b_pool: float32 [128], replicated, may hold values from -1.75 to 1.75
- w_class: float32 [128, 14], replicated, may hold values from -1 to 1
- b_class: float32 [14], replicated, may hold values from -1.75 to 1.75
Outputs:
- hidden_out: bfloat16 [32768, 768], P('dp')
- logits: float32 [8, 14], P('dp')
- grad_in: bfloat16 [32768, 768], P('dp')
- grad_w_query: float32 [768, 768], P(None, 'tensor')
- grad_b_query: float32 [768], P('tensor')
- grad_w_key: float32 [768, 768], P(None, 'tensor')
- grad_w_value: float32 [768, 768], P(None, 'tensor')
- grad_b_value: float32 [768], P('tensor')
- grad_w_out: float32 [768, 768], P('tensor')
- grad_b_out: float32 [768], replicated
- grad_ln1_gain: float32 [768], replicated
- grad_ln1_bias: float32 [768], replicated
- grad_w_in: float32 [768, 3072], P(None, 'tensor')
- grad_b_in: float32 [3072], P('tensor')
- grad_w_down: float32 [3072, 768], P('tensor')
- grad_b_down: float32 [768], replicated
- grad_ln2_gain: float32 [768], replicated
- grad_ln2_bias: float32 [768], replicated
- grad_w_student: float32 [768, 128], P(None, 'tensor')
- grad_b_student: float32 [128], P('tensor')
- grad_pool_query: float32 [128], replicated
- grad_w_pool: float32 [128, 128], replicated
- grad_b_pool: float32 [128], replicated
- grad_w_class: float32 [128, 14], replicated
- grad_b_class: float32 [14], replicated
The draws below stay inside these ranges and needn't reach their ends.
Inputs may be any that keep to these rules, and one draw needn't show every extreme that they name: Slot s holds one sequence in its first lengths[s] positions; some slot has all 4096 positions valid and some other has exactly 1024.
All inputs are finite; a program needn't handle non-finite values.
Results may differ from the reference program's by a relative error of at most 0.023.
Values may be sent and summed in bfloat16 or wider, within the bound.
No kernel may reach another device: no remote copies, remote signals or barrier semaphores. Data moves between devices by JAX's collectives and lax.ppermute only.
A program may use at most 256 MiB of HBM per device.

```python
import math
import jax
import jax.numpy as jnp
from jax import lax

D = 768
HEADS = 12
HD = 64
FF = 3072
STU = 128
POOL_HEADS = 2
CLASSES = 14
SLOT = 4096
MIN_LEN = 1024
SEQS = 8
TOKENS = 32768


def draw_lengths(key, part):
    base_key = jax.random.fold_in(key, 11)
    pick_key = jax.random.fold_in(key, 12)
    other_key = jax.random.fold_in(key, 13)
    drawn = jax.random.randint(base_key, (SEQS,), MIN_LEN, SLOT + 1, dtype=jnp.int32)
    chosen = jax.random.randint(pick_key, (), 0, SEQS, dtype=jnp.int32)
    offset = jax.random.randint(other_key, (), 1, SEQS, dtype=jnp.int32)
    shortest = (chosen + offset) % SEQS
    slots = jnp.arange(SEQS, dtype=jnp.int32)
    drawn = jnp.where(slots == chosen, SLOT, drawn)
    return jnp.where(slots == shortest, MIN_LEN, drawn)


def with_ends(entries, own_key, low, top_value):
    longest = entries.shape.index(max(entries.shape))
    spots = []
    for shift in (0, 1):
        where = [jax.random.randint(jax.random.fold_in(own_key, axis), (), 0, length) for axis, length in enumerate(entries.shape)]
        where[longest] = (where[longest] + shift) % entries.shape[longest]
        spots.append(tuple(where))
    return entries.at[spots[0]].set(low).at[spots[1]].set(top_value)


def block_levels(key, extent, split, least, largest):
    level = 1.0
    for axis_at, parts in split:
        heights = jax.random.uniform(jax.random.fold_in(jax.random.fold_in(key, 6), axis_at), (parts,), jnp.float32, least / len(split), largest / len(split))
        level = level * jnp.repeat(jnp.exp(heights), extent[axis_at] // parts).reshape((-1,) + (1,) * (len(extent) - 1 - axis_at))
    return level


def gaussian(rng, dims, spread, reach, shards=(), kind=jnp.bfloat16):
    entries = jax.random.normal(rng, dims, jnp.float32) * spread
    if len(shards) > 0:
        entries = block_levels(rng, dims, shards, -0.22, 0.18) * entries
    return jnp.clip(entries, min=-reach, max=reach).astype(kind)


def setup_inputs(seed: int = 0) -> dict:
    key_list = jax.random.split(jax.random.key(seed), 27)
    hidden_in = gaussian(key_list[0], (TOKENS, D), 1.0, 6.0, ((0, 8),))
    lengths = draw_lengths(jax.random.fold_in(key_list[26], 71), 0)
    labels = with_ends(jax.random.randint(key_list[2], (SEQS,), 0, CLASSES), jax.random.fold_in(key_list[2], 1), 0, CLASSES - 1).astype(jnp.int32)
    out_cotangent = gaussian(key_list[3], (TOKENS, D), 1.0, 6.0, ((0, 8),))
    w_query = gaussian(key_list[4], (D, D), D ** -0.5, 0.21875, ((1, 4),))
    b_query = gaussian(key_list[5], (D,), 0.3, 1.75, ((0, 4),), jnp.float32)
    w_key = gaussian(key_list[6], (D, D), D ** -0.5, 0.21875, ((1, 4),))
    w_value = gaussian(key_list[7], (D, D), D ** -0.5, 0.21875, ((1, 4),))
    b_value = gaussian(key_list[8], (D,), 0.3, 1.75, ((0, 4),), jnp.float32)
    w_out = gaussian(key_list[9], (D, D), (max(1, 3 * D // SLOT)) ** -0.5, 6.0, ((0, 4),))
    b_out = gaussian(key_list[10], (D,), 0.3, 1.75, (), jnp.float32)
    ln1_gain = jnp.clip(1.0 + 0.1 * jax.random.normal(key_list[11], (D,), jnp.float32), 0.5, 1.5)
    ln1_bias = gaussian(key_list[12], (D,), 0.3, 1.75, (), jnp.float32)
    w_in = gaussian(key_list[13], (D, FF), D ** -0.5, 0.21875, ((1, 4),))
    b_in = gaussian(key_list[14], (FF,), 0.3, 1.75, ((0, 4),))
    w_down = gaussian(key_list[15], (FF, D), FF ** -0.5, 0.109375, ((0, 4),))
    b_down = gaussian(key_list[16], (D,), 0.3, 1.75, (), jnp.float32)
    ln2_gain = jnp.clip(1.0 + 0.1 * jax.random.normal(key_list[17], (D,), jnp.float32), 0.5, 1.5)
    ln2_bias = gaussian(key_list[18], (D,), 0.3, 1.75, (), jnp.float32)
    w_student = gaussian(key_list[19], (D, STU), D ** -0.5, 0.21875, ((1, 4),))
    b_student = gaussian(key_list[20], (STU,), 0.3, 1.75, ((0, 4),))
    pool_query = gaussian(key_list[21], (STU,), 1.5, 8.0, (), jnp.float32)
    w_pool = gaussian(key_list[22], (STU, STU), STU ** -0.5, 0.5, (), jnp.float32)
    b_pool = gaussian(key_list[23], (STU,), 0.3, 1.75, (), jnp.float32)
    w_class = gaussian(key_list[24], (STU, CLASSES), (STU // 4) ** -0.5, 1.0, (), jnp.float32)
    b_class = gaussian(key_list[25], (CLASSES,), 0.3, 1.75, (), jnp.float32)
    return dict(hidden_in=hidden_in, lengths=lengths, labels=labels, out_cotangent=out_cotangent, w_query=w_query, b_query=b_query, w_key=w_key, w_value=w_value, b_value=b_value, w_out=w_out, b_out=b_out, ln1_gain=ln1_gain, ln1_bias=ln1_bias, w_in=w_in, b_in=b_in, w_down=w_down, b_down=b_down, ln2_gain=ln2_gain, ln2_bias=ln2_bias, w_student=w_student, b_student=b_student, pool_query=pool_query, w_pool=w_pool, b_pool=b_pool, w_class=w_class, b_class=b_class)


@jax.custom_vjp
def low(v):
    return lax.optimization_barrier(v.astype(jnp.bfloat16)).astype(jnp.float32)

@jax.custom_vjp
def low_back(v):
    return v

def low_keep(v):
    return (low(v), None)

def low_pass(kept, grad):
    return (grad,)

def back_keep(v):
    return (v, None)

def back_low(kept, grad):
    return (low(grad),)
low.defvjp(low_keep, low_pass)
low_back.defvjp(back_keep, back_low)
epsilon = 1e-06
mask_fill = -1e+30
highest = lax.Precision.HIGHEST

def rounded_both(values):
    return low(low_back(values))

def product(left, right):
    return jnp.dot(left, right, precision=highest)

def normalize(resid, gain, shift):
    center = resid - lax.optimization_barrier(jnp.mean(resid, axis=-1, keepdims=True))
    invstd = lax.rsqrt(lax.optimization_barrier(jnp.mean(center * center, axis=-1, keepdims=True)) + epsilon)
    normed = center * invstd
    return normed * gain + shift

def student_tail(student, valid_keys, labels, pool_query, w_pool, b_pool, w_class, b_class):
    seq_count, slot_len, student_width = student.shape
    head_width = student_width // POOL_HEADS
    split_heads = student.reshape(seq_count, slot_len, POOL_HEADS, head_width)
    probes = pool_query.reshape(POOL_HEADS, head_width)
    scores = jnp.einsum('nthd,hd->nht', split_heads, probes, precision=highest) * (1.0 / math.sqrt(head_width))
    scores = jnp.where(valid_keys[:, None, :], scores, mask_fill)
    weights = jax.nn.softmax(scores, axis=-1)
    pooled = jnp.einsum('nht,nthd->nhd', weights, split_heads, precision=highest).reshape(seq_count, student_width)
    squashed = jnp.tanh(jnp.dot(pooled, w_pool, precision=highest) + b_pool)
    logits = jnp.dot(squashed, w_class, precision=highest) + b_class
    classes = jnp.arange(logits.shape[1], dtype=jnp.int32)
    picked = lax.optimization_barrier(jnp.sum(jnp.where(classes[None, :] == labels[:, None], logits, 0.0), axis=1))
    return (jnp.sum(jax.nn.logsumexp(logits, axis=1) - picked), logits)

def sequence_objective(params, hidden, cotangent, length, label):
    w_query, b_query, w_key, w_value, b_value, w_out, b_out, ln1_gain, ln1_bias, w_in, b_in, w_down, b_down, ln2_gain, ln2_bias, w_student, b_student, pool_query, w_pool, b_pool, w_class, b_class = params
    valid_keys = jnp.arange(SLOT, dtype=jnp.int32) < length
    queries = rounded_both(product(hidden, w_query) + b_query).reshape(SLOT, HEADS, HD)
    keys = rounded_both(product(hidden, w_key)).reshape(SLOT, HEADS, HD)
    values = rounded_both(product(hidden, w_value) + b_value).reshape(SLOT, HEADS, HD)
    score_scale = 1.0 / math.sqrt(HD)
    block_len = min(512, SLOT)

    def attend_block(query_block):
        scores = low_back(jnp.einsum('qhd,khd->hqk', query_block, keys, precision=highest) * score_scale)
        scores = jnp.where(valid_keys[None, None, :], scores, mask_fill)
        probs = jax.nn.softmax(scores, axis=-1)
        return jnp.einsum('hqk,khd->qhd', low(probs), values, precision=highest)
    attended = lax.map(jax.checkpoint(attend_block), queries.reshape(SLOT // block_len, block_len, HEADS, HD))
    attended = rounded_both(attended.reshape(SLOT, D))
    resid1 = low_back(product(attended, w_out)) + b_out + hidden
    first = low(normalize(resid1, ln1_gain, ln1_bias))
    pre = low_back(product(first, w_in) + b_in)
    act = low(jax.nn.gelu(pre, approximate=False))
    resid2 = low_back(product(act, w_down)) + b_down + first
    second = low(normalize(resid2, ln2_gain, ln2_bias))
    student = rounded_both(product(second, w_student) + b_student)
    seq_loss, logits = student_tail(student[None], valid_keys[None], label[None], pool_query, w_pool, b_pool, w_class, b_class)
    valid_rows = valid_keys.astype(jnp.float32)[:, None]
    objective = jnp.sum(second * cotangent * valid_rows) + seq_loss
    return (objective, (second, logits[0]))

def reference(hidden_in, lengths, labels, out_cotangent, w_query, b_query, w_key, w_value, b_value, w_out, b_out, ln1_gain, ln1_bias, w_in, b_in, w_down, b_down, ln2_gain, ln2_bias, w_student, b_student, pool_query, w_pool, b_pool, w_class, b_class):
    params = tuple((p.astype(jnp.float32) for p in (w_query, b_query, w_key, w_value, b_value, w_out, b_out, ln1_gain, ln1_bias, w_in, b_in, w_down, b_down, ln2_gain, ln2_bias, w_student, b_student, pool_query, w_pool, b_pool, w_class, b_class)))
    hidden = hidden_in.astype(jnp.float32).reshape(SEQS, SLOT, D)
    cotangents = out_cotangent.astype(jnp.float32).reshape(SEQS, SLOT, D)

    def one_sequence(totals, seq_item):
        hidden_seq, cot_seq, length, label = seq_item

        def objective(param_set, hidden_rows):
            return sequence_objective(param_set, hidden_rows, cot_seq, length, label)
        value, backward, extras = jax.vjp(objective, params, hidden_seq, has_aux=True)
        grads, grad_hidden = backward(jnp.ones_like(value))
        totals = tuple((total + grad for total, grad in zip(totals, grads)))
        return (totals, (extras[0].astype(jnp.bfloat16), extras[1], grad_hidden.astype(jnp.bfloat16)))
    initial = tuple((jnp.zeros_like(p) for p in params))
    totals, (outputs, logits, grads_in) = lax.scan(one_sequence, initial, (hidden, cotangents, lengths, labels))
    return (outputs.reshape(TOKENS, D), logits, grads_in.reshape(TOKENS, D), totals[0], totals[1], totals[2], totals[3], totals[4], totals[5], totals[6], totals[7], totals[8], totals[9], totals[10], totals[11], totals[12], totals[13], totals[14], totals[15], totals[16], totals[17], totals[18], totals[19], totals[20], totals[21])
```

```python
import functools
import math

import jax
import jax.numpy as jnp
from jax import lax
from jax.experimental import pallas as pl
from jax.experimental.pallas import tpu as pltpu
from jax.sharding import PartitionSpec as P

HD = 64
POOL_HEADS = 2

epsilon = 1e-06
mask_fill = -1e30
highest = lax.Precision.HIGHEST
bf16 = jnp.bfloat16
f32 = jnp.float32
SCORE_SCALE = 1.0 / math.sqrt(HD)
SCORE_SCALE_2 = math.log2(math.e) * SCORE_SCALE
PLANE = 256
VMEM_LIMIT = 60 * 1024 * 1024


def matmul(left, right):
    return jnp.dot(left, right, preferred_element_type=f32)


def across_rows(left, right):
    return lax.dot_general(left, right, (((0,), (0,)), ((), ())), preferred_element_type=f32)


def against(left, right):
    return lax.dot_general(left, right, (((1,), (1,)), ((), ())), preferred_element_type=f32)


def widen_keys(wide_ref, narrow_ref, length):
    rows, width = narrow_ref.shape
    wide_ref[:, :width] = narrow_ref[...]
    row = lax.broadcasted_iota(jnp.int32, (rows, PLANE - width), 0)
    lane = lax.broadcasted_iota(jnp.int32, (rows, PLANE - width), 1)
    wide_ref[:, width:] = jnp.where((lane == 0) & (row >= length), mask_fill, 0.0).astype(bf16)


def forward_kernel(
    bq, bk, heads, length_ref, k_ref, qt_ref, vt_ref, ot_ref, lse_ref, wide_k, head_q, acc
):
    width = k_ref.shape[1]
    length = length_ref[0]
    key_blocks = (length + bk - 1) // bk
    widen_keys(wide_k, k_ref, length)
    row = lax.broadcasted_iota(jnp.int32, (PLANE, bq), 0)
    for h in range(heads):
        head_q[h] = jnp.where(row == width, 1.0, 0.0).astype(bf16)

    def query_step(qb, unused):
        q0 = pl.multiple_of(qb * bq, bq)
        for h in range(heads):
            own = slice(HD * h, HD * h + HD)
            head_q[h, own, :] = qt_ref[own, pl.ds(q0, bq)]
        acc[...] = jnp.zeros_like(acc)

        def key_step(kb, carry):
            k0 = pl.multiple_of(kb * bk, bk)
            keys = wide_k[pl.ds(k0, bk), :]
            scores = [matmul(keys, head_q[h]) for h in range(heads)]
            kept = []
            for h in range(heads):
                top, total = carry[h]
                new_top = jnp.maximum(
                    top, jnp.max(scores[h], axis=0, keepdims=True) * SCORE_SCALE_2
                )
                weights = jnp.exp2(scores[h] * SCORE_SCALE_2 - new_top)
                fade = jnp.exp2(top - new_top)
                total = fade * total + jnp.sum(weights, axis=0, keepdims=True)
                values_t = vt_ref[HD * h : HD * h + HD, pl.ds(k0, bk)]
                acc[h] = fade * acc[h] + matmul(values_t, weights.astype(bf16))
                kept.append((new_top, total))
            return tuple(kept)

        start = tuple(
            (jnp.full((1, bq), mask_fill, f32), jnp.zeros((1, bq), f32)) for _ in range(heads)
        )
        done = lax.fori_loop(0, key_blocks, key_step, start)
        for h in range(heads):
            top, total = done[h]
            ot_ref[HD * h : HD * h + HD, pl.ds(q0, bq)] = (acc[h] * (1.0 / total)).astype(bf16)
            lse_ref[pl.ds(h, 1), pl.ds(q0, bq)] = top + jnp.log2(total)
        return unused

    lax.fori_loop(0, qt_ref.shape[1] // bq, query_step, 0)


def attend_forward(length, keys, queries_t, values_t):
    slot_len, width = keys.shape
    heads = width // HD
    query_count = queries_t.shape[1]
    bq, bk = min(512, query_count), min(2048, slot_len)
    vmem = pl.BlockSpec(memory_space=pltpu.VMEM)
    pairs = heads * query_count * slot_len
    return pl.pallas_call(
        functools.partial(forward_kernel, bq, bk, heads),
        out_shape=(
            jax.ShapeDtypeStruct((width, query_count), bf16),
            jax.ShapeDtypeStruct((8, query_count), f32),
        ),
        in_specs=[pl.BlockSpec(memory_space=pltpu.SMEM)] + [vmem] * 3,
        out_specs=[vmem] * 2,
        scratch_shapes=[
            pltpu.VMEM((slot_len, PLANE), bf16),
            pltpu.VMEM((heads, PLANE, bq), bf16),
            pltpu.VMEM((heads, HD, bq), f32),
        ],
        compiler_params=pltpu.CompilerParams(vmem_limit_bytes=VMEM_LIMIT),
        cost_estimate=pl.CostEstimate(
            flops=4 * HD * pairs * 4, bytes_accessed=slot_len * width * 8, transcendentals=pairs
        ),
        name="attend_forward",
    )(length, keys, queries_t, values_t)


def backward_kernel(
    bq,
    bk,
    heads,
    length_ref,
    k_ref,
    kt_ref,
    v_ref,
    qt_ref,
    got_ref,
    ot_ref,
    lse_ref,
    gqt_ref,
    gk_ref,
    gv_ref,
    wide_k,
    wide_v,
    head_q,
    head_go,
    gq_acc,
    gk_acc,
    gv_acc,
):
    rows, width = k_ref.shape
    length = length_ref[0]
    key_blocks = (length + bk - 1) // bk
    query_blocks = (length + bq - 1) // bq
    widen_keys(wide_k, k_ref, length)
    wide_v[:, :width] = v_ref[...]
    wide_v[:, width:] = jnp.zeros((rows, PLANE - width), bf16)
    row = lax.broadcasted_iota(jnp.int32, (PLANE, bq), 0)
    for h in range(heads):
        head_q[h] = jnp.where(row == width, 1.0, 0.0).astype(bf16)
        head_go[h] = jnp.zeros((PLANE, bq), bf16)
    gk_acc[...] = jnp.zeros_like(gk_acc)
    gv_acc[...] = jnp.zeros_like(gv_acc)
    gqt_ref[...] = jnp.zeros_like(gqt_ref)

    def query_step(qb, unused):
        q0 = pl.multiple_of(qb * bq, bq)
        span = pl.ds(q0, bq)
        deltas = []
        for h in range(heads):
            own = slice(HD * h, HD * h + HD)
            head_q[h, own, :] = qt_ref[own, span]
            grad_out = got_ref[own, span]
            head_go[h, own, :] = grad_out
            deltas.append(
                jnp.sum(
                    grad_out.astype(f32) * ot_ref[own, span].astype(f32), axis=0, keepdims=True
                )
            )
        gq_acc[...] = jnp.zeros_like(gq_acc)

        def key_step(kb, inner):
            k0 = pl.multiple_of(kb * bk, bk)
            keys = wide_k[pl.ds(k0, bk), :]
            values = wide_v[pl.ds(k0, bk), :]
            grad_v = None
            grad_k = None
            for h in range(heads):
                scores = matmul(keys, head_q[h])
                grad_weights = matmul(values, head_go[h])
                weights = jnp.exp2(scores * SCORE_SCALE_2 - lse_ref[pl.ds(h, 1), span])
                grad_scores = (weights * (grad_weights - deltas[h])).astype(bf16)
                more_v = against(weights.astype(bf16), head_go[h])
                more_k = against(grad_scores, head_q[h])
                grad_v = more_v if grad_v is None else grad_v + more_v
                grad_k = more_k if grad_k is None else grad_k + more_k
                gq_acc[h] += matmul(kt_ref[HD * h : HD * h + HD, pl.ds(k0, bk)], grad_scores)
            gk_acc[pl.ds(k0, bk), :] += grad_k
            gv_acc[pl.ds(k0, bk), :] += grad_v
            return inner

        lax.fori_loop(0, key_blocks, key_step, 0)
        for h in range(heads):
            gqt_ref[HD * h : HD * h + HD, span] = (gq_acc[h] * SCORE_SCALE).astype(bf16)
        return unused

    lax.fori_loop(0, query_blocks, query_step, 0)
    gk_ref[...] = (gk_acc[:, :width] * SCORE_SCALE).astype(bf16)
    gv_ref[...] = gv_acc[:, :width].astype(bf16)


def attend_backward(length, keys, keys_t, values, queries_t, grad_out_t, out_t, lse):
    slot_len, width = keys.shape
    heads = width // HD
    bq, bk = min(512, slot_len), min(1024, slot_len)
    vmem = pl.BlockSpec(memory_space=pltpu.VMEM)
    pairs = heads * slot_len * slot_len
    return pl.pallas_call(
        functools.partial(backward_kernel, bq, bk, heads),
        out_shape=(
            jax.ShapeDtypeStruct((width, slot_len), bf16),
            jax.ShapeDtypeStruct((slot_len, width), bf16),
            jax.ShapeDtypeStruct((slot_len, width), bf16),
        ),
        in_specs=[pl.BlockSpec(memory_space=pltpu.SMEM)] + [vmem] * 7,
        out_specs=[vmem] * 3,
        scratch_shapes=[
            pltpu.VMEM((slot_len, PLANE), bf16),
            pltpu.VMEM((slot_len, PLANE), bf16),
            pltpu.VMEM((heads, PLANE, bq), bf16),
            pltpu.VMEM((heads, PLANE, bq), bf16),
            pltpu.VMEM((heads, HD, bq), f32),
            pltpu.VMEM((slot_len, PLANE), f32),
            pltpu.VMEM((slot_len, PLANE), f32),
        ],
        compiler_params=pltpu.CompilerParams(vmem_limit_bytes=VMEM_LIMIT),
        cost_estimate=pl.CostEstimate(
            flops=10 * HD * pairs * 4, bytes_accessed=slot_len * width * 20, transcendentals=pairs
        ),
        name="attend_backward",
    )(length, keys, keys_t, values, queries_t, grad_out_t, out_t, lse)


def normalize(resid, gain, shift):
    center = resid - jnp.mean(resid, axis=-1, keepdims=True)
    invstd = lax.rsqrt(jnp.mean(center * center, axis=-1, keepdims=True) + epsilon)
    normed = center * invstd
    return (normed * gain + shift, normed, invstd)


def normalize_back(grad, normed, invstd, gain):
    scaled = grad * gain
    inner = (
        scaled
        - jnp.mean(scaled, axis=-1, keepdims=True)
        - normed * jnp.mean(scaled * normed, axis=-1, keepdims=True)
    )
    return (invstd * inner, jnp.sum(grad * normed, axis=0), jnp.sum(grad, axis=0))


def exchange(pieces, rank, group_size, shift_sign):
    arrived = [pieces[0]]
    for s in range(1, group_size):
        moves = [(i, (i + shift_sign * s) % group_size) for i in range(group_size)]
        arrived.append(lax.ppermute(pieces[s], "tensor", moves))
    return arrived


def ring_gather(own, rank, group_size):
    rows = own.shape[0]
    whole = jnp.zeros((group_size * rows,) + own.shape[1:], own.dtype)
    whole = lax.dynamic_update_slice_in_dim(whole, own, rank * rows, 0)
    moves = [(i, (i + 1) % group_size) for i in range(group_size)]
    held = own
    for s in range(1, group_size):
        held = lax.ppermute(held, "tensor", moves)
        source = (rank - s) % group_size
        whole = lax.dynamic_update_slice_in_dim(whole, held, source * rows, 0)
    return whole


def spread_gather(shard, row_unit):
    dp_size = lax.axis_size("dp")
    rows = shard.shape[0]
    unit = row_unit * dp_size
    padded = -(-rows // unit) * unit
    if padded != rows:
        shard = jnp.pad(shard, ((0, padded - rows), (0, 0)))
    part = padded // dp_size
    mine = lax.dynamic_slice_in_dim(shard, lax.axis_index("dp") * part, part, 0)
    whole = lax.all_gather(mine, ("tensor", "dp"), axis=0, tiled=True)
    return whole.reshape(lax.axis_size("tensor"), padded, shard.shape[1])


def body(
    hidden_in,
    lengths,
    labels,
    out_cotangent,
    w_query,
    b_query,
    w_key,
    w_value,
    b_value,
    w_out,
    b_out,
    ln1_gain,
    ln1_bias,
    w_in,
    b_in,
    w_down,
    b_down,
    ln2_gain,
    ln2_bias,
    w_student,
    b_student,
    pool_query,
    w_pool,
    b_pool,
    w_class,
    b_class,
):
    slot_len, model = hidden_in.shape
    group_size = lax.axis_size("tensor")
    dp_size = lax.axis_size("dp")
    own_count = slot_len // group_size
    rank = lax.axis_index("tensor")
    own_start = rank * own_count
    width = w_query.shape[1]
    hidden_width = w_in.shape[1]
    stu_cols = w_student.shape[1]
    length = lengths[0]

    early = spread_gather(jnp.concatenate([w_out, w_in, b_in[None, :]], axis=0), 16)
    w_out_all = early[:, :width].reshape(group_size * width, model)
    w_in_all = early[:, width : width + model]
    b_in_all = early[:, width + model]
    w_down_all = spread_gather(w_down, 16)[:, :hidden_width]
    stud = jnp.concatenate([w_student, b_student[None, :]], axis=0)
    stud_all = lax.all_gather(stud, "tensor", axis=1, tiled=True)
    w_stud_all = stud_all[:model]
    b_stud_all = stud_all[model:]

    hidden_own = lax.dynamic_slice_in_dim(hidden_in, own_start, own_count, 0)
    cot_own = lax.dynamic_slice_in_dim(out_cotangent, own_start, own_count, 0)
    w_project = jnp.concatenate([w_query, w_key, w_value], axis=1)
    bias_project = jnp.concatenate([b_query, jnp.zeros_like(b_query), b_value])
    projected_t = (
        lax.dot_general(w_project, hidden_in, (((0,), (1,)), ((), ())), preferred_element_type=f32)
        + bias_project[:, None]
    ).astype(bf16)
    key_value = (matmul(hidden_in, w_project[:, width:]) + bias_project[width:]).astype(bf16)
    queries_t = projected_t[:width]
    keys_t = projected_t[width : 2 * width]
    values_t = projected_t[2 * width :]
    keys = key_value[:, :width]
    values = key_value[:, width:]

    chunk_outs = [None] * group_size
    chunk_lses = [None] * group_size
    for s in list(range(1, group_size)) + [0]:
        target = (rank + s) % group_size
        query_chunk = lax.dynamic_slice_in_dim(queries_t, target * own_count, own_count, 1)
        chunk_outs[s], chunk_lses[s] = attend_forward(lengths, keys, query_chunk, values_t)
    arrived = exchange(chunk_outs, rank, group_size, 1)
    attended_t = jnp.zeros((group_size * width, own_count), bf16)
    out_t = jnp.zeros((width, slot_len), bf16)
    lse = jnp.zeros((8, slot_len), f32)
    for s in range(group_size):
        source = (rank - s) % group_size
        attended_t = lax.dynamic_update_slice_in_dim(attended_t, arrived[s], source * width, 0)
        target = (rank + s) % group_size
        out_t = lax.dynamic_update_slice_in_dim(out_t, chunk_outs[s], target * own_count, 1)
        lse = lax.dynamic_update_slice_in_dim(lse, chunk_lses[s], target * own_count, 1)

    resid1 = across_rows(attended_t, w_out_all) + b_out + hidden_own.astype(f32)
    first, normed1, invstd1 = normalize(resid1, ln1_gain, ln1_bias)
    first_low = first.astype(bf16)
    acts = []
    slopes = []
    ffn = None
    for b in range(group_size):
        pre = matmul(first_low, w_in_all[b]) + b_in_all[b].astype(f32)
        below = 0.5 * (1.0 + lax.erf(pre * math.sqrt(0.5)))
        density = jnp.exp(-0.5 * pre * pre) * (1.0 / math.sqrt(2.0 * math.pi))
        acts.append((pre * below).astype(bf16))
        slopes.append((below + pre * density).astype(bf16))
        more = matmul(acts[b], w_down_all[b])
        ffn = more if ffn is None else ffn + more
    resid2 = ffn + b_down + first_low.astype(f32)
    second, normed2, invstd2 = normalize(resid2, ln2_gain, ln2_bias)
    second_low = second.astype(bf16)
    hidden_out = ring_gather(second_low, rank, group_size)

    student_low = (matmul(second_low, w_stud_all) + b_stud_all.astype(f32)).astype(bf16)
    student = student_low.astype(f32)
    student_width = student.shape[1]
    head_width = student_width // POOL_HEADS
    probe_scale = 1.0 / math.sqrt(head_width)
    own_rows = own_start + lax.broadcasted_iota(jnp.int32, (own_count, 1), 0)
    row_valid = own_rows < length
    head_of = lax.broadcasted_iota(jnp.int32, (1, student_width), 1) // head_width

    def per_head(values_wide):
        whole = jnp.zeros_like(values_wide)
        for h in range(POOL_HEADS):
            part = jnp.sum(
                jnp.where(head_of == h, values_wide, 0.0), axis=-1, keepdims=True
            )
            whole = jnp.where(head_of == h, part, whole)
        return whole

    probes = pool_query[None, :]
    energies = jnp.where(row_valid, per_head(student * probes) * probe_scale, mask_fill)
    local_top = jnp.max(energies, axis=0, keepdims=True)
    local_weights = jnp.exp(energies - local_top)
    local_total = jnp.sum(local_weights, axis=0, keepdims=True)
    local_pooled = jnp.sum(local_weights * student, axis=0, keepdims=True)
    stats = jnp.concatenate(
        [local_top, local_total, local_pooled, jnp.zeros((5, student_width), f32)], axis=0
    )
    stats_all = lax.all_gather(stats[None], "tensor", axis=0, tiled=True)
    top = jnp.max(stats_all[:, 0], axis=0, keepdims=True)
    fade = jnp.exp(stats_all[:, 0] - top)
    inv_total = 1.0 / jnp.sum(fade * stats_all[:, 1], axis=0, keepdims=True)
    pooled = jnp.sum(fade * stats_all[:, 2], axis=0, keepdims=True) * inv_total
    squashed = jnp.tanh(jnp.dot(pooled, w_pool, precision=highest) + b_pool)
    logits = jnp.dot(squashed, w_class, precision=highest) + b_class
    classes = lax.broadcasted_iota(jnp.int32, logits.shape, 1)
    g_logits = jax.nn.softmax(logits, axis=-1) - (classes == labels[:, None]).astype(f32)
    grad_w_class = squashed.reshape(-1, 1) * g_logits
    grad_b_class = g_logits[0]
    g_u = lax.dot_general(
        g_logits, w_class, (((1,), (1,)), ((), ())), precision=highest
    ) * (1.0 - squashed * squashed)
    grad_w_pool = pooled.reshape(-1, 1) * g_u
    grad_b_pool = g_u[0]
    g_pooled = lax.dot_general(g_u, w_pool, (((1,), (1,)), ((), ())), precision=highest)
    inner = per_head(pooled * g_pooled)
    pool = jnp.exp(energies - top) * inv_total
    g_energy = pool * (per_head(student * g_pooled) - inner)
    g_stud_low = (pool * g_pooled + g_energy * probes * probe_scale).astype(bf16)
    grad_pool_query = jnp.sum(g_energy * student, axis=0) * probe_scale

    grad_second = jnp.where(row_valid, cot_own.astype(f32), 0.0) + against(g_stud_low, w_stud_all)
    grad_stud_weight = across_rows(second_low, g_stud_low)
    grad_stud_bias = jnp.sum(g_stud_low, axis=0, dtype=f32)
    grad_resid2, grad_ln2_gain, grad_ln2_bias = normalize_back(
        grad_second, normed2, invstd2, ln2_gain
    )
    grad_b_down = jnp.sum(grad_resid2, axis=0)
    grad_ffn_low = grad_resid2.astype(bf16)
    grad_first = grad_resid2
    grad_w_in = []
    grad_w_down = []
    grad_b_in = []
    for b in range(group_size):
        grad_pre = (against(grad_ffn_low, w_down_all[b]) * slopes[b].astype(f32)).astype(bf16)
        grad_w_down.append(across_rows(acts[b], grad_ffn_low).astype(bf16))
        grad_w_in.append(across_rows(first_low, grad_pre).astype(bf16))
        grad_b_in.append(jnp.sum(grad_pre, axis=0, dtype=f32))
        grad_first = grad_first + against(grad_pre, w_in_all[b])
    grad_resid1, grad_ln1_gain, grad_ln1_bias = normalize_back(
        grad_first, normed1, invstd1, ln1_gain
    )
    grad_b_out = jnp.sum(grad_resid1, axis=0)
    grad_mix = grad_resid1.astype(bf16)
    grad_att_t = against(w_out_all, grad_mix).astype(bf16)
    grad_pieces = [
        lax.dynamic_slice_in_dim(grad_att_t, ((rank + s) % group_size) * width, width, 0)
        for s in range(group_size)
    ]
    grad_arrived = exchange(grad_pieces, rank, group_size, 1)
    grad_out_t = jnp.zeros((width, slot_len), bf16)
    for s in range(group_size):
        source = (rank - s) % group_size
        grad_out_t = lax.dynamic_update_slice_in_dim(
            grad_out_t, grad_arrived[s], source * own_count, 1
        )
    grad_w_out = matmul(attended_t, grad_mix).astype(bf16)

    blocks = jnp.stack(
        [
            jnp.concatenate(
                [grad_w_in[b], grad_w_down[b], grad_w_out[b * width : (b + 1) * width]], axis=0
            )
            for b in range(group_size)
        ],
        axis=0,
    )
    block_rows = blocks.shape[1]
    part_rows = -(-block_rows // (8 * dp_size)) * 8
    if part_rows * dp_size != block_rows:
        blocks = jnp.pad(blocks, ((0, 0), (0, part_rows * dp_size - block_rows), (0, 0)))
    blocks = blocks.reshape(group_size, dp_size, part_rows, model).transpose(1, 0, 2, 3)
    reduced = lax.psum_scatter(
        blocks.reshape(dp_size * group_size, part_rows, model),
        "dp",
        scatter_dimension=0,
        tiled=True,
    )
    reduced = lax.psum_scatter(reduced, "tensor", scatter_dimension=0, tiled=True)
    reduced = lax.all_gather(reduced[0], "dp", axis=0, tiled=True)

    only_once = (rank == 0).astype(f32)
    small = lax.psum(
        (
            jnp.stack(grad_b_in),
            grad_pool_query,
            grad_w_pool * only_once,
            grad_b_pool * only_once,
            grad_w_class * only_once,
            grad_b_class * only_once,
            grad_b_out,
            grad_ln1_gain,
            grad_ln1_bias,
            grad_b_down,
            grad_ln2_gain,
            grad_ln2_bias,
            grad_stud_weight,
            grad_stud_bias,
        ),
        ("dp", "tensor"),
    )

    grad_q_t, grad_k, grad_v = attend_backward(
        lengths, keys, keys_t, values, queries_t, grad_out_t, out_t, lse
    )
    grad_kv = jnp.concatenate([grad_k, grad_v], axis=1)
    partial_in = (
        lax.dot_general(grad_q_t, w_query, (((0,), (1,)), ((), ())), preferred_element_type=f32)
        + against(grad_kv, w_project[:, width:])
    ).astype(bf16)
    grad_in_own = (
        lax.psum_scatter(partial_in, "tensor", scatter_dimension=0, tiled=True).astype(f32)
        + grad_resid1
    )
    grad_in = ring_gather(grad_in_own.astype(bf16), rank, group_size)
    grad_w_query = lax.dot_general(
        hidden_in, grad_q_t, (((0,), (1,)), ((), ())), preferred_element_type=f32
    )
    grad_w_kv = across_rows(hidden_in, grad_kv)
    late = lax.psum(
        (
            grad_w_query,
            grad_w_kv,
            jnp.sum(grad_q_t, axis=1, dtype=f32),
            jnp.sum(grad_v, axis=0, dtype=f32),
        ),
        "dp",
    )
    grad_w_student = lax.dynamic_slice_in_dim(small[12], rank * stu_cols, stu_cols, 1)
    grad_b_student = lax.dynamic_slice_in_dim(small[13], rank * stu_cols, stu_cols, 0)
    grad_b_in_own = lax.dynamic_index_in_dim(small[0], rank, 0, keepdims=False)
    return (
        hidden_out,
        logits,
        grad_in,
        late[0],
        late[2],
        late[1][:, :width],
        late[1][:, width:],
        late[3],
        reduced[model + hidden_width : model + hidden_width + width].astype(f32),
        small[6],
        small[7],
        small[8],
        reduced[:model].astype(f32),
        grad_b_in_own,
        reduced[model : model + hidden_width].astype(f32),
        small[9],
        small[10],
        small[11],
        grad_w_student,
        grad_b_student,
        small[1],
        small[2],
        small[3],
        small[4],
        small[5],
    )


def solution(mesh):
    by_dp = P("dp", None)
    cols = P(None, "tensor")
    rows = P("tensor", None)
    cut = P("tensor")
    in_specs = (
        (by_dp, P("dp"), P("dp"), by_dp, cols, cut, cols, cols, cut, rows, P(), P(), P(), cols)
        + (cut, rows, P(), P(), P(), cols, cut, P(), P(), P(), P(), P())
    )
    out_specs = (
        (by_dp, by_dp, by_dp, cols, cut, cols, cols, cut, rows, P(), P(), P(), cols, cut, rows)
        + (P(), P(), P(), cols, cut, P(), P(), P(), P(), P())
    )
    return jax.shard_map(body, mesh=mesh, in_specs=in_specs, out_specs=out_specs, check_vma=False)
```

```python
import functools
import math

import jax
import jax.numpy as jnp
from jax import lax
from jax.experimental import pallas as pl
from jax.experimental.pallas import tpu as pltpu
from jax.sharding import PartitionSpec as P

HD = 64
POOL_HEADS = 2

epsilon = 1e-06
mask_fill = -1e30
highest = lax.Precision.HIGHEST
bf16 = jnp.bfloat16
f32 = jnp.float32
SCORE_SCALE = 1.0 / math.sqrt(HD)
SCORE_SCALE_2 = math.log2(math.e) * SCORE_SCALE
PLANE = 256
VMEM_LIMIT = 60 * 1024 * 1024


def matmul(left, right):
    return jnp.dot(left, right, preferred_element_type=f32)


def across_rows(left, right):
    return lax.dot_general(left, right, (((0,), (0,)), ((), ())), preferred_element_type=f32)


def against(left, right):
    return lax.dot_general(left, right, (((1,), (1,)), ((), ())), preferred_element_type=f32)


def project_kernel(
    width, info_ref, h_ref, wkv_ref, wt_ref, bkv_ref, bt_ref, rot_ref, k_ref, v_ref, t_ref
):
    hidden = h_ref[...]
    rot_ref[...] = hidden
    rows = hidden.shape[0]
    valid = info_ref[1 + pl.program_id(0)]
    key_value = (matmul(hidden, wkv_ref[...]) + bkv_ref[...]).astype(bf16)
    row = lax.broadcasted_iota(jnp.int32, (rows, PLANE - width), 0)
    lane = lax.broadcasted_iota(jnp.int32, (rows, PLANE - width), 1)
    k_ref[:, :width] = key_value[:, :width]
    k_ref[:, width:] = jnp.where((lane == 0) & (row >= valid), mask_fill, 0.0).astype(bf16)
    v_ref[:, :width] = key_value[:, width:]
    v_ref[:, width:] = jnp.zeros((rows, PLANE - width), bf16)
    t_ref[...] = (against(wt_ref[...], hidden) + bt_ref[...]).astype(bf16)


def project(info, hidden_in, w_kv, w_all_t, bias_kv, bias_t, chunks):
    slot_len, model = hidden_in.shape
    width = w_all_t.shape[0] // 3
    rows = slot_len // chunks
    whole = lambda c, info_ref: (0, 0)
    return pl.pallas_call(
        functools.partial(project_kernel, width),
        grid_spec=pltpu.PrefetchScalarGridSpec(
            num_scalar_prefetch=1,
            grid=(chunks,),
            in_specs=[
                pl.BlockSpec((rows, model), lambda c, info_ref: ((info_ref[0] + c) % chunks, 0)),
                pl.BlockSpec((model, 2 * width), whole),
                pl.BlockSpec((3 * width, model), whole),
                pl.BlockSpec((1, 2 * width), whole),
                pl.BlockSpec((3 * width, 1), whole),
            ],
            out_specs=[
                pl.BlockSpec((rows, model), lambda c, info_ref: (c, 0)),
                pl.BlockSpec((rows, PLANE), lambda c, info_ref: (c, 0)),
                pl.BlockSpec((rows, PLANE), lambda c, info_ref: (c, 0)),
                pl.BlockSpec((3 * width, rows), lambda c, info_ref: (0, c)),
            ],
        ),
        out_shape=(
            jax.ShapeDtypeStruct((slot_len, model), bf16),
            jax.ShapeDtypeStruct((slot_len, PLANE), bf16),
            jax.ShapeDtypeStruct((slot_len, PLANE), bf16),
            jax.ShapeDtypeStruct((3 * width, slot_len), bf16),
        ),
        compiler_params=pltpu.CompilerParams(vmem_limit_bytes=VMEM_LIMIT),
        cost_estimate=pl.CostEstimate(
            flops=10 * width * model * slot_len,
            bytes_accessed=slot_len * model * 8,
            transcendentals=0,
        ),
        name="project",
    )(info, hidden_in, w_kv, w_all_t, bias_kv, bias_t)


def forward_kernel(bq, bk, heads, info_ref, k_ref, qt_ref, vt_ref, ot_ref, lse_ref, head_q, acc):
    width = HD * heads
    chunks = info_ref.shape[0] - 3
    first_tile = info_ref[1 + chunks]
    tile_count = info_ref[2 + chunks]
    row = lax.broadcasted_iota(jnp.int32, (PLANE, bq), 0)
    for h in range(heads):
        head_q[h] = jnp.where(row == width, 1.0, 0.0).astype(bf16)

    def query_step(qb, unused):
        q0 = pl.multiple_of(qb * bq, bq)
        for h in range(heads):
            own = slice(HD * h, HD * h + HD)
            head_q[h, own, :] = qt_ref[own, pl.ds(q0, bq)]
        acc[...] = jnp.zeros_like(acc)

        def key_step(step, carry):
            k0 = pl.multiple_of(((first_tile + step) % 2) * bk, bk)
            keys = k_ref[pl.ds(k0, bk), :]
            scores = [matmul(keys, head_q[h]) for h in range(heads)]
            kept = []
            for h in range(heads):
                top, total = carry[h]
                new_top = jnp.maximum(
                    top, jnp.max(scores[h], axis=0, keepdims=True) * SCORE_SCALE_2
                )
                weights = jnp.exp2(scores[h] * SCORE_SCALE_2 - new_top)
                fade = jnp.exp2(top - new_top)
                total = fade * total + jnp.sum(weights, axis=0, keepdims=True)
                values_t = vt_ref[HD * h : HD * h + HD, pl.ds(k0, bk)]
                acc[h] = fade * acc[h] + matmul(values_t, weights.astype(bf16))
                kept.append((new_top, total))
            return tuple(kept)

        start = tuple(
            (jnp.full((1, bq), mask_fill, f32), jnp.zeros((1, bq), f32)) for _ in range(heads)
        )
        done = lax.fori_loop(0, tile_count, key_step, start)
        for h in range(heads):
            top, total = done[h]
            ot_ref[HD * h : HD * h + HD, pl.ds(q0, bq)] = (acc[h] * (1.0 / total)).astype(bf16)
            lse_ref[pl.ds(h, 1), pl.ds(q0, bq)] = top + jnp.log2(total)
        return unused

    lax.fori_loop(0, qt_ref.shape[1] // bq, query_step, 0)


def attend_forward(info, wide_k, projected_t, chunk, chunks):
    slot_len = wide_k.shape[0]
    width = projected_t.shape[0] // 3
    heads = width // HD
    rows = slot_len // chunks
    bq, bk = min(512, rows), slot_len // 2
    pairs = heads * rows * slot_len
    return pl.pallas_call(
        functools.partial(forward_kernel, bq, bk, heads),
        grid=(1,),
        out_shape=(
            jax.ShapeDtypeStruct((width, rows), bf16),
            jax.ShapeDtypeStruct((8, rows), f32),
        ),
        in_specs=[
            pl.BlockSpec(memory_space=pltpu.SMEM),
            pl.BlockSpec((slot_len, PLANE), lambda i: (0, 0)),
            pl.BlockSpec((width, rows), lambda i: (0, chunk)),
            pl.BlockSpec((width, slot_len), lambda i: (2, 0)),
        ],
        out_specs=[
            pl.BlockSpec((width, rows), lambda i: (0, 0)),
            pl.BlockSpec((8, rows), lambda i: (0, 0)),
        ],
        scratch_shapes=[
            pltpu.VMEM((heads, PLANE, bq), bf16),
            pltpu.VMEM((heads, HD, bq), f32),
        ],
        compiler_params=pltpu.CompilerParams(vmem_limit_bytes=VMEM_LIMIT),
        cost_estimate=pl.CostEstimate(
            flops=16 * HD * pairs, bytes_accessed=slot_len * width * 8, transcendentals=pairs
        ),
        name="attend_forward",
    )(info, wide_k, projected_t, projected_t)


def backward_kernel(bq, heads, q_span, k_span, rows, has_q, has_k, end_q, end_k, *refs):
    width = HD * heads
    one_key = k_span[1] - k_span[0] == 1
    refs = list(refs)
    info_ref, k_ref, v_ref, kt_ref, qt_ref, got_ref, ot_ref, lse_ref = refs[:8]
    del refs[:8]
    gq_in = refs.pop(0) if has_q else None
    gk_in = refs.pop(0) if has_k else None
    gv_in = refs.pop(0) if has_k else None
    gq_low = refs.pop(0) if end_q else None
    gq = None if end_q else refs.pop(0)
    gkv_low = refs.pop(0) if end_k else None
    gk = None if end_k else refs.pop(0)
    gv = None if end_k else refs.pop(0)
    head_q, head_go = refs[:2]
    del refs[:2]
    if end_q:
        gq = refs.pop(0)
    if end_k:
        gk, gv = refs.pop(0), refs.pop(0)
    gq[...] = gq_in[...] if has_q else jnp.zeros_like(gq)
    gk[...] = gk_in[...] if has_k else jnp.zeros_like(gk)
    gv[...] = gv_in[...] if has_k else jnp.zeros_like(gv)
    row = lax.broadcasted_iota(jnp.int32, (PLANE, bq), 0)
    for h in range(heads):
        head_q[h] = jnp.where(row == width, 1.0, 0.0).astype(bf16)
        head_go[h] = jnp.zeros((PLANE, bq), bf16)

    def chunk_step(q, unused):
        def query_step(qb, inner):
            q0 = pl.multiple_of(qb * bq, bq)
            span = pl.ds(q0, bq)
            all_span = pl.ds(pl.multiple_of(q * rows + q0, bq), bq)
            deltas = []
            tops = []
            for h in range(heads):
                own = slice(HD * h, HD * h + HD)
                head_q[h, own, :] = qt_ref[own, all_span]
                grad_out = got_ref[q - q_span[0], own, span]
                head_go[h, own, :] = grad_out
                outs = ot_ref[q - q_span[0], own, span]
                deltas.append(
                    jnp.sum(grad_out.astype(f32) * outs.astype(f32), axis=0, keepdims=True)
                )
                tops.append(lse_ref[q - q_span[0], pl.ds(h, 1), span])

            def key_step(k, innermost):
                @pl.when(info_ref[1 + k] > 0)
                def one_tile():
                    at = k - k_span[0]
                    k0 = pl.multiple_of((at if one_key else k) * rows, rows)
                    keys = k_ref[pl.ds(k0, rows), :]
                    values = v_ref[pl.ds(k0, rows), :]
                    grad_v = None
                    grad_k = None
                    for h in range(heads):
                        own = slice(HD * h, HD * h + HD)
                        scores = matmul(keys, head_q[h])
                        grad_weights = matmul(values, head_go[h])
                        weights = jnp.exp2(scores * SCORE_SCALE_2 - tops[h])
                        grad_scores = (weights * (grad_weights - deltas[h])).astype(bf16)
                        more_v = against(weights.astype(bf16), head_go[h])
                        more_k = against(grad_scores, head_q[h])
                        grad_v = more_v if grad_v is None else grad_v + more_v
                        grad_k = more_k if grad_k is None else grad_k + more_k
                        gq[q - q_span[0], own, span] += matmul(
                            kt_ref[own, pl.ds(k0, rows)], grad_scores
                        )
                    gk[at] += grad_k
                    gv[at] += grad_v

                return innermost

            lax.fori_loop(k_span[0], k_span[1], key_step, 0)
            return inner

        lax.fori_loop(0, (info_ref[1 + q] + bq - 1) // bq, query_step, 0)
        return unused

    lax.fori_loop(q_span[0], q_span[1], chunk_step, 0)
    if end_q:
        gq_low[...] = (gq[...] * SCORE_SCALE).astype(bf16)
    if end_k:
        gkv_low[:, :, :width] = (gk[:, :, :width] * SCORE_SCALE).astype(bf16)
        gkv_low[:, :, width:] = gv[:, :, :width].astype(bf16)


def attend_backward(
    info, wide_k, wide_v, projected_t, grad_out_t, out_t, lse, q_span, k_span, gq, gkv, end_q, end_k
):
    chunks = info.shape[0] - 3
    slot_len = wide_k.shape[0]
    width = projected_t.shape[0] // 3
    heads = width // HD
    rows = slot_len // chunks
    nq, nk = q_span[1] - q_span[0], k_span[1] - k_span[0]
    bq = min(512, rows)
    one = nk == 1
    k_at = k_span[0]
    if one:
        key_spec = pl.BlockSpec((rows, PLANE), lambda i: (k_at, 0))
        kt_spec = pl.BlockSpec((width, rows), lambda i: (1, k_at))
    else:
        key_spec = pl.BlockSpec((slot_len, PLANE), lambda i: (0, 0))
        kt_spec = pl.BlockSpec((width, slot_len), lambda i: (1, 0))
    full3 = lambda i: (0, 0, 0)
    gq_shape, gk_shape = (nq, width, rows), (nk, rows, PLANE)
    gq_spec, gk_spec = pl.BlockSpec(gq_shape, full3), pl.BlockSpec(gk_shape, full3)
    operands = [info, wide_k, wide_v, projected_t, projected_t, grad_out_t, out_t, lse]
    in_specs = [
        pl.BlockSpec(memory_space=pltpu.SMEM),
        key_spec,
        key_spec,
        kt_spec,
        pl.BlockSpec((width, slot_len), lambda i: (0, 0)),
        gq_spec,
        gq_spec,
        pl.BlockSpec((nq, 8, rows), full3),
    ]
    if gq is not None:
        operands.append(gq)
        in_specs.append(gq_spec)
    if gkv is not None:
        operands.extend(gkv)
        in_specs.extend([gk_spec, gk_spec])
    out_shape = [jax.ShapeDtypeStruct(gq_shape, bf16 if end_q else f32)]
    out_specs = [gq_spec]
    scratch = [
        pltpu.VMEM((heads, PLANE, bq), bf16),
        pltpu.VMEM((heads, PLANE, bq), bf16),
    ]
    if end_q:
        scratch.append(pltpu.VMEM(gq_shape, f32))
    if end_k:
        out_shape.append(jax.ShapeDtypeStruct((nk, rows, 2 * width), bf16))
        out_specs.append(pl.BlockSpec((nk, rows, 2 * width), full3))
        scratch.extend([pltpu.VMEM(gk_shape, f32)] * 2)
    else:
        out_shape.extend([jax.ShapeDtypeStruct(gk_shape, f32)] * 2)
        out_specs.extend([gk_spec] * 2)
    pairs = heads * nq * nk * rows * rows
    results = pl.pallas_call(
        functools.partial(
            backward_kernel,
            bq,
            heads,
            q_span,
            k_span,
            rows,
            gq is not None,
            gkv is not None,
            end_q,
            end_k,
        ),
        grid=(1,),
        out_shape=tuple(out_shape),
        in_specs=in_specs,
        out_specs=out_specs,
        scratch_shapes=scratch,
        compiler_params=pltpu.CompilerParams(vmem_limit_bytes=VMEM_LIMIT),
        cost_estimate=pl.CostEstimate(
            flops=40 * HD * pairs,
            bytes_accessed=(nq + nk) * rows * width * 12,
            transcendentals=pairs,
        ),
        name="attend_backward",
    )(*operands)
    return results[0], (results[1] if end_k else (results[1], results[2]))


def transposed(left, right):
    return lax.dot_general(left, right, (((0,), (0,)), ((), ())), preferred_element_type=f32)


def ffn_forward_kernel(row_step, x_ref, w_in_ref, b_ref, w_down_ref, act_ref, slope_ref, out_ref):
    for r0 in range(0, x_ref.shape[0], row_step):
        rows = slice(r0, r0 + row_step)
        pre = matmul(x_ref[rows, :], w_in_ref[0]) + b_ref[0].astype(f32)
        below = 0.5 + 0.5 * lax.erf(pre * math.sqrt(0.5))
        density = jnp.exp(-0.5 * pre * pre) * (1.0 / math.sqrt(2.0 * math.pi))
        act = (pre * below).astype(bf16)
        act_ref[0, rows, :] = act
        slope_ref[0, rows, :] = (below + pre * density).astype(bf16)
        more = matmul(act, w_down_ref[0])

        @pl.when(pl.program_id(0) == 0)
        def first():
            out_ref[rows, :] = more

        @pl.when(pl.program_id(0) > 0)
        def later():
            out_ref[rows, :] += more


def ffn_forward(first_low, gathered, b_in_all):
    count, model = first_low.shape
    groups = gathered.shape[0]
    units = b_in_all.shape[-1]
    block = pl.BlockSpec((1, count, units), lambda b: (b, 0, 0))
    return pl.pallas_call(
        functools.partial(ffn_forward_kernel, min(256, count)),
        grid=(groups,),
        in_specs=[
            pl.BlockSpec((count, model), lambda b: (0, 0)),
            pl.BlockSpec((1, model, units), lambda b: (b, 0, 0)),
            pl.BlockSpec((1, 1, units), lambda b: (b, 0, 0)),
            pl.BlockSpec((1, units, model), lambda b: (b, 1, 0)),
        ],
        out_specs=[block, block, pl.BlockSpec((count, model), lambda b: (0, 0))],
        out_shape=(
            jax.ShapeDtypeStruct((groups, count, units), bf16),
            jax.ShapeDtypeStruct((groups, count, units), bf16),
            jax.ShapeDtypeStruct((count, model), f32),
        ),
        compiler_params=pltpu.CompilerParams(vmem_limit_bytes=VMEM_LIMIT),
        cost_estimate=pl.CostEstimate(
            flops=8 * count * model * units * groups,
            bytes_accessed=8 * groups * count * units,
            transcendentals=groups * count * units,
        ),
        name="ffn_forward",
    )(first_low, gathered, b_in_all, gathered)


def ffn_backward_kernel(row_step, g_ref, w_in_ref, w_down_ref, slope_ref, pre_ref, out_ref):
    for r0 in range(0, g_ref.shape[0], row_step):
        rows = slice(r0, r0 + row_step)
        grad_act = against(g_ref[rows, :], w_down_ref[0])
        grad_pre = (grad_act * slope_ref[0, rows, :].astype(f32)).astype(bf16)
        pre_ref[0, rows, :] = grad_pre
        more = against(grad_pre, w_in_ref[0])

        @pl.when(pl.program_id(0) == 0)
        def first():
            out_ref[rows, :] = more

        @pl.when(pl.program_id(0) > 0)
        def later():
            out_ref[rows, :] += more


def ffn_backward(grad_ffn_low, gathered, slopes):
    count, model = grad_ffn_low.shape
    groups, _, units = slopes.shape
    block = pl.BlockSpec((1, count, units), lambda b: (b, 0, 0))
    return pl.pallas_call(
        functools.partial(ffn_backward_kernel, min(256, count)),
        grid=(groups,),
        in_specs=[
            pl.BlockSpec((count, model), lambda b: (0, 0)),
            pl.BlockSpec((1, model, units), lambda b: (b, 0, 0)),
            pl.BlockSpec((1, units, model), lambda b: (b, 1, 0)),
            block,
        ],
        out_specs=[block, pl.BlockSpec((count, model), lambda b: (0, 0))],
        out_shape=(
            jax.ShapeDtypeStruct((groups, count, units), bf16),
            jax.ShapeDtypeStruct((count, model), f32),
        ),
        compiler_params=pltpu.CompilerParams(vmem_limit_bytes=VMEM_LIMIT),
        cost_estimate=pl.CostEstimate(
            flops=4 * count * model * units * groups,
            bytes_accessed=8 * groups * count * units,
            transcendentals=0,
        ),
        name="ffn_backward",
    )(grad_ffn_low, gathered, gathered, slopes)


SMALL_ROWS = 32
UNIT = 128


def pack_kernel(
    dp_size,
    part,
    first_ref,
    gpre_ref,
    act_ref,
    gffn_ref,
    att_ref,
    gmix_ref,
    gstud_ref,
    second_ref,
    columns_ref,
    pool_ref,
    class_ref,
    tail_ref,
    out_ref,
    stud_acc,
    small,
):
    b = pl.program_id(0)
    at = 0

    def store(rows_value):
        nonlocal at
        done = 0
        count = rows_value.shape[0]
        while done < count:
            d, offset = divmod(at, part)
            take = min(part - offset, count - done)
            out_ref[d, 0, offset : offset + take, :] = rows_value[done : done + take].astype(bf16)
            done += take
            at += take

    store(transposed(first_ref[...], gpre_ref[0]))
    store(transposed(act_ref[0], gffn_ref[...]))
    store(matmul(att_ref[...], gmix_ref[...]))
    groups = pl.num_programs(0)
    stud_cols = stud_acc.shape[1]

    @pl.when(b == 0)
    def student():
        whole = transposed(gstud_ref[...], second_ref[...])
        for i in range(stud_acc.shape[0]):
            stud_acc[i] = whole[i * stud_cols : (i + 1) * stud_cols]

    store(stud_acc[b])
    small[...] = jnp.zeros_like(small)
    small[:, :UNIT] = pool_ref[...]
    units = columns_ref.shape[1] // UNIT
    count = columns_ref.shape[0] * units
    share = -(-count // stud_acc.shape[0])
    for block in range(stud_acc.shape[0]):

        @pl.when(b == block)
        def own_columns():
            for r in range(share):
                u = block * share + r
                if u < count:
                    lanes = slice((u % units) * UNIT, (u % units + 1) * UNIT)
                    small[r : r + 1, UNIT : 2 * UNIT] = columns_ref[
                        u // units : u // units + 1, lanes
                    ]

    small[: class_ref.shape[1], 2 * UNIT : 3 * UNIT] = class_ref[0]

    @pl.when(b == 0)
    def tail_rows():
        small[: tail_ref.shape[0], 3 * UNIT : 4 * UNIT] = tail_ref[...]

    grad_b_in = jnp.sum(gpre_ref[0].astype(f32), axis=0, keepdims=True)
    for u in range(grad_b_in.shape[1] // UNIT):
        small[u : u + 1, 4 * UNIT : 5 * UNIT] = grad_b_in[:, u * UNIT : (u + 1) * UNIT]
    small[0:1, 5 * UNIT : 6 * UNIT] = jnp.sum(gstud_ref[...].astype(f32), axis=0, keepdims=True)
    store(small[...])
    if at < dp_size * part:
        store(jnp.zeros((dp_size * part - at, small.shape[1]), f32))


def pack_gradients(dp_size, part, groups, dense, columns, pool, classes, tail):
    first_low, grad_pre, acts, grad_ffn, attended_t, grad_mix, grad_stud, second_low = dense
    count, model = first_low.shape
    units = acts.shape[2]
    width = attended_t.shape[0] // groups
    students = grad_stud.shape[1]
    stud_cols = students // groups
    rows = lambda cols: pl.BlockSpec((count, cols), lambda b: (0, 0))
    block = pl.BlockSpec((1, count, units), lambda b: (b, 0, 0))
    whole = lambda array: pl.BlockSpec(array.shape, lambda b: (0,) * array.ndim)
    return pl.pallas_call(
        functools.partial(pack_kernel, dp_size, part),
        grid=(groups,),
        in_specs=[
            rows(model),
            block,
            block,
            rows(model),
            pl.BlockSpec((width, count), lambda b: (b, 0)),
            rows(model),
            rows(students),
            rows(model),
            whole(columns),
            pl.BlockSpec((pool.shape[0] // groups, pool.shape[1]), lambda b: (b, 0)),
            pl.BlockSpec((1,) + classes.shape[1:], lambda b: (b, 0, 0)),
            whole(tail),
        ],
        out_specs=pl.BlockSpec((dp_size, 1, part, model), lambda b: (0, b, 0, 0)),
        out_shape=jax.ShapeDtypeStruct((dp_size, groups, part, model), bf16),
        scratch_shapes=[
            pltpu.VMEM((groups, stud_cols, model), f32),
            pltpu.VMEM((SMALL_ROWS, model), f32),
        ],
        compiler_params=pltpu.CompilerParams(vmem_limit_bytes=VMEM_LIMIT),
        cost_estimate=pl.CostEstimate(
            flops=6 * count * model * units * groups,
            bytes_accessed=8 * groups * count * units,
            transcendentals=0,
        ),
        name="pack_gradients",
    )(
        first_low,
        grad_pre,
        acts,
        grad_ffn,
        attended_t,
        grad_mix,
        grad_stud,
        second_low,
        columns,
        pool,
        classes,
        tail,
    )


def normalize(resid, gain, shift):
    center = resid - jnp.mean(resid, axis=-1, keepdims=True)
    invstd = lax.rsqrt(jnp.mean(center * center, axis=-1, keepdims=True) + epsilon)
    normed = center * invstd
    return (normed * gain + shift, normed, invstd)


def normalize_back(grad, normed, invstd, gain):
    scaled = grad * gain
    inner = (
        scaled
        - jnp.mean(scaled, axis=-1, keepdims=True)
        - normed * jnp.mean(scaled * normed, axis=-1, keepdims=True)
    )
    return (invstd * inner, jnp.sum(grad * normed, axis=0), jnp.sum(grad, axis=0))


def shift(array, ahead, group_size):
    if ahead % group_size == 0:
        return array
    moves = [(i, (i + ahead) % group_size) for i in range(group_size)]
    return lax.ppermute(array, "tensor", moves)


def group_tiles(tile, rank, group_size):
    found = [shift(tile, s, group_size) for s in range(group_size)]
    tiles = jnp.zeros((group_size,) + tile.shape, tile.dtype)
    for s in range(group_size):
        tiles = lax.dynamic_update_index_in_dim(tiles, found[s], (rank - s) % group_size, 0)
    return tiles


def ring_gather(own, rank, group_size):
    rows = own.shape[0]
    whole = jnp.zeros((group_size * rows,) + own.shape[1:], own.dtype)
    whole = lax.dynamic_update_slice_in_dim(whole, own, rank * rows, 0)
    held = own
    for s in range(1, group_size):
        held = shift(held, 1, group_size)
        source = (rank - s) % group_size
        whole = lax.dynamic_update_slice_in_dim(whole, held, source * rows, 0)
    return whole


def row_parts(rows):
    dp_size = lax.axis_size("dp")
    part = -(-rows // (16 * dp_size)) * 16
    return dp_size, part


def spread_gather(shard):
    dp_size, part = row_parts(shard.shape[0])
    shard = jnp.pad(shard, ((0, part * dp_size - shard.shape[0]), (0, 0)))
    mine = lax.dynamic_slice_in_dim(shard, lax.axis_index("dp") * part, part, 0)
    whole = lax.all_gather(mine, ("tensor", "dp"), axis=0, tiled=True)
    return whole.reshape(lax.axis_size("tensor"), part * dp_size, shard.shape[1])


def body(
    hidden_in,
    lengths,
    labels,
    out_cotangent,
    w_query,
    b_query,
    w_key,
    w_value,
    b_value,
    w_out,
    b_out,
    ln1_gain,
    ln1_bias,
    w_in,
    b_in,
    w_down,
    b_down,
    ln2_gain,
    ln2_bias,
    w_student,
    b_student,
    pool_query,
    w_pool,
    b_pool,
    w_class,
    b_class,
):
    slot_len, model = hidden_in.shape
    group_size = lax.axis_size("tensor")
    own_count = slot_len // group_size
    rank = lax.axis_index("tensor")
    own_start = rank * own_count
    width = w_query.shape[1]
    hidden_width = w_in.shape[1]
    stu_cols = w_student.shape[1]
    length = lengths[0]
    pad_row = lambda row: jnp.pad(row[None, :], ((0, 0), (0, model - row.shape[0])))

    w_kv = jnp.concatenate([w_key, w_value], axis=1)
    w_project_t = jnp.concatenate([w_query.T, w_key.T, w_value.T], axis=0)
    gathered = spread_gather(jnp.concatenate([w_in, w_down, w_out], axis=0))
    w_out_all = gathered[:, model + hidden_width : model + hidden_width + width].reshape(
        group_size * width, model
    )
    w_project_all = spread_gather(w_project_t)
    stud_tile = jnp.concatenate(
        [w_student.T, b_in[None, :], pad_row(b_student), jnp.zeros((6, model), bf16)], axis=0
    )
    stud_tiles = group_tiles(stud_tile, rank, group_size)
    w_stud_t = stud_tiles[:, :stu_cols].reshape(group_size * stu_cols, model)
    b_in_all = stud_tiles[:, stu_cols : stu_cols + 1]
    b_stud_all = stud_tiles[:, stu_cols + 1, :stu_cols].reshape(1, group_size * stu_cols)

    hidden_own = lax.dynamic_slice_in_dim(hidden_in, own_start, own_count, 0)
    cot_own = lax.dynamic_slice_in_dim(out_cotangent, own_start, own_count, 0)
    chunk_at = (rank + jnp.arange(group_size, dtype=jnp.int32)) % group_size
    chunk_valid = jnp.clip(length - chunk_at * own_count, 0, own_count)
    half = group_size // 2
    first_empty = (jnp.sum(chunk_valid[:half]) == 0).astype(jnp.int32)
    second_empty = (jnp.sum(chunk_valid[half:]) == 0).astype(jnp.int32)
    info = jnp.concatenate(
        [
            rank[None],
            chunk_valid,
            first_empty[None],
            (2 - first_empty - second_empty)[None],
        ]
    ).astype(jnp.int32)
    bias_t = jnp.concatenate([b_query, jnp.zeros_like(b_query), b_value])
    hidden_rot, wide_k, wide_v, projected_t = project(
        info, hidden_in, w_kv, w_project_t, bias_t[None, width:], bias_t[:, None], group_size
    )

    outs = [None] * group_size
    lses = [None] * group_size
    attended = [None] * group_size
    for s in list(range(1, group_size)) + [0]:
        outs[s], lses[s] = attend_forward(info, wide_k, projected_t, s, group_size)
        attended[s] = shift(outs[s], s, group_size)
    attended_t = jnp.zeros((group_size * width, own_count), bf16)
    for s in range(group_size):
        source = (rank - s) % group_size
        attended_t = lax.dynamic_update_slice_in_dim(attended_t, attended[s], source * width, 0)

    resid1 = across_rows(attended_t, w_out_all) + b_out + hidden_own.astype(f32)
    first, normed1, invstd1 = normalize(resid1, ln1_gain, ln1_bias)
    first_low = first.astype(bf16)
    acts, slopes, ffn = ffn_forward(first_low, gathered, b_in_all)
    resid2 = ffn + b_down + first_low.astype(f32)
    second, normed2, invstd2 = normalize(resid2, ln2_gain, ln2_bias)
    second_low = second.astype(bf16)
    leaving, w_project_all = lax.optimization_barrier((second_low, w_project_all))
    hidden_out = lax.all_gather(leaving, "tensor", axis=0, tiled=True)

    student_low = (against(second_low, w_stud_t) + b_stud_all.astype(f32)).astype(bf16)
    student = student_low.astype(f32)
    student_width = student.shape[1]
    head_width = student_width // POOL_HEADS
    probe_scale = 1.0 / math.sqrt(head_width)
    own_rows = own_start + lax.broadcasted_iota(jnp.int32, (own_count, 1), 0)
    row_valid = own_rows < length
    head_of = lax.broadcasted_iota(jnp.int32, (1, student_width), 1) // head_width

    def per_head(values_wide):
        whole = jnp.zeros_like(values_wide)
        for h in range(POOL_HEADS):
            part = jnp.sum(
                jnp.where(head_of == h, values_wide, 0.0), axis=-1, keepdims=True
            )
            whole = jnp.where(head_of == h, part, whole)
        return whole

    probes = pool_query[None, :]
    energies = jnp.where(row_valid, per_head(student * probes) * probe_scale, mask_fill)
    local_top = jnp.max(energies, axis=0, keepdims=True)
    local_weights = jnp.exp(energies - local_top)
    local_total = jnp.sum(local_weights, axis=0, keepdims=True)
    local_pooled = jnp.sum(local_weights * student, axis=0, keepdims=True)
    stats = jnp.concatenate(
        [local_top, local_total, local_pooled, jnp.zeros((5, student_width), f32)], axis=0
    )
    stats_all = jnp.stack([shift(stats, s, group_size) for s in range(group_size)])
    top = jnp.max(stats_all[:, 0], axis=0, keepdims=True)
    fade = jnp.exp(stats_all[:, 0] - top)
    inv_total = 1.0 / jnp.sum(fade * stats_all[:, 1], axis=0, keepdims=True)
    pooled = jnp.sum(fade * stats_all[:, 2], axis=0, keepdims=True) * inv_total
    squashed = jnp.tanh(jnp.dot(pooled, w_pool, precision=highest) + b_pool)
    logits = jnp.dot(squashed, w_class, precision=highest) + b_class
    classes = lax.broadcasted_iota(jnp.int32, logits.shape, 1)
    g_logits = jax.nn.softmax(logits, axis=-1) - (classes == labels[:, None]).astype(f32)
    grad_w_class_t = g_logits.reshape(-1, 1) * squashed
    grad_b_class = g_logits[0]
    g_u = lax.dot_general(
        g_logits, w_class, (((1,), (1,)), ((), ())), precision=highest
    ) * (1.0 - squashed * squashed)
    grad_w_pool = pooled.reshape(-1, 1) * g_u
    grad_b_pool = g_u[0]
    g_pooled = lax.dot_general(g_u, w_pool, (((1,), (1,)), ((), ())), precision=highest)
    inner = per_head(pooled * g_pooled)
    pool = jnp.exp(energies - top) * inv_total
    g_energy = pool * (per_head(student * g_pooled) - inner)
    g_stud_low = (pool * g_pooled + g_energy * probes * probe_scale).astype(bf16)
    grad_pool_query = jnp.sum(g_energy * student, axis=0) * probe_scale

    grad_second = jnp.where(row_valid, cot_own.astype(f32), 0.0) + matmul(g_stud_low, w_stud_t)
    grad_resid2, grad_ln2_gain, grad_ln2_bias = normalize_back(
        grad_second, normed2, invstd2, ln2_gain
    )
    grad_b_down = jnp.sum(grad_resid2, axis=0)
    grad_ffn_low = grad_resid2.astype(bf16)
    grad_pre, grad_first = ffn_backward(grad_ffn_low, gathered, slopes)
    grad_first = grad_first + grad_resid2
    grad_resid1, grad_ln1_gain, grad_ln1_bias = normalize_back(
        grad_first, normed1, invstd1, ln1_gain
    )
    grad_b_out = jnp.sum(grad_resid1, axis=0)
    grad_mix = grad_resid1.astype(bf16)
    grad_att_t = against(w_out_all, grad_mix).astype(bf16)
    grad_outs = []
    for s in range(group_size):
        target = (rank - s) % group_size
        piece = lax.dynamic_slice_in_dim(grad_att_t, target * width, width, 0)
        grad_outs.append(shift(piece, -s, group_size))

    only_once = (rank == 0).astype(f32)
    lanes = student_width
    class_count = grad_b_class.shape[0]
    columns = jnp.stack(
        [grad_b_out, grad_ln1_gain, grad_ln1_bias, grad_b_down, grad_ln2_gain, grad_ln2_bias]
    )
    class_share = -(-class_count // group_size)
    grad_w_class_t = jnp.pad(
        grad_w_class_t * only_once, ((0, class_share * group_size - class_count), (0, 0))
    ).reshape(group_size, class_share, lanes)
    tail = jnp.stack(
        [
            grad_b_pool * only_once,
            jnp.pad(grad_b_class, (0, lanes - class_count)) * only_once,
            grad_pool_query,
        ]
    )
    at = model + hidden_width
    small_at = at + width + stu_cols
    dp_size, part = row_parts(small_at + SMALL_ROWS)
    dense = (first_low, grad_pre, acts, grad_ffn_low, attended_t, grad_mix, g_stud_low, second_low)
    blocks = pack_gradients(
        dp_size, part, group_size, dense, columns, grad_w_pool * only_once, grad_w_class_t, tail
    )
    grad_outs[0], blocks = lax.optimization_barrier((grad_outs[0], blocks))
    part_of = functools.partial(attend_backward, info, wide_k, wide_v, projected_t)
    others = (1, group_size)
    own_side = (grad_outs[0][None], outs[0][None], lses[0][None])
    other_side = tuple(jnp.stack(side[1:]) for side in (grad_outs, outs, lses))
    gq_own, gkv_others = part_of(*own_side, (0, 1), others, None, None, False, False)
    blocks, hidden_out, gq_own = lax.optimization_barrier((blocks, hidden_out, gq_own))
    reduced = lax.psum_scatter(
        blocks.reshape(dp_size * group_size, part, model), "dp", scatter_dimension=0, tiled=True
    )
    gq_others = None
    grad_kv = [None] * group_size
    kv_arrived = [None] * group_size
    for s in range(1, group_size):
        so_far = tuple(side[s - 1 : s] for side in gkv_others)
        gq_others, low = part_of(
            *other_side, others, (s, s + 1), gq_others, so_far, False, True
        )
        grad_kv[s] = low[0]
        kv_arrived[s] = shift(grad_kv[s], s, group_size)
    reduced, gq_others = lax.optimization_barrier((reduced, gq_others))
    reduced = lax.psum_scatter(reduced, "tensor", scatter_dimension=0, tiled=True)
    gkv_own = None
    grad_q = [None] * group_size
    q_arrived = [None] * group_size
    for s in range(1, group_size):
        side = (grad_outs[s][None], outs[s][None], lses[s][None])
        low, gkv_own = part_of(
            *side, (s, s + 1), (0, 1), gq_others[s - 1 : s], gkv_own, True, False
        )
        grad_q[s] = low[0]
        q_arrived[s] = shift(grad_q[s], s, group_size)
    reduced, gkv_own = lax.optimization_barrier((reduced, gkv_own))
    reduced = lax.all_gather(reduced[0], "dp", axis=0, tiled=True)
    low_q, low_kv = part_of(*own_side, (0, 1), (0, 1), gq_own, gkv_own, True, True)
    grad_q[0] = q_arrived[0] = low_q[0]
    grad_kv[0] = kv_arrived[0] = low_kv[0]

    grad_in_own = grad_resid1
    for s in range(group_size):
        source = (rank - s) % group_size
        w_source = lax.dynamic_index_in_dim(w_project_all, source, 0, keepdims=False)
        grad_in_own = (
            grad_in_own
            + across_rows(q_arrived[s], w_source[:width])
            + matmul(kv_arrived[s], w_source[width : 3 * width])
        )
    grad_in = ring_gather(grad_in_own.astype(bf16), rank, group_size)

    grad_w_q = None
    grad_w_kv = None
    grad_b_q = None
    grad_b_kv = None
    for s in range(group_size):
        rows_here = hidden_rot[s * own_count : (s + 1) * own_count]
        more_q = lax.dot_general(
            grad_q[s], rows_here, (((1,), (0,)), ((), ())), preferred_element_type=f32
        )
        more_kv = across_rows(grad_kv[s], rows_here)
        more_bq = jnp.sum(grad_q[s], axis=1, dtype=f32)
        more_bkv = jnp.sum(grad_kv[s], axis=0, dtype=f32)
        grad_w_q = more_q if s == 0 else grad_w_q + more_q
        grad_w_kv = more_kv if s == 0 else grad_w_kv + more_kv
        grad_b_q = more_bq if s == 0 else grad_b_q + more_bq
        grad_b_kv = more_bkv if s == 0 else grad_b_kv + more_bkv
    late = jnp.concatenate(
        [grad_w_q, grad_w_kv, pad_row(grad_b_q), pad_row(grad_b_kv[width:])], axis=0
    ).astype(bf16)
    late, reduced = lax.optimization_barrier((late, reduced))
    small_own = reduced[small_at : small_at + SMALL_ROWS]
    small = group_tiles(small_own[:, : 4 * UNIT], rank, group_size).astype(f32)
    small_own = small_own[:, 4 * UNIT :].astype(f32)
    grad_w_pool = small[:, :, :UNIT].reshape(grad_w_pool.shape)
    column_share = -(-columns.size // (UNIT * group_size))
    columns = small[:, :column_share, UNIT : 2 * UNIT].reshape(-1)[: columns.size].reshape(
        columns.shape
    )
    grad_w_class = (
        small[:, :class_share, 2 * UNIT : 3 * UNIT].reshape(-1, lanes)[:class_count].T
    )
    grad_b_pool = small[0, 0, 3 * UNIT :]
    grad_b_class = small[0, 1, 3 * UNIT : 3 * UNIT + class_count]
    grad_pool_query = small[0, 2, 3 * UNIT :]
    grad_b_in = small_own[: hidden_width // UNIT, :UNIT].reshape(-1)
    grad_b_stud = lax.dynamic_slice_in_dim(small_own[0, UNIT:], rank * stu_cols, stu_cols, 0)

    late = lax.psum(late, "dp").astype(f32)
    reduced = reduced.astype(f32)
    return (
        hidden_out,
        logits,
        grad_in,
        late[:width].T,
        late[3 * width, :width],
        late[width : 2 * width].T,
        late[2 * width : 3 * width].T,
        late[3 * width + 1, :width],
        reduced[at : at + width],
        columns[0],
        columns[1],
        columns[2],
        reduced[:model],
        grad_b_in,
        reduced[model:at],
        columns[3],
        columns[4],
        columns[5],
        reduced[at + width : small_at].T,
        grad_b_stud,
        grad_pool_query,
        grad_w_pool,
        grad_b_pool,
        grad_w_class,
        grad_b_class,
    )


def solution(mesh):
    by_dp = P("dp", None)
    cols = P(None, "tensor")
    rows = P("tensor", None)
    cut = P("tensor")
    in_specs = (
        (by_dp, P("dp"), P("dp"), by_dp, cols, cut, cols, cols, cut, rows, P(), P(), P(), cols)
        + (cut, rows, P(), P(), P(), cols, cut, P(), P(), P(), P(), P())
    )
    out_specs = (
        (by_dp, by_dp, by_dp, cols, cut, cols, cols, cut, rows, P(), P(), P(), cols, cut, rows)
        + (P(), P(), P(), cols, cut, P(), P(), P(), P(), P())
    )
    return jax.shard_map(body, mesh=mesh, in_specs=in_specs, out_specs=out_specs, check_vma=False)
```

```python
import functools
import math

import jax
import jax.numpy as jnp
from jax import lax
from jax.experimental import pallas as pl
from jax.experimental.pallas import tpu as pltpu
from jax.sharding import PartitionSpec as P

HD = 64
POOL_HEADS = 2

epsilon = 1e-06
mask_fill = -1e30
highest = lax.Precision.HIGHEST
bf16 = jnp.bfloat16
f32 = jnp.float32
SCORE_SCALE = 1.0 / math.sqrt(HD)
SCORE_SCALE_2 = math.log2(math.e) * SCORE_SCALE
PLANE = 256
UNIT = 128
SMALL_ROWS = 32
VMEM_LIMIT = 60 * 1024 * 1024


def matmul(left, right):
    return jnp.dot(left, right, preferred_element_type=f32)


def across_rows(left, right):
    return lax.dot_general(left, right, (((0,), (0,)), ((), ())), preferred_element_type=f32)


def against(left, right):
    return lax.dot_general(left, right, (((1,), (1,)), ((), ())), preferred_element_type=f32)


def project_kernel(
    width, info_ref, h_ref, wkv_ref, wt_ref, bkv_ref, bt_ref, rot_ref, k_ref, v_ref, t_ref
):
    hidden = h_ref[...]
    rot_ref[...] = hidden
    rows = hidden.shape[0]
    valid = info_ref[1 + pl.program_id(0)]
    key_value = (matmul(hidden, wkv_ref[...]) + bkv_ref[...]).astype(bf16)
    row = lax.broadcasted_iota(jnp.int32, (rows, PLANE - width), 0)
    lane = lax.broadcasted_iota(jnp.int32, (rows, PLANE - width), 1)
    k_ref[:, :width] = key_value[:, :width]
    k_ref[:, width:] = jnp.where((lane == 0) & (row >= valid), mask_fill, 0.0).astype(bf16)
    v_ref[:, :width] = key_value[:, width:]
    v_ref[:, width:] = jnp.zeros((rows, PLANE - width), bf16)
    t_ref[...] = (against(wt_ref[...], hidden) + bt_ref[...]).astype(bf16)


def project(info, hidden_in, w_kv, w_all_t, bias_kv, bias_t, chunks):
    slot_len, model = hidden_in.shape
    width = w_all_t.shape[0] // 3
    rows = slot_len // chunks
    whole = lambda c, info_ref: (0, 0)
    return pl.pallas_call(
        functools.partial(project_kernel, width),
        grid_spec=pltpu.PrefetchScalarGridSpec(
            num_scalar_prefetch=1,
            grid=(chunks,),
            in_specs=[
                pl.BlockSpec((rows, model), lambda c, info_ref: ((info_ref[0] + c) % chunks, 0)),
                pl.BlockSpec((model, 2 * width), whole),
                pl.BlockSpec((3 * width, model), whole),
                pl.BlockSpec((1, 2 * width), whole),
                pl.BlockSpec((3 * width, 1), whole),
            ],
            out_specs=[
                pl.BlockSpec((rows, model), lambda c, info_ref: (c, 0)),
                pl.BlockSpec((rows, PLANE), lambda c, info_ref: (c, 0)),
                pl.BlockSpec((rows, PLANE), lambda c, info_ref: (c, 0)),
                pl.BlockSpec((3 * width, rows), lambda c, info_ref: (0, c)),
            ],
        ),
        out_shape=(
            jax.ShapeDtypeStruct((slot_len, model), bf16),
            jax.ShapeDtypeStruct((slot_len, PLANE), bf16),
            jax.ShapeDtypeStruct((slot_len, PLANE), bf16),
            jax.ShapeDtypeStruct((3 * width, slot_len), bf16),
        ),
        compiler_params=pltpu.CompilerParams(vmem_limit_bytes=VMEM_LIMIT),
        cost_estimate=pl.CostEstimate(flops=1, bytes_accessed=1, transcendentals=0),
        name="project",
    )(info, hidden_in, w_kv, w_all_t, bias_kv, bias_t)


def forward_kernel(bq, bk, heads, info_ref, k_ref, qt_ref, vt_ref, ot_ref, lse_ref, head_q, acc):
    width = HD * heads
    chunks = info_ref.shape[0] - 3
    first_tile = info_ref[1 + chunks]
    tile_count = info_ref[2 + chunks]
    row = lax.broadcasted_iota(jnp.int32, (PLANE, bq), 0)
    for h in range(heads):
        head_q[h] = jnp.where(row == width, 1.0, 0.0).astype(bf16)

    def query_step(qb, unused):
        q0 = pl.multiple_of(qb * bq, bq)
        for h in range(heads):
            own = slice(HD * h, HD * h + HD)
            head_q[h, own, :] = qt_ref[own, pl.ds(q0, bq)]
        acc[...] = jnp.zeros_like(acc)

        def key_step(step, carry):
            k0 = pl.multiple_of(((first_tile + step) % 2) * bk, bk)
            keys = k_ref[pl.ds(k0, bk), :]
            scores = [matmul(keys, head_q[h]) for h in range(heads)]
            kept = []
            for h in range(heads):
                top, total = carry[h]
                new_top = jnp.maximum(
                    top, jnp.max(scores[h], axis=0, keepdims=True) * SCORE_SCALE_2
                )
                weights = jnp.exp2(scores[h] * SCORE_SCALE_2 - new_top)
                fade = jnp.exp2(top - new_top)
                total = fade * total + jnp.sum(weights, axis=0, keepdims=True)
                values_t = vt_ref[HD * h : HD * h + HD, pl.ds(k0, bk)]
                acc[h] = fade * acc[h] + matmul(values_t, weights.astype(bf16))
                kept.append((new_top, total))
            return tuple(kept)

        start = tuple(
            (jnp.full((1, bq), mask_fill, f32), jnp.zeros((1, bq), f32)) for _ in range(heads)
        )
        done = lax.fori_loop(0, tile_count, key_step, start)
        for h in range(heads):
            top, total = done[h]
            ot_ref[HD * h : HD * h + HD, pl.ds(q0, bq)] = (acc[h] * (1.0 / total)).astype(bf16)
            lse_ref[pl.ds(h, 1), pl.ds(q0, bq)] = top + jnp.log2(total)
        return unused

    lax.fori_loop(0, qt_ref.shape[1] // bq, query_step, 0)


def attend_forward(info, wide_k, projected_t, chunk, chunks):
    slot_len = wide_k.shape[0]
    width = projected_t.shape[0] // 3
    heads = width // HD
    rows = slot_len // chunks
    bq, bk = min(512, rows), slot_len // 2
    pairs = heads * rows * slot_len
    return pl.pallas_call(
        functools.partial(forward_kernel, bq, bk, heads),
        grid=(1,),
        out_shape=(
            jax.ShapeDtypeStruct((width, rows), bf16),
            jax.ShapeDtypeStruct((8, rows), f32),
        ),
        in_specs=[
            pl.BlockSpec(memory_space=pltpu.SMEM),
            pl.BlockSpec((slot_len, PLANE), lambda i: (0, 0)),
            pl.BlockSpec((width, rows), lambda i: (0, chunk)),
            pl.BlockSpec((width, slot_len), lambda i: (2, 0)),
        ],
        out_specs=[
            pl.BlockSpec((width, rows), lambda i: (0, 0)),
            pl.BlockSpec((8, rows), lambda i: (0, 0)),
        ],
        scratch_shapes=[
            pltpu.VMEM((heads, PLANE, bq), bf16),
            pltpu.VMEM((heads, HD, bq), f32),
        ],
        compiler_params=pltpu.CompilerParams(vmem_limit_bytes=VMEM_LIMIT),
        cost_estimate=pl.CostEstimate(flops=1, bytes_accessed=1, transcendentals=0),
        name="attend_forward",
    )(info, wide_k, projected_t, projected_t)


def backward_kernel(bq, heads, q_span, k_span, rows, has, end_q, end_k, *refs):
    width = HD * heads
    one_key = k_span[1] - k_span[0] == 1
    refs = list(refs)
    info_ref, k_ref, v_ref, kt_ref, qt_ref, got_ref, ot_ref, lse_ref = refs[:8]
    del refs[:8]
    hidden_ref = refs.pop(0) if end_q or end_k else None
    gq_in = refs.pop(0) if "q" in has else None
    gk_in = refs.pop(0) if "k" in has else None
    gv_in = refs.pop(0) if "k" in has else None
    wq_in = refs.pop(0) if "wq" in has else None
    wkv_in = refs.pop(0) if "wkv" in has else None
    gq_out = refs.pop(0)
    gkv_low = refs.pop(0) if end_k else None
    gk = None if end_k else refs.pop(0)
    gv = None if end_k else refs.pop(0)
    w_out_ref = refs.pop(0) if end_q or end_k else None
    head_q, head_go = refs[:2]
    del refs[:2]
    gq = refs.pop(0) if end_q else gq_out
    if end_k:
        gk, gv = refs.pop(0), refs.pop(0)
    gq[...] = jnp.zeros_like(gq) if gq_in is None else gq_in[...]
    gk[...] = jnp.zeros_like(gk) if gk_in is None else gk_in[...]
    gv[...] = jnp.zeros_like(gv) if gv_in is None else gv_in[...]
    row = lax.broadcasted_iota(jnp.int32, (PLANE, bq), 0)
    for h in range(heads):
        head_q[h] = jnp.where(row == width, 1.0, 0.0).astype(bf16)
        head_go[h] = jnp.zeros((PLANE, bq), bf16)

    def chunk_step(q, unused):
        def query_step(qb, inner):
            q0 = pl.multiple_of(qb * bq, bq)
            span = pl.ds(q0, bq)
            all_span = pl.ds(pl.multiple_of(q * rows + q0, bq), bq)
            deltas = []
            tops = []
            for h in range(heads):
                own = slice(HD * h, HD * h + HD)
                head_q[h, own, :] = qt_ref[own, all_span]
                grad_out = got_ref[q - q_span[0], own, span]
                head_go[h, own, :] = grad_out
                outs = ot_ref[q - q_span[0], own, span]
                deltas.append(
                    jnp.sum(grad_out.astype(f32) * outs.astype(f32), axis=0, keepdims=True)
                )
                tops.append(lse_ref[q - q_span[0], pl.ds(h, 1), span])

            def key_step(k, innermost):
                @pl.when(info_ref[1 + k] > 0)
                def one_tile():
                    at = k - k_span[0]
                    k0 = pl.multiple_of((at if one_key else k) * rows, rows)
                    keys = k_ref[pl.ds(k0, rows), :]
                    values = v_ref[pl.ds(k0, rows), :]
                    grad_v = None
                    grad_k = None
                    for h in range(heads):
                        own = slice(HD * h, HD * h + HD)
                        scores = matmul(keys, head_q[h])
                        grad_weights = matmul(values, head_go[h])
                        weights = jnp.exp2(scores * SCORE_SCALE_2 - tops[h])
                        grad_scores = (weights * (grad_weights - deltas[h])).astype(bf16)
                        more_v = against(weights.astype(bf16), head_go[h])
                        more_k = against(grad_scores, head_q[h])
                        grad_v = more_v if grad_v is None else grad_v + more_v
                        grad_k = more_k if grad_k is None else grad_k + more_k
                        gq[q - q_span[0], own, span] += matmul(
                            kt_ref[own, pl.ds(k0, rows)], grad_scores
                        )
                    gk[at] += grad_k
                    gv[at] += grad_v

                return innermost

            lax.fori_loop(k_span[0], k_span[1], key_step, 0)
            return inner

        lax.fori_loop(0, (info_ref[1 + q] + bq - 1) // bq, query_step, 0)
        return unused

    lax.fori_loop(q_span[0], q_span[1], chunk_step, 0)
    ones = jnp.ones((rows, UNIT), bf16)

    def add_weights(first_row, product, sum_in):
        lead = slice(first_row, first_row + product(ones).shape[0])
        model = hidden_ref.shape[1]
        for lanes, right in ((slice(0, model), hidden_ref[...]), (slice(model, None), ones)):
            value = product(right)
            if sum_in is not None:
                value = value + sum_in[:, lanes]
            w_out_ref[lead, lanes] = value.astype(w_out_ref.dtype)

    if end_q:
        low = (gq[0] * SCORE_SCALE).astype(bf16)
        gq_out[0] = low
        add_weights(0, lambda right: matmul(low, right), wq_in)
    if end_k:
        gkv_low[0, :, :width] = (gk[0, :, :width] * SCORE_SCALE).astype(bf16)
        gkv_low[0, :, width:] = gv[0, :, :width].astype(bf16)
        both = gkv_low[0]
        add_weights(
            width if end_q else 0,
            lambda right: lax.dot_general(
                both, right, (((0,), (0,)), ((), ())), preferred_element_type=f32
            ),
            wkv_in,
        )


def attend_backward(
    info,
    wide_k,
    wide_v,
    projected_t,
    hidden_rot,
    grad_out_t,
    out_t,
    lse,
    q_span,
    k_span,
    gq=None,
    gkv=None,
    wq=None,
    wkv=None,
    gq_at=0,
    gkv_at=0,
    end_q=False,
    end_k=False,
):
    chunks = info.shape[0] - 3
    slot_len = wide_k.shape[0]
    width = projected_t.shape[0] // 3
    model = hidden_rot.shape[1]
    heads = width // HD
    rows = slot_len // chunks
    nq, nk = q_span[1] - q_span[0], k_span[1] - k_span[0]
    bq = min(512, rows)
    k_at = k_span[0]
    if nk == 1:
        key_spec = pl.BlockSpec((rows, PLANE), lambda i: (k_at, 0))
        kt_spec = pl.BlockSpec((width, rows), lambda i: (1, k_at))
    else:
        key_spec = pl.BlockSpec((slot_len, PLANE), lambda i: (0, 0))
        kt_spec = pl.BlockSpec((width, slot_len), lambda i: (1, 0))
    at_zero = lambda i: (0, 0, 0)
    gq_shape, gk_shape = (nq, width, rows), (nk, rows, PLANE)
    gq_spec, gk_spec = pl.BlockSpec(gq_shape, at_zero), pl.BlockSpec(gk_shape, at_zero)
    whole2 = lambda array: pl.BlockSpec(array.shape, lambda i: (0, 0))
    operands = [info, wide_k, wide_v, projected_t, projected_t, grad_out_t, out_t, lse]
    in_specs = [
        pl.BlockSpec(memory_space=pltpu.SMEM),
        key_spec,
        key_spec,
        kt_spec,
        pl.BlockSpec((width, slot_len), lambda i: (0, 0)),
        gq_spec,
        gq_spec,
        pl.BlockSpec((nq, 8, rows), at_zero),
    ]
    has = []
    if end_q or end_k:
        ended = k_at if end_k else q_span[0]
        operands.append(hidden_rot)
        in_specs.append(pl.BlockSpec((rows, model), lambda i: (ended, 0)))
    if gq is not None:
        has.append("q")
        operands.append(gq)
        in_specs.append(pl.BlockSpec(gq_shape, lambda i: (gq_at, 0, 0)))
    if gkv is not None:
        has.append("k")
        operands.extend(gkv)
        in_specs.extend([pl.BlockSpec(gk_shape, lambda i: (gkv_at, 0, 0))] * 2)
    for name, array in (("wq", wq), ("wkv", wkv)):
        if array is not None:
            has.append(name)
            operands.append(array)
            in_specs.append(whole2(array))
    out_shape = [jax.ShapeDtypeStruct(gq_shape, bf16 if end_q else f32)]
    out_specs = [gq_spec]
    scratch = [
        pltpu.VMEM((heads, PLANE, bq), bf16),
        pltpu.VMEM((heads, PLANE, bq), bf16),
    ]
    if end_q:
        scratch.append(pltpu.VMEM(gq_shape, f32))
    if end_k:
        out_shape.append(jax.ShapeDtypeStruct((nk, rows, 2 * width), bf16))
        out_specs.append(pl.BlockSpec((nk, rows, 2 * width), at_zero))
        scratch.extend([pltpu.VMEM(gk_shape, f32)] * 2)
    else:
        out_shape.extend([jax.ShapeDtypeStruct(gk_shape, f32)] * 2)
        out_specs.extend([gk_spec] * 2)
    if end_q or end_k:
        w_rows = width * ((1 if end_q else 0) + (2 if end_k else 0))
        w_shape = (w_rows, model + UNIT)
        out_shape.append(jax.ShapeDtypeStruct(w_shape, bf16 if end_q and end_k else f32))
        out_specs.append(pl.BlockSpec(w_shape, lambda i: (0, 0)))
    pairs = heads * nq * nk * rows * rows
    return pl.pallas_call(
        functools.partial(
            backward_kernel, bq, heads, q_span, k_span, rows, tuple(has), end_q, end_k
        ),
        grid=(1,),
        out_shape=tuple(out_shape),
        in_specs=in_specs,
        out_specs=out_specs,
        scratch_shapes=scratch,
        compiler_params=pltpu.CompilerParams(vmem_limit_bytes=VMEM_LIMIT),
        cost_estimate=pl.CostEstimate(flops=1, bytes_accessed=1, transcendentals=0),
        name="attend_backward",
    )(*operands)


def input_kernel(width, kv_from, q_from, rank_ref, sum_ref, w_ref, *refs):
    out_ref = refs[-1]
    groups = w_ref.shape[0]
    total = sum_ref[...]
    for at, behind in enumerate(kv_from + q_from):
        source = lax.rem(rank_ref[0] + groups - behind, groups)
        if at < len(kv_from):
            total += matmul(refs[at][...], w_ref[source, width : 3 * width, :])
        else:
            total += across_rows(refs[at][...], w_ref[source, :width, :])
    out_ref[...] = total.astype(out_ref.dtype)


def add_input_gradients(info, so_far, w_project_all, kv_pieces, q_pieces, dtype):
    width = next(iter(kv_pieces.values())).shape[1] // 2
    count, model = so_far.shape
    rows = min(256, count)
    pieces = list(kv_pieces.values()) + list(q_pieces.values())
    by_rows = pl.BlockSpec((rows, model), lambda r: (r, 0))
    return pl.pallas_call(
        functools.partial(input_kernel, width, tuple(kv_pieces), tuple(q_pieces)),
        grid=(count // rows,),
        in_specs=[
            pl.BlockSpec(memory_space=pltpu.SMEM),
            by_rows,
            pl.BlockSpec(w_project_all.shape, lambda r: (0, 0, 0)),
        ]
        + [pl.BlockSpec((rows, 2 * width), lambda r: (r, 0))] * len(kv_pieces)
        + [pl.BlockSpec((width, rows), lambda r: (0, r))] * len(q_pieces),
        out_specs=by_rows,
        out_shape=jax.ShapeDtypeStruct(so_far.shape, dtype),
        compiler_params=pltpu.CompilerParams(vmem_limit_bytes=VMEM_LIMIT),
        cost_estimate=pl.CostEstimate(flops=1, bytes_accessed=1, transcendentals=0),
        name="add_input_gradients",
    )(info, so_far, w_project_all, *pieces)


def ffn_forward_kernel(row_step, x_ref, w_in_ref, b_ref, w_down_ref, act_ref, slope_ref, out_ref):
    for r0 in range(0, x_ref.shape[0], row_step):
        rows = slice(r0, r0 + row_step)
        pre = matmul(x_ref[rows, :], w_in_ref[0]) + b_ref[0].astype(f32)
        below = 0.5 + 0.5 * lax.erf(pre * math.sqrt(0.5))
        density = jnp.exp(-0.5 * pre * pre) * (1.0 / math.sqrt(2.0 * math.pi))
        act = (pre * below).astype(bf16)
        act_ref[0, rows, :] = act
        slope_ref[0, rows, :] = (below + pre * density).astype(bf16)
        more = matmul(act, w_down_ref[0])

        @pl.when(pl.program_id(0) == 0)
        def first():
            out_ref[rows, :] = more

        @pl.when(pl.program_id(0) > 0)
        def later():
            out_ref[rows, :] += more


def ffn_forward(first_low, gathered, b_in_all):
    count, model = first_low.shape
    groups = gathered.shape[0]
    units = b_in_all.shape[-1]
    block = pl.BlockSpec((1, count, units), lambda b: (b, 0, 0))
    return pl.pallas_call(
        functools.partial(ffn_forward_kernel, min(256, count)),
        grid=(groups,),
        in_specs=[
            pl.BlockSpec((count, model), lambda b: (0, 0)),
            pl.BlockSpec((1, model, units), lambda b: (b, 0, 0)),
            pl.BlockSpec((1, 1, units), lambda b: (b, 0, 0)),
            pl.BlockSpec((1, units, model), lambda b: (b, 1, 0)),
        ],
        out_specs=[block, block, pl.BlockSpec((count, model), lambda b: (0, 0))],
        out_shape=(
            jax.ShapeDtypeStruct((groups, count, units), bf16),
            jax.ShapeDtypeStruct((groups, count, units), bf16),
            jax.ShapeDtypeStruct((count, model), f32),
        ),
        compiler_params=pltpu.CompilerParams(vmem_limit_bytes=VMEM_LIMIT),
        cost_estimate=pl.CostEstimate(flops=1, bytes_accessed=1, transcendentals=0),
        name="ffn_forward",
    )(first_low, gathered, b_in_all, gathered)


def ffn_backward_kernel(row_step, g_ref, w_in_ref, w_down_ref, slope_ref, pre_ref, out_ref):
    for r0 in range(0, g_ref.shape[0], row_step):
        rows = slice(r0, r0 + row_step)
        grad_act = against(g_ref[rows, :], w_down_ref[0])
        grad_pre = (grad_act * slope_ref[0, rows, :].astype(f32)).astype(bf16)
        pre_ref[0, rows, :] = grad_pre
        more = against(grad_pre, w_in_ref[0])

        @pl.when(pl.program_id(0) == 0)
        def first():
            out_ref[rows, :] = more

        @pl.when(pl.program_id(0) > 0)
        def later():
            out_ref[rows, :] += more


def ffn_backward(grad_ffn_low, gathered, slopes):
    count, model = grad_ffn_low.shape
    groups, _, units = slopes.shape
    block = pl.BlockSpec((1, count, units), lambda b: (b, 0, 0))
    return pl.pallas_call(
        functools.partial(ffn_backward_kernel, min(256, count)),
        grid=(groups,),
        in_specs=[
            pl.BlockSpec((count, model), lambda b: (0, 0)),
            pl.BlockSpec((1, model, units), lambda b: (b, 0, 0)),
            pl.BlockSpec((1, units, model), lambda b: (b, 1, 0)),
            block,
        ],
        out_specs=[block, pl.BlockSpec((count, model), lambda b: (0, 0))],
        out_shape=(
            jax.ShapeDtypeStruct((groups, count, units), bf16),
            jax.ShapeDtypeStruct((count, model), f32),
        ),
        compiler_params=pltpu.CompilerParams(vmem_limit_bytes=VMEM_LIMIT),
        cost_estimate=pl.CostEstimate(flops=1, bytes_accessed=1, transcendentals=0),
        name="ffn_backward",
    )(grad_ffn_low, gathered, gathered, slopes)


def pack_kernel(
    dp_size,
    part,
    first_ref,
    gpre_ref,
    act_ref,
    gffn_ref,
    att_ref,
    gmix_ref,
    gstud_ref,
    second_ref,
    columns_ref,
    pool_ref,
    class_ref,
    tail_ref,
    out_ref,
    stud_acc,
    small,
):
    b = pl.program_id(0)
    at = 0

    def store(rows_value):
        nonlocal at
        done = 0
        count = rows_value.shape[0]
        while done < count:
            d, offset = divmod(at, part)
            take = min(part - offset, count - done)
            out_ref[d, 0, offset : offset + take, :] = rows_value[done : done + take].astype(bf16)
            done += take
            at += take

    store(across_rows(first_ref[...], gpre_ref[0]))
    store(across_rows(act_ref[0], gffn_ref[...]))
    store(matmul(att_ref[...], gmix_ref[...]))
    groups = pl.num_programs(0)
    stud_cols = stud_acc.shape[1]

    @pl.when(b == 0)
    def student():
        whole = across_rows(gstud_ref[...], second_ref[...])
        for i in range(stud_acc.shape[0]):
            stud_acc[i] = whole[i * stud_cols : (i + 1) * stud_cols]

    store(stud_acc[b])
    small[...] = jnp.zeros_like(small)
    small[:, :UNIT] = pool_ref[...]
    units = columns_ref.shape[1] // UNIT
    count = columns_ref.shape[0] * units
    share = -(-count // stud_acc.shape[0])
    for block in range(stud_acc.shape[0]):

        @pl.when(b == block)
        def own_columns():
            for r in range(share):
                u = block * share + r
                if u < count:
                    lanes = slice((u % units) * UNIT, (u % units + 1) * UNIT)
                    small[r : r + 1, UNIT : 2 * UNIT] = columns_ref[
                        u // units : u // units + 1, lanes
                    ]

    small[: class_ref.shape[1], 2 * UNIT : 3 * UNIT] = class_ref[0]

    @pl.when(b == 0)
    def tail_rows():
        small[: tail_ref.shape[0], 3 * UNIT : 4 * UNIT] = tail_ref[...]

    grad_b_in = jnp.sum(gpre_ref[0].astype(f32), axis=0, keepdims=True)
    for u in range(grad_b_in.shape[1] // UNIT):
        small[u : u + 1, 4 * UNIT : 5 * UNIT] = grad_b_in[:, u * UNIT : (u + 1) * UNIT]
    small[0:1, 5 * UNIT : 6 * UNIT] = jnp.sum(gstud_ref[...].astype(f32), axis=0, keepdims=True)
    store(small[...])
    if at < dp_size * part:
        store(jnp.zeros((dp_size * part - at, small.shape[1]), f32))


def pack_gradients(dp_size, part, groups, dense, columns, pool, classes, tail):
    first_low, grad_pre, acts, grad_ffn, attended_t, grad_mix, grad_stud, second_low = dense
    count, model = first_low.shape
    units = acts.shape[2]
    width = attended_t.shape[0] // groups
    students = grad_stud.shape[1]
    stud_cols = students // groups
    rows = lambda cols: pl.BlockSpec((count, cols), lambda b: (0, 0))
    block = pl.BlockSpec((1, count, units), lambda b: (b, 0, 0))
    whole = lambda array: pl.BlockSpec(array.shape, lambda b: (0,) * array.ndim)
    return pl.pallas_call(
        functools.partial(pack_kernel, dp_size, part),
        grid=(groups,),
        in_specs=[
            rows(model),
            block,
            block,
            rows(model),
            pl.BlockSpec((width, count), lambda b: (b, 0)),
            rows(model),
            rows(students),
            rows(model),
            whole(columns),
            pl.BlockSpec((pool.shape[0] // groups, pool.shape[1]), lambda b: (b, 0)),
            pl.BlockSpec((1,) + classes.shape[1:], lambda b: (b, 0, 0)),
            whole(tail),
        ],
        out_specs=pl.BlockSpec((dp_size, 1, part, model), lambda b: (0, b, 0, 0)),
        out_shape=jax.ShapeDtypeStruct((dp_size, groups, part, model), bf16),
        scratch_shapes=[
            pltpu.VMEM((groups, stud_cols, model), f32),
            pltpu.VMEM((SMALL_ROWS, model), f32),
        ],
        compiler_params=pltpu.CompilerParams(vmem_limit_bytes=VMEM_LIMIT),
        cost_estimate=pl.CostEstimate(flops=1, bytes_accessed=1, transcendentals=0),
        name="pack_gradients",
    )(
        first_low,
        grad_pre,
        acts,
        grad_ffn,
        attended_t,
        grad_mix,
        grad_stud,
        second_low,
        columns,
        pool,
        classes,
        tail,
    )


def normalize(resid, gain, shift):
    center = resid - jnp.mean(resid, axis=-1, keepdims=True)
    invstd = lax.rsqrt(jnp.mean(center * center, axis=-1, keepdims=True) + epsilon)
    normed = center * invstd
    return (normed * gain + shift, normed, invstd)


def normalize_back(grad, normed, invstd, gain):
    scaled = grad * gain
    inner = (
        scaled
        - jnp.mean(scaled, axis=-1, keepdims=True)
        - normed * jnp.mean(scaled * normed, axis=-1, keepdims=True)
    )
    return (invstd * inner, jnp.sum(grad * normed, axis=0), jnp.sum(grad, axis=0))


def shift(array, ahead, group_size):
    if ahead % group_size == 0:
        return array
    moves = [(i, (i + ahead) % group_size) for i in range(group_size)]
    return lax.ppermute(array, "tensor", moves)


def group_tiles(tile, rank, group_size):
    found = [shift(tile, s, group_size) for s in range(group_size)]
    tiles = jnp.zeros((group_size,) + tile.shape, tile.dtype)
    for s in range(group_size):
        tiles = lax.dynamic_update_index_in_dim(tiles, found[s], (rank - s) % group_size, 0)
    return tiles


def exchange_add(array, other, distance):
    moves = [(i, i ^ distance) for i in range(lax.axis_size("dp"))]
    came = lax.ppermute(array, "dp", moves)
    came, other = lax.optimization_barrier((came, other))
    return (array.astype(f32) + came.astype(f32)).astype(array.dtype), other


def place_rows(whole, rows, rank, behind, group_size):
    source = (rank - behind) % group_size
    return lax.dynamic_update_slice_in_dim(whole, rows, source * rows.shape[0], 0)


def row_parts(rows):
    dp_size = lax.axis_size("dp")
    part = -(-rows // (16 * dp_size)) * 16
    return dp_size, part


def spread_gather(shard):
    dp_size, part = row_parts(shard.shape[0])
    shard = jnp.pad(shard, ((0, part * dp_size - shard.shape[0]), (0, 0)))
    mine = lax.dynamic_slice_in_dim(shard, lax.axis_index("dp") * part, part, 0)
    whole = lax.all_gather(mine, ("tensor", "dp"), axis=0, tiled=True)
    return whole.reshape(lax.axis_size("tensor"), part * dp_size, shard.shape[1])


def body(
    hidden_in,
    lengths,
    labels,
    out_cotangent,
    w_query,
    b_query,
    w_key,
    w_value,
    b_value,
    w_out,
    b_out,
    ln1_gain,
    ln1_bias,
    w_in,
    b_in,
    w_down,
    b_down,
    ln2_gain,
    ln2_bias,
    w_student,
    b_student,
    pool_query,
    w_pool,
    b_pool,
    w_class,
    b_class,
):
    slot_len, model = hidden_in.shape
    group_size = lax.axis_size("tensor")
    own_count = slot_len // group_size
    rank = lax.axis_index("tensor")
    own_start = rank * own_count
    width = w_query.shape[1]
    hidden_width = w_in.shape[1]
    stu_cols = w_student.shape[1]
    length = lengths[0]
    pad_row = lambda row: jnp.pad(row[None, :], ((0, 0), (0, model - row.shape[0])))

    w_kv = jnp.concatenate([w_key, w_value], axis=1)
    w_project_t = jnp.concatenate([w_query.T, w_key.T, w_value.T], axis=0)
    gathered = spread_gather(jnp.concatenate([w_in, w_down, w_out], axis=0))
    w_out_all = gathered[:, model + hidden_width : model + hidden_width + width].reshape(
        group_size * width, model
    )
    w_project_all = spread_gather(w_project_t)
    stud_tile = jnp.concatenate(
        [w_student.T, b_in[None, :], pad_row(b_student), jnp.zeros((6, model), bf16)], axis=0
    )
    stud_tiles = group_tiles(stud_tile, rank, group_size)
    w_stud_t = stud_tiles[:, :stu_cols].reshape(group_size * stu_cols, model)
    b_in_all = stud_tiles[:, stu_cols : stu_cols + 1]
    b_stud_all = stud_tiles[:, stu_cols + 1, :stu_cols].reshape(1, group_size * stu_cols)

    hidden_own = lax.dynamic_slice_in_dim(hidden_in, own_start, own_count, 0)
    cot_own = lax.dynamic_slice_in_dim(out_cotangent, own_start, own_count, 0)
    chunk_at = (rank + jnp.arange(group_size, dtype=jnp.int32)) % group_size
    chunk_valid = jnp.clip(length - chunk_at * own_count, 0, own_count)
    half = group_size // 2
    first_empty = (jnp.sum(chunk_valid[:half]) == 0).astype(jnp.int32)
    second_empty = (jnp.sum(chunk_valid[half:]) == 0).astype(jnp.int32)
    info = jnp.concatenate(
        [
            rank[None],
            chunk_valid,
            first_empty[None],
            (2 - first_empty - second_empty)[None],
        ]
    ).astype(jnp.int32)
    bias_t = jnp.concatenate([b_query, jnp.zeros_like(b_query), b_value])
    hidden_rot, wide_k, wide_v, projected_t = project(
        info, hidden_in, w_kv, w_project_t, bias_t[None, width:], bias_t[:, None], group_size
    )

    outs = [None] * group_size
    lses = [None] * group_size
    attended = [None] * group_size
    for s in list(range(1, group_size)) + [0]:
        outs[s], lses[s] = attend_forward(info, wide_k, projected_t, s, group_size)
        attended[s] = shift(outs[s], s, group_size)
    attended_t = jnp.zeros((group_size * width, own_count), bf16)
    for s in range(group_size):
        source = (rank - s) % group_size
        attended_t = lax.dynamic_update_slice_in_dim(attended_t, attended[s], source * width, 0)

    resid1 = across_rows(attended_t, w_out_all) + b_out + hidden_own.astype(f32)
    first, normed1, invstd1 = normalize(resid1, ln1_gain, ln1_bias)
    first_low = first.astype(bf16)
    acts, slopes, ffn = ffn_forward(first_low, gathered, b_in_all)
    resid2 = ffn + b_down + first_low.astype(f32)
    second, normed2, invstd2 = normalize(resid2, ln2_gain, ln2_bias)
    second_low = second.astype(bf16)
    held = shift(second_low, 1, group_size)

    student_low = (against(second_low, w_stud_t) + b_stud_all.astype(f32)).astype(bf16)
    student = student_low.astype(f32)
    student_width = student.shape[1]
    head_width = student_width // POOL_HEADS
    probe_scale = 1.0 / math.sqrt(head_width)
    own_rows = own_start + lax.broadcasted_iota(jnp.int32, (own_count, 1), 0)
    row_valid = own_rows < length
    head_of = lax.broadcasted_iota(jnp.int32, (1, student_width), 1) // head_width

    def per_head(values_wide):
        whole = jnp.zeros_like(values_wide)
        for h in range(POOL_HEADS):
            part = jnp.sum(
                jnp.where(head_of == h, values_wide, 0.0), axis=-1, keepdims=True
            )
            whole = jnp.where(head_of == h, part, whole)
        return whole

    probes = pool_query[None, :]
    energies = jnp.where(row_valid, per_head(student * probes) * probe_scale, mask_fill)
    local_top = jnp.max(energies, axis=0, keepdims=True)
    local_weights = jnp.exp(energies - local_top)
    local_total = jnp.sum(local_weights, axis=0, keepdims=True)
    local_pooled = jnp.sum(local_weights * student, axis=0, keepdims=True)
    stats = jnp.concatenate(
        [local_top, local_total, local_pooled, jnp.zeros((5, student_width), f32)], axis=0
    )
    stats_all = jnp.stack([shift(stats, s, group_size) for s in range(group_size)])
    top = jnp.max(stats_all[:, 0], axis=0, keepdims=True)
    fade = jnp.exp(stats_all[:, 0] - top)
    inv_total = 1.0 / jnp.sum(fade * stats_all[:, 1], axis=0, keepdims=True)
    pooled = jnp.sum(fade * stats_all[:, 2], axis=0, keepdims=True) * inv_total
    squashed = jnp.tanh(jnp.dot(pooled, w_pool, precision=highest) + b_pool)
    logits = jnp.dot(squashed, w_class, precision=highest) + b_class
    classes = lax.broadcasted_iota(jnp.int32, logits.shape, 1)
    g_logits = jax.nn.softmax(logits, axis=-1) - (classes == labels[:, None]).astype(f32)
    grad_w_class_t = g_logits.reshape(-1, 1) * squashed
    grad_b_class = g_logits[0]
    g_u = lax.dot_general(
        g_logits, w_class, (((1,), (1,)), ((), ())), precision=highest
    ) * (1.0 - squashed * squashed)
    grad_w_pool = pooled.reshape(-1, 1) * g_u
    grad_b_pool = g_u[0]
    g_pooled = lax.dot_general(g_u, w_pool, (((1,), (1,)), ((), ())), precision=highest)
    inner = per_head(pooled * g_pooled)
    pool = jnp.exp(energies - top) * inv_total
    g_energy = pool * (per_head(student * g_pooled) - inner)
    g_stud_low = (pool * g_pooled + g_energy * probes * probe_scale).astype(bf16)
    grad_pool_query = jnp.sum(g_energy * student, axis=0) * probe_scale

    grad_second = jnp.where(row_valid, cot_own.astype(f32), 0.0) + matmul(g_stud_low, w_stud_t)
    grad_resid2, grad_ln2_gain, grad_ln2_bias = normalize_back(
        grad_second, normed2, invstd2, ln2_gain
    )
    grad_b_down = jnp.sum(grad_resid2, axis=0)
    grad_ffn_low = grad_resid2.astype(bf16)
    grad_pre, grad_first = ffn_backward(grad_ffn_low, gathered, slopes)
    grad_first, held = lax.optimization_barrier((grad_first, held))
    hidden_out = jnp.zeros((slot_len, model), bf16)
    hidden_out = place_rows(hidden_out, second_low, rank, 0, group_size)
    hidden_out = place_rows(hidden_out, held, rank, 1, group_size)
    held = shift(held, 1, group_size)
    grad_first = grad_first + grad_resid2
    grad_resid1, grad_ln1_gain, grad_ln1_bias = normalize_back(
        grad_first, normed1, invstd1, ln1_gain
    )
    grad_b_out = jnp.sum(grad_resid1, axis=0)
    grad_mix = grad_resid1.astype(bf16)
    grad_att_t = against(w_out_all, grad_mix).astype(bf16)
    grad_outs = []
    for s in range(group_size):
        target = (rank - s) % group_size
        piece = lax.dynamic_slice_in_dim(grad_att_t, target * width, width, 0)
        grad_outs.append(shift(piece, -s, group_size))

    only_once = (rank == 0).astype(f32)
    lanes = student_width
    class_count = grad_b_class.shape[0]
    columns = jnp.stack(
        [grad_b_out, grad_ln1_gain, grad_ln1_bias, grad_b_down, grad_ln2_gain, grad_ln2_bias]
    )
    class_share = -(-class_count // group_size)
    grad_w_class_t = jnp.pad(
        grad_w_class_t * only_once, ((0, class_share * group_size - class_count), (0, 0))
    ).reshape(group_size, class_share, lanes)
    tail = jnp.stack(
        [
            grad_b_pool * only_once,
            jnp.pad(grad_b_class, (0, lanes - class_count)) * only_once,
            grad_pool_query,
        ]
    )
    at = model + hidden_width
    small_at = at + width + stu_cols
    dp_size, part = row_parts(small_at + SMALL_ROWS)
    dense = (first_low, grad_pre, acts, grad_ffn_low, attended_t, grad_mix, g_stud_low, second_low)
    blocks = pack_gradients(
        dp_size, part, group_size, dense, columns, grad_w_pool * only_once, grad_w_class_t, tail
    )
    *grad_outs, blocks, w_project_all = lax.optimization_barrier(
        (*grad_outs, blocks, w_project_all)
    )
    reduced = lax.psum_scatter(
        blocks.reshape(dp_size * group_size, part, model), "dp", scatter_dimension=0, tiled=True
    )

    part_of = functools.partial(attend_backward, info, wide_k, wide_v, projected_t, hidden_rot)
    others = (1, group_size)
    own_side = (grad_outs[0][None], outs[0][None], lses[0][None])
    gq_own, gk_others, gv_others = part_of(*own_side, (0, 1), others)
    gq_own, held, grad_outs[1] = lax.optimization_barrier((gq_own, held, grad_outs[1]))
    hidden_out = place_rows(hidden_out, held, rank, 2, group_size)
    held = shift(held, 1, group_size)
    other_side = tuple(jnp.stack(side[1:]) for side in (grad_outs, outs, lses))
    gq_others = None
    w_kv_sum = None
    kv_arrived = {}
    order = sorted(range(1, group_size), key=lambda s: -min(s, group_size - s))
    for step, s in enumerate(order):
        gq_others, low, w_kv_sum = part_of(
            *other_side,
            others,
            (s, s + 1),
            gq=gq_others,
            gkv=(gk_others, gv_others),
            wkv=w_kv_sum,
            gkv_at=s - 1,
            end_k=True,
        )
        kv_arrived[s] = shift(low[0], s, group_size)
        if step == 1:
            earlier = order[0]
            reduced, held, gq_others, kv_arrived[earlier] = lax.optimization_barrier(
                (reduced, held, gq_others, kv_arrived[earlier])
            )
            reduced = lax.psum_scatter(reduced, "tensor", scatter_dimension=0, tiled=True)
            hidden_out = place_rows(hidden_out, held, rank, 3, group_size)
    gkv_own = None
    w_q_sum = None
    q_arrived = {}
    for step, s in enumerate(order):
        low, *gkv_own, w_q_sum = part_of(
            grad_outs[s][None],
            outs[s][None],
            lses[s][None],
            (s, s + 1),
            (0, 1),
            gq=gq_others,
            gkv=gkv_own,
            wq=w_q_sum,
            gq_at=s - 1,
            end_q=True,
        )
        q_arrived[s] = shift(low[0], s, group_size)
        if step < 2:
            earlier = order[step + 1]
            kv_arrived[earlier], w_q_sum = lax.optimization_barrier(
                (kv_arrived[earlier], w_q_sum)
            )
    grad_resid1, w_q_sum = lax.optimization_barrier((grad_resid1, w_q_sum))
    grad_in_own = add_input_gradients(
        info, grad_resid1, w_project_all, kv_arrived, {}, f32
    )
    gq_own, reduced, grad_in_own, *arrivals = lax.optimization_barrier(
        (gq_own, reduced, grad_in_own, *q_arrived.values())
    )
    q_arrived = dict(zip(q_arrived, arrivals))
    reduced = lax.all_gather(reduced[0], "dp", axis=0, tiled=True)
    low_q, low_kv, late = part_of(
        *own_side,
        (0, 1),
        (0, 1),
        gq=gq_own,
        gkv=gkv_own,
        wq=w_q_sum,
        wkv=w_kv_sum,
        end_q=True,
        end_k=True,
    )
    late, grad_in_own = exchange_add(late, grad_in_own, 1)
    q_arrived[0] = low_q[0]
    grad_in_own = add_input_gradients(
        info, grad_in_own, w_project_all, {0: low_kv[0]}, q_arrived, bf16
    )
    grad_in, grad_in_own = lax.optimization_barrier((hidden_rot, grad_in_own))
    held = shift(grad_in_own, 1, group_size)
    grad_in = place_rows(grad_in, grad_in_own, rank, 0, group_size)
    small_own = reduced[small_at : small_at + SMALL_ROWS]
    small = group_tiles(small_own[:, : 4 * UNIT], rank, group_size)
    late, held = exchange_add(late, held, 2)
    grad_in = place_rows(grad_in, held, rank, 1, group_size)
    held = shift(held, 1, group_size)
    distance = 4
    while distance < dp_size:
        late, held = exchange_add(late, held, distance)
        distance *= 2
    held, small = lax.optimization_barrier((held, small))
    for s in range(2, group_size):
        grad_in = place_rows(grad_in, held, rank, s, group_size)
        if s < group_size - 1:
            held = shift(held, 1, group_size)
    late = late.astype(f32)
    small = small.astype(f32)
    small_own = small_own[:, 4 * UNIT :].astype(f32)
    grad_w_pool = small[:, :, :UNIT].reshape(grad_w_pool.shape)
    column_share = -(-columns.size // (UNIT * group_size))
    columns = small[:, :column_share, UNIT : 2 * UNIT].reshape(-1)[: columns.size].reshape(
        columns.shape
    )
    grad_w_class = (
        small[:, :class_share, 2 * UNIT : 3 * UNIT].reshape(-1, lanes)[:class_count].T
    )
    grad_b_pool = small[0, 0, 3 * UNIT :]
    grad_b_class = small[0, 1, 3 * UNIT : 3 * UNIT + class_count]
    grad_pool_query = small[0, 2, 3 * UNIT :]
    grad_b_in = small_own[: hidden_width // UNIT, :UNIT].reshape(-1)
    grad_b_stud = lax.dynamic_slice_in_dim(small_own[0, UNIT:], rank * stu_cols, stu_cols, 0)

    reduced = reduced.astype(f32)
    return (
        hidden_out,
        logits,
        grad_in,
        late[:width, :model].T,
        late[:width, model],
        late[width : 2 * width, :model].T,
        late[2 * width :, :model].T,
        late[2 * width :, model],
        reduced[at : at + width],
        columns[0],
        columns[1],
        columns[2],
        reduced[:model],
        grad_b_in,
        reduced[model:at],
        columns[3],
        columns[4],
        columns[5],
        reduced[at + width : small_at].T,
        grad_b_stud,
        grad_pool_query,
        grad_w_pool,
        grad_b_pool,
        grad_w_class,
        grad_b_class,
    )


def solution(mesh):
    by_dp = P("dp", None)
    cols = P(None, "tensor")
    rows = P("tensor", None)
    cut = P("tensor")
    in_specs = (
        (by_dp, P("dp"), P("dp"), by_dp, cols, cut, cols, cols, cut, rows, P(), P(), P(), cols)
        + (cut, rows, P(), P(), P(), cols, cut, P(), P(), P(), P(), P())
    )
    out_specs = (
        (by_dp, by_dp, by_dp, cols, cut, cols, cols, cut, rows, P(), P(), P(), cols, cut, rows)
        + (P(), P(), P(), cols, cut, P(), P(), P(), P(), P())
    )
    return jax.shard_map(body, mesh=mesh, in_specs=in_specs, out_specs=out_specs, check_vma=False)
```

```python
import functools
import math

import jax
import jax.numpy as jnp
from jax import lax
from jax.experimental import pallas as pl
from jax.experimental.pallas import tpu as pltpu
from jax.sharding import PartitionSpec as P

HD = 64
POOL_HEADS = 2

epsilon = 1e-06
mask_fill = -1e30
highest = lax.Precision.HIGHEST
bf16 = jnp.bfloat16
f32 = jnp.float32
SCORE_SCALE = 1.0 / math.sqrt(HD)
SCORE_SCALE_2 = math.log2(math.e) * SCORE_SCALE
SAFE_SCORE = 50.0
PLANE = 256
UNIT = 128
SMALL_ROWS = 32
VMEM_LIMIT = 60 * 1024 * 1024


def matmul(left, right):
    return jnp.dot(left, right, preferred_element_type=f32)


def across_rows(left, right):
    return lax.dot_general(left, right, (((0,), (0,)), ((), ())), preferred_element_type=f32)


def against(left, right):
    return lax.dot_general(left, right, (((1,), (1,)), ((), ())), preferred_element_type=f32)


def project_kernel(
    width, info_ref, h_ref, wkv_ref, wt_ref, bkv_ref, bt_ref, rot_ref, k_ref, v_ref, t_ref, n_ref
):
    hidden = h_ref[...]
    rot_ref[...] = hidden
    rows = hidden.shape[0]
    valid = info_ref[1 + pl.program_id(0)]
    key_value = (matmul(hidden, wkv_ref[...]) + bkv_ref[...]).astype(bf16)
    row = lax.broadcasted_iota(jnp.int32, (rows, PLANE - width), 0)
    lane = lax.broadcasted_iota(jnp.int32, (rows, PLANE - width), 1)
    k_ref[:, :width] = key_value[:, :width]
    k_ref[:, width:] = jnp.where((lane == 0) & (row >= valid), mask_fill, 0.0).astype(bf16)
    v_ref[:, :width] = key_value[:, width:]
    v_ref[:, width:] = jnp.zeros((rows, PLANE - width), bf16)
    part = lax.broadcasted_iota(jnp.int32, (3 * width, 1), 0)
    scale = jnp.where(part < width, SCORE_SCALE_2, 1.0)
    turned = ((against(wt_ref[...], hidden) + bt_ref[...]) * scale).astype(bf16)
    t_ref[...] = turned
    n_ref[...] = jnp.zeros_like(n_ref)
    for h in range(2 * width // HD):
        rows_h = turned[HD * h : HD * h + HD].astype(f32)
        norms = jnp.sum(rows_h * rows_h, axis=0, keepdims=True)
        n_ref[0, h : h + 1, :] = jnp.broadcast_to(
            jnp.max(norms, axis=1, keepdims=True), (1, UNIT)
        )


def project(info, hidden_in, w_kv, w_all_t, bias_kv, bias_t, chunks):
    slot_len, model = hidden_in.shape
    width = w_all_t.shape[0] // 3
    rows = slot_len // chunks
    whole = lambda c, info_ref: (0, 0)
    return pl.pallas_call(
        functools.partial(project_kernel, width),
        grid_spec=pltpu.PrefetchScalarGridSpec(
            num_scalar_prefetch=1,
            grid=(chunks,),
            in_specs=[
                pl.BlockSpec((rows, model), lambda c, info_ref: ((info_ref[0] + c) % chunks, 0)),
                pl.BlockSpec((model, 2 * width), whole),
                pl.BlockSpec((3 * width, model), whole),
                pl.BlockSpec((1, 2 * width), whole),
                pl.BlockSpec((3 * width, 1), whole),
            ],
            out_specs=[
                pl.BlockSpec((rows, model), lambda c, info_ref: (c, 0)),
                pl.BlockSpec((rows, PLANE), lambda c, info_ref: (c, 0)),
                pl.BlockSpec((rows, PLANE), lambda c, info_ref: (c, 0)),
                pl.BlockSpec((3 * width, rows), lambda c, info_ref: (0, c)),
                pl.BlockSpec((1, 8, UNIT), lambda c, info_ref: (c, 0, 0)),
            ],
        ),
        out_shape=(
            jax.ShapeDtypeStruct((slot_len, model), bf16),
            jax.ShapeDtypeStruct((slot_len, PLANE), bf16),
            jax.ShapeDtypeStruct((slot_len, PLANE), bf16),
            jax.ShapeDtypeStruct((3 * width, slot_len), bf16),
            jax.ShapeDtypeStruct((chunks, 8, UNIT), f32),
        ),
        compiler_params=pltpu.CompilerParams(vmem_limit_bytes=VMEM_LIMIT),
        cost_estimate=pl.CostEstimate(flops=1, bytes_accessed=1, transcendentals=0),
        name="project",
    )(info, hidden_in, w_kv, w_all_t, bias_kv, bias_t)


def forward_kernel(
    bq, bk, heads, info_ref, n_ref, k_ref, qt_ref, vt_ref, ot_ref, lse_ref, head_q, acc
):
    width = HD * heads
    chunks = info_ref.shape[0] - 3
    first_tile = info_ref[1 + chunks]
    tile_count = info_ref[2 + chunks]
    row = lax.broadcasted_iota(jnp.int32, (PLANE, bq), 0)
    for h in range(heads):
        head_q[h] = jnp.where(row == width, 1.0, 0.0).astype(bf16)
    most = jnp.max(n_ref[...], axis=0)
    small_scores = jnp.max(most[:heads] * most[heads : 2 * heads]) < SAFE_SCORE * SAFE_SCORE

    def head_values(h, k0):
        return vt_ref[HD * h : HD * h + HD, pl.ds(k0, bk)]

    def key_tile(step):
        k0 = pl.multiple_of(((first_tile + step) % 2) * bk, bk)
        return k0, k_ref[pl.ds(k0, bk), :]

    def run(key_step, start, finish):
        def query_step(qb, unused):
            q0 = pl.multiple_of(qb * bq, bq)
            for h in range(heads):
                own = slice(HD * h, HD * h + HD)
                head_q[h, own, :] = qt_ref[own, pl.ds(q0, bq)]
            acc[...] = jnp.zeros_like(acc)
            done = lax.fori_loop(0, tile_count, key_step, start)
            for h in range(heads):
                total, lse = finish(done[h])
                ot_ref[HD * h : HD * h + HD, pl.ds(q0, bq)] = (acc[h] * (1.0 / total)).astype(
                    bf16
                )
                lse_ref[pl.ds(h, 1), pl.ds(q0, bq)] = lse
            return unused

        lax.fori_loop(0, qt_ref.shape[1] // bq, query_step, 0)

    @pl.when(small_scores)
    def unshifted():
        def key_step(step, totals):
            k0, keys = key_tile(step)
            kept = []
            for h in range(heads):
                weights = jnp.exp2(matmul(keys, head_q[h]))
                kept.append(totals[h] + jnp.sum(weights, axis=0, keepdims=True))
                acc[h] += matmul(head_values(h, k0), weights.astype(bf16))
            return tuple(kept)

        start = tuple(jnp.zeros((1, bq), f32) for _ in range(heads))
        run(key_step, start, lambda total: (total, jnp.log2(total)))

    @pl.when(jnp.logical_not(small_scores))
    def shifted():
        def key_step(step, carry):
            k0, keys = key_tile(step)
            kept = []
            for h in range(heads):
                scores = matmul(keys, head_q[h])
                top, total = carry[h]
                new_top = jnp.maximum(top, jnp.max(scores, axis=0, keepdims=True))
                weights = jnp.exp2(scores - new_top)
                fade = jnp.exp2(top - new_top)
                total = fade * total + jnp.sum(weights, axis=0, keepdims=True)
                acc[h] = fade * acc[h] + matmul(head_values(h, k0), weights.astype(bf16))
                kept.append((new_top, total))
            return tuple(kept)

        start = tuple(
            (jnp.full((1, bq), mask_fill, f32), jnp.zeros((1, bq), f32)) for _ in range(heads)
        )
        run(key_step, start, lambda pair: (pair[1], pair[0] + jnp.log2(pair[1])))


def attend_forward(info, norms, wide_k, projected_t, chunk, chunks):
    slot_len = wide_k.shape[0]
    width = projected_t.shape[0] // 3
    heads = width // HD
    rows = slot_len // chunks
    bq, bk = min(512, rows), slot_len // 2
    pairs = heads * rows * slot_len
    return pl.pallas_call(
        functools.partial(forward_kernel, bq, bk, heads),
        grid=(1,),
        out_shape=(
            jax.ShapeDtypeStruct((width, rows), bf16),
            jax.ShapeDtypeStruct((8, rows), f32),
        ),
        in_specs=[
            pl.BlockSpec(memory_space=pltpu.SMEM),
            pl.BlockSpec(norms.shape, lambda i: (0, 0, 0)),
            pl.BlockSpec((slot_len, PLANE), lambda i: (0, 0)),
            pl.BlockSpec((width, rows), lambda i: (0, chunk)),
            pl.BlockSpec((width, slot_len), lambda i: (2, 0)),
        ],
        out_specs=[
            pl.BlockSpec((width, rows), lambda i: (0, 0)),
            pl.BlockSpec((8, rows), lambda i: (0, 0)),
        ],
        scratch_shapes=[
            pltpu.VMEM((heads, PLANE, bq), bf16),
            pltpu.VMEM((heads, HD, bq), f32),
        ],
        compiler_params=pltpu.CompilerParams(vmem_limit_bytes=VMEM_LIMIT),
        cost_estimate=pl.CostEstimate(flops=1, bytes_accessed=1, transcendentals=0),
        name="attend_forward",
    )(info, norms, wide_k, projected_t, projected_t)


def backward_kernel(bq, heads, q_span, k_span, rows, has, end_q, end_k, *refs):
    width = HD * heads
    one_key = k_span[1] - k_span[0] == 1
    refs = list(refs)
    info_ref, k_ref, v_ref, kt_ref, qt_ref, got_ref, ot_ref, lse_ref = refs[:8]
    del refs[:8]
    hidden_ref = refs.pop(0) if end_q or end_k else None
    gq_in = refs.pop(0) if "q" in has else None
    gk_in = refs.pop(0) if "k" in has else None
    gv_in = refs.pop(0) if "k" in has else None
    wq_in = refs.pop(0) if "wq" in has else None
    wkv_in = refs.pop(0) if "wkv" in has else None
    gq_out = refs.pop(0)
    gkv_low = refs.pop(0) if end_k else None
    gk = None if end_k else refs.pop(0)
    gv = None if end_k else refs.pop(0)
    w_out_ref = refs.pop(0) if end_q or end_k else None
    head_q, head_go = refs[:2]
    del refs[:2]
    gq = refs.pop(0) if end_q else gq_out
    if end_k:
        gk, gv = refs.pop(0), refs.pop(0)
    gq[...] = jnp.zeros_like(gq) if gq_in is None else gq_in[...]
    gk[...] = jnp.zeros_like(gk) if gk_in is None else gk_in[...]
    gv[...] = jnp.zeros_like(gv) if gv_in is None else gv_in[...]
    row = lax.broadcasted_iota(jnp.int32, (PLANE, bq), 0)
    for h in range(heads):
        head_q[h] = jnp.where(row == width, 1.0, 0.0).astype(bf16)
        head_go[h] = jnp.zeros((PLANE, bq), bf16)

    def chunk_step(q, unused):
        def query_step(qb, inner):
            q0 = pl.multiple_of(qb * bq, bq)
            span = pl.ds(q0, bq)
            all_span = pl.ds(pl.multiple_of(q * rows + q0, bq), bq)
            deltas = []
            tops = []
            for h in range(heads):
                own = slice(HD * h, HD * h + HD)
                head_q[h, own, :] = qt_ref[own, all_span]
                grad_out = got_ref[q - q_span[0], own, span]
                head_go[h, own, :] = grad_out
                outs = ot_ref[q - q_span[0], own, span]
                deltas.append(
                    jnp.sum(grad_out.astype(f32) * outs.astype(f32), axis=0, keepdims=True)
                )
                tops.append(lse_ref[q - q_span[0], pl.ds(h, 1), span])

            def key_step(k, innermost):
                @pl.when(info_ref[1 + k] > 0)
                def one_tile():
                    at = k - k_span[0]
                    k0 = pl.multiple_of((at if one_key else k) * rows, rows)
                    keys = k_ref[pl.ds(k0, rows), :]
                    values = v_ref[pl.ds(k0, rows), :]
                    grad_v = None
                    grad_k = None
                    for h in range(heads):
                        own = slice(HD * h, HD * h + HD)
                        scores = matmul(keys, head_q[h])
                        grad_weights = matmul(values, head_go[h])
                        weights = jnp.exp2(scores - tops[h])
                        grad_scores = (weights * (grad_weights - deltas[h])).astype(bf16)
                        more_v = against(weights.astype(bf16), head_go[h])
                        more_k = against(grad_scores, head_q[h])
                        grad_v = more_v if grad_v is None else grad_v + more_v
                        grad_k = more_k if grad_k is None else grad_k + more_k
                        gq[q - q_span[0], own, span] += matmul(
                            kt_ref[own, pl.ds(k0, rows)], grad_scores
                        )
                    gk[at] += grad_k
                    gv[at] += grad_v

                return innermost

            lax.fori_loop(k_span[0], k_span[1], key_step, 0)
            return inner

        lax.fori_loop(0, (info_ref[1 + q] + bq - 1) // bq, query_step, 0)
        return unused

    lax.fori_loop(q_span[0], q_span[1], chunk_step, 0)
    ones = jnp.ones((rows, UNIT), bf16)

    def add_weights(first_row, product, sum_in):
        lead = slice(first_row, first_row + product(ones).shape[0])
        model = hidden_ref.shape[1]
        for lanes, right in ((slice(0, model), hidden_ref[...]), (slice(model, None), ones)):
            value = product(right)
            if sum_in is not None:
                value = value + sum_in[:, lanes]
            w_out_ref[lead, lanes] = value.astype(w_out_ref.dtype)

    if end_q:
        low = (gq[0] * SCORE_SCALE).astype(bf16)
        gq_out[0] = low
        add_weights(0, lambda right: matmul(low, right), wq_in)
    if end_k:
        gkv_low[0, :, :width] = (gk[0, :, :width] * math.log(2.0)).astype(bf16)
        gkv_low[0, :, width:] = gv[0, :, :width].astype(bf16)
        both = gkv_low[0]
        add_weights(
            width if end_q else 0,
            lambda right: lax.dot_general(
                both, right, (((0,), (0,)), ((), ())), preferred_element_type=f32
            ),
            wkv_in,
        )


def attend_backward(
    info,
    wide_k,
    wide_v,
    projected_t,
    hidden_rot,
    grad_out_t,
    out_t,
    lse,
    q_span,
    k_span,
    gq=None,
    gkv=None,
    wq=None,
    wkv=None,
    gq_at=0,
    gkv_at=0,
    end_q=False,
    end_k=False,
):
    chunks = info.shape[0] - 3
    slot_len = wide_k.shape[0]
    width = projected_t.shape[0] // 3
    model = hidden_rot.shape[1]
    heads = width // HD
    rows = slot_len // chunks
    nq, nk = q_span[1] - q_span[0], k_span[1] - k_span[0]
    bq = min(512, rows)
    k_at = k_span[0]
    if nk == 1:
        key_spec = pl.BlockSpec((rows, PLANE), lambda i: (k_at, 0))
        kt_spec = pl.BlockSpec((width, rows), lambda i: (1, k_at))
    else:
        key_spec = pl.BlockSpec((slot_len, PLANE), lambda i: (0, 0))
        kt_spec = pl.BlockSpec((width, slot_len), lambda i: (1, 0))
    at_zero = lambda i: (0, 0, 0)
    gq_shape, gk_shape = (nq, width, rows), (nk, rows, PLANE)
    gq_spec, gk_spec = pl.BlockSpec(gq_shape, at_zero), pl.BlockSpec(gk_shape, at_zero)
    whole2 = lambda array: pl.BlockSpec(array.shape, lambda i: (0, 0))
    operands = [info, wide_k, wide_v, projected_t, projected_t, grad_out_t, out_t, lse]
    in_specs = [
        pl.BlockSpec(memory_space=pltpu.SMEM),
        key_spec,
        key_spec,
        kt_spec,
        pl.BlockSpec((width, slot_len), lambda i: (0, 0)),
        gq_spec,
        gq_spec,
        pl.BlockSpec((nq, 8, rows), at_zero),
    ]
    has = []
    if end_q or end_k:
        ended = k_at if end_k else q_span[0]
        operands.append(hidden_rot)
        in_specs.append(pl.BlockSpec((rows, model), lambda i: (ended, 0)))
    if gq is not None:
        has.append("q")
        operands.append(gq)
        in_specs.append(pl.BlockSpec(gq_shape, lambda i: (gq_at, 0, 0)))
    if gkv is not None:
        has.append("k")
        operands.extend(gkv)
        in_specs.extend([pl.BlockSpec(gk_shape, lambda i: (gkv_at, 0, 0))] * 2)
    for name, array in (("wq", wq), ("wkv", wkv)):
        if array is not None:
            has.append(name)
            operands.append(array)
            in_specs.append(whole2(array))
    out_shape = [jax.ShapeDtypeStruct(gq_shape, bf16 if end_q else f32)]
    out_specs = [gq_spec]
    scratch = [
        pltpu.VMEM((heads, PLANE, bq), bf16),
        pltpu.VMEM((heads, PLANE, bq), bf16),
    ]
    if end_q:
        scratch.append(pltpu.VMEM(gq_shape, f32))
    if end_k:
        out_shape.append(jax.ShapeDtypeStruct((nk, rows, 2 * width), bf16))
        out_specs.append(pl.BlockSpec((nk, rows, 2 * width), at_zero))
        scratch.extend([pltpu.VMEM(gk_shape, f32)] * 2)
    else:
        out_shape.extend([jax.ShapeDtypeStruct(gk_shape, f32)] * 2)
        out_specs.extend([gk_spec] * 2)
    if end_q or end_k:
        w_rows = width * ((1 if end_q else 0) + (2 if end_k else 0))
        w_shape = (w_rows, model + UNIT)
        out_shape.append(jax.ShapeDtypeStruct(w_shape, bf16 if end_q and end_k else f32))
        out_specs.append(pl.BlockSpec(w_shape, lambda i: (0, 0)))
    pairs = heads * nq * nk * rows * rows
    return pl.pallas_call(
        functools.partial(
            backward_kernel, bq, heads, q_span, k_span, rows, tuple(has), end_q, end_k
        ),
        grid=(1,),
        out_shape=tuple(out_shape),
        in_specs=in_specs,
        out_specs=out_specs,
        scratch_shapes=scratch,
        compiler_params=pltpu.CompilerParams(vmem_limit_bytes=VMEM_LIMIT),
        cost_estimate=pl.CostEstimate(flops=1, bytes_accessed=1, transcendentals=0),
        name="attend_backward",
    )(*operands)


def input_kernel(width, kv_from, q_from, rank_ref, sum_ref, w_ref, *refs):
    out_ref = refs[-1]
    groups = w_ref.shape[0]
    total = sum_ref[...]
    for at, behind in enumerate(kv_from + q_from):
        source = lax.rem(rank_ref[0] + groups - behind, groups)
        if at < len(kv_from):
            total += matmul(refs[at][...], w_ref[source, width : 3 * width, :])
        else:
            total += across_rows(refs[at][...], w_ref[source, :width, :])
    out_ref[...] = total.astype(out_ref.dtype)


def add_input_gradients(info, so_far, w_project_all, kv_pieces, q_pieces, dtype):
    width = next(iter(kv_pieces.values())).shape[1] // 2
    count, model = so_far.shape
    rows = min(256, count)
    pieces = list(kv_pieces.values()) + list(q_pieces.values())
    by_rows = pl.BlockSpec((rows, model), lambda r: (r, 0))
    return pl.pallas_call(
        functools.partial(input_kernel, width, tuple(kv_pieces), tuple(q_pieces)),
        grid=(count // rows,),
        in_specs=[
            pl.BlockSpec(memory_space=pltpu.SMEM),
            by_rows,
            pl.BlockSpec(w_project_all.shape, lambda r: (0, 0, 0)),
        ]
        + [pl.BlockSpec((rows, 2 * width), lambda r: (r, 0))] * len(kv_pieces)
        + [pl.BlockSpec((width, rows), lambda r: (0, r))] * len(q_pieces),
        out_specs=by_rows,
        out_shape=jax.ShapeDtypeStruct(so_far.shape, dtype),
        compiler_params=pltpu.CompilerParams(vmem_limit_bytes=VMEM_LIMIT),
        cost_estimate=pl.CostEstimate(flops=1, bytes_accessed=1, transcendentals=0),
        name="add_input_gradients",
    )(info, so_far, w_project_all, *pieces)


def ffn_forward_kernel(row_step, x_ref, w_in_ref, b_ref, w_down_ref, act_ref, slope_ref, out_ref):
    @pl.when(pl.program_id(0) == 0)
    def start():
        out_ref[...] = jnp.zeros_like(out_ref)

    for r0 in range(0, x_ref.shape[0], row_step):
        rows = slice(r0, r0 + row_step)
        pre = matmul(x_ref[rows, :], w_in_ref[0]) + b_ref[0].astype(f32)
        below = 0.5 + 0.5 * lax.erf(pre * math.sqrt(0.5))
        density = jnp.exp(-0.5 * pre * pre) * (1.0 / math.sqrt(2.0 * math.pi))
        act = (pre * below).astype(bf16)
        act_ref[0, rows, :] = act
        slope_ref[0, rows, :] = (below + pre * density).astype(bf16)
        more = matmul(act, w_down_ref[0])
        out_ref[rows, :] += more


def ffn_forward(first_low, gathered, b_in_all):
    count, model = first_low.shape
    groups = gathered.shape[0]
    units = b_in_all.shape[-1]
    block = pl.BlockSpec((1, count, units), lambda b: (b, 0, 0))
    return pl.pallas_call(
        functools.partial(ffn_forward_kernel, min(256, count)),
        grid=(groups,),
        in_specs=[
            pl.BlockSpec((count, model), lambda b: (0, 0)),
            pl.BlockSpec((1, model, units), lambda b: (b, 0, 0)),
            pl.BlockSpec((1, 1, units), lambda b: (b, 0, 0)),
            pl.BlockSpec((1, units, model), lambda b: (b, 1, 0)),
        ],
        out_specs=[block, block, pl.BlockSpec((count, model), lambda b: (0, 0))],
        out_shape=(
            jax.ShapeDtypeStruct((groups, count, units), bf16),
            jax.ShapeDtypeStruct((groups, count, units), bf16),
            jax.ShapeDtypeStruct((count, model), f32),
        ),
        compiler_params=pltpu.CompilerParams(vmem_limit_bytes=VMEM_LIMIT),
        cost_estimate=pl.CostEstimate(flops=1, bytes_accessed=1, transcendentals=0),
        name="ffn_forward",
    )(first_low, gathered, b_in_all, gathered)


def ffn_backward_kernel(row_step, g_ref, w_in_ref, w_down_ref, slope_ref, pre_ref, out_ref):
    @pl.when(pl.program_id(0) == 0)
    def start():
        out_ref[...] = jnp.zeros_like(out_ref)

    for r0 in range(0, g_ref.shape[0], row_step):
        rows = slice(r0, r0 + row_step)
        grad_act = against(g_ref[rows, :], w_down_ref[0])
        grad_pre = (grad_act * slope_ref[0, rows, :].astype(f32)).astype(bf16)
        pre_ref[0, rows, :] = grad_pre
        more = against(grad_pre, w_in_ref[0])
        out_ref[rows, :] += more


def ffn_backward(grad_ffn_low, gathered, slopes):
    count, model = grad_ffn_low.shape
    groups, _, units = slopes.shape
    block = pl.BlockSpec((1, count, units), lambda b: (b, 0, 0))
    return pl.pallas_call(
        functools.partial(ffn_backward_kernel, min(256, count)),
        grid=(groups,),
        in_specs=[
            pl.BlockSpec((count, model), lambda b: (0, 0)),
            pl.BlockSpec((1, model, units), lambda b: (b, 0, 0)),
            pl.BlockSpec((1, units, model), lambda b: (b, 1, 0)),
            block,
        ],
        out_specs=[block, pl.BlockSpec((count, model), lambda b: (0, 0))],
        out_shape=(
            jax.ShapeDtypeStruct((groups, count, units), bf16),
            jax.ShapeDtypeStruct((count, model), f32),
        ),
        compiler_params=pltpu.CompilerParams(vmem_limit_bytes=VMEM_LIMIT),
        cost_estimate=pl.CostEstimate(flops=1, bytes_accessed=1, transcendentals=0),
        name="ffn_backward",
    )(grad_ffn_low, gathered, gathered, slopes)


def pack_kernel(
    dp_size,
    part,
    first_ref,
    gpre_ref,
    act_ref,
    gffn_ref,
    att_ref,
    gmix_ref,
    gstud_ref,
    second_ref,
    columns_ref,
    pool_ref,
    class_ref,
    tail_ref,
    out_ref,
    stud_acc,
    small,
):
    b = pl.program_id(0)
    at = 0

    def store(rows_value):
        nonlocal at
        done = 0
        count = rows_value.shape[0]
        while done < count:
            d, offset = divmod(at, part)
            take = min(part - offset, count - done)
            out_ref[d, 0, offset : offset + take, :] = rows_value[done : done + take].astype(bf16)
            done += take
            at += take

    store(across_rows(first_ref[...], gpre_ref[0]))
    store(across_rows(act_ref[0], gffn_ref[...]))
    store(matmul(att_ref[...], gmix_ref[...]))
    groups = pl.num_programs(0)
    stud_cols = stud_acc.shape[1]

    @pl.when(b == 0)
    def student():
        whole = across_rows(gstud_ref[...], second_ref[...])
        for i in range(stud_acc.shape[0]):
            stud_acc[i] = whole[i * stud_cols : (i + 1) * stud_cols]

    store(stud_acc[b])
    small[...] = jnp.zeros_like(small)
    small[:, :UNIT] = pool_ref[...]
    units = columns_ref.shape[1] // UNIT
    count = columns_ref.shape[0] * units
    share = -(-count // stud_acc.shape[0])
    for block in range(stud_acc.shape[0]):

        @pl.when(b == block)
        def own_columns():
            for r in range(share):
                u = block * share + r
                if u < count:
                    lanes = slice((u % units) * UNIT, (u % units + 1) * UNIT)
                    small[r : r + 1, UNIT : 2 * UNIT] = columns_ref[
                        u // units : u // units + 1, lanes
                    ]

    small[: class_ref.shape[1], 2 * UNIT : 3 * UNIT] = class_ref[0]

    @pl.when(b == 0)
    def tail_rows():
        small[: tail_ref.shape[0], 3 * UNIT : 4 * UNIT] = tail_ref[...]

    grad_b_in = jnp.sum(gpre_ref[0].astype(f32), axis=0, keepdims=True)
    for u in range(grad_b_in.shape[1] // UNIT):
        small[u : u + 1, 4 * UNIT : 5 * UNIT] = grad_b_in[:, u * UNIT : (u + 1) * UNIT]
    small[0:1, 5 * UNIT : 6 * UNIT] = jnp.sum(gstud_ref[...].astype(f32), axis=0, keepdims=True)
    store(small[...])
    if at < dp_size * part:
        store(jnp.zeros((dp_size * part - at, small.shape[1]), f32))


def pack_gradients(dp_size, part, groups, dense, columns, pool, classes, tail):
    first_low, grad_pre, acts, grad_ffn, attended_t, grad_mix, grad_stud, second_low = dense
    count, model = first_low.shape
    units = acts.shape[2]
    width = attended_t.shape[0] // groups
    students = grad_stud.shape[1]
    stud_cols = students // groups
    rows = lambda cols: pl.BlockSpec((count, cols), lambda b: (0, 0))
    block = pl.BlockSpec((1, count, units), lambda b: (b, 0, 0))
    whole = lambda array: pl.BlockSpec(array.shape, lambda b: (0,) * array.ndim)
    return pl.pallas_call(
        functools.partial(pack_kernel, dp_size, part),
        grid=(groups,),
        in_specs=[
            rows(model),
            block,
            block,
            rows(model),
            pl.BlockSpec((width, count), lambda b: (b, 0)),
            rows(model),
            rows(students),
            rows(model),
            whole(columns),
            pl.BlockSpec((pool.shape[0] // groups, pool.shape[1]), lambda b: (b, 0)),
            pl.BlockSpec((1,) + classes.shape[1:], lambda b: (b, 0, 0)),
            whole(tail),
        ],
        out_specs=pl.BlockSpec((dp_size, 1, part, model), lambda b: (0, b, 0, 0)),
        out_shape=jax.ShapeDtypeStruct((dp_size, groups, part, model), bf16),
        scratch_shapes=[
            pltpu.VMEM((groups, stud_cols, model), f32),
            pltpu.VMEM((SMALL_ROWS, model), f32),
        ],
        compiler_params=pltpu.CompilerParams(vmem_limit_bytes=VMEM_LIMIT),
        cost_estimate=pl.CostEstimate(flops=1, bytes_accessed=1, transcendentals=0),
        name="pack_gradients",
    )(
        first_low,
        grad_pre,
        acts,
        grad_ffn,
        attended_t,
        grad_mix,
        grad_stud,
        second_low,
        columns,
        pool,
        classes,
        tail,
    )


def normalize(resid, gain, shift):
    center = resid - jnp.mean(resid, axis=-1, keepdims=True)
    invstd = lax.rsqrt(jnp.mean(center * center, axis=-1, keepdims=True) + epsilon)
    normed = center * invstd
    return (normed * gain + shift, normed, invstd)


def normalize_back(grad, normed, invstd, gain):
    scaled = grad * gain
    inner = (
        scaled
        - jnp.mean(scaled, axis=-1, keepdims=True)
        - normed * jnp.mean(scaled * normed, axis=-1, keepdims=True)
    )
    return (invstd * inner, jnp.sum(grad * normed, axis=0), jnp.sum(grad, axis=0))


def shift(array, ahead, group_size):
    if ahead % group_size == 0:
        return array
    moves = [(i, (i + ahead) % group_size) for i in range(group_size)]
    return lax.ppermute(array, "tensor", moves)


def send_tiles(tile, group_size):
    return [shift(tile, s, group_size) for s in range(group_size)]


def order_tiles(found, rank):
    tile, group_size = found[0], len(found)
    tiles = jnp.zeros((group_size,) + tile.shape, tile.dtype)
    for s in range(group_size):
        tiles = lax.dynamic_update_index_in_dim(tiles, found[s], (rank - s) % group_size, 0)
    return tiles


def exchange_add(array, other, distance):
    moves = [(i, i ^ distance) for i in range(lax.axis_size("dp"))]
    came = lax.ppermute(array, "dp", moves)
    came, other = lax.optimization_barrier((came, other))
    return (array.astype(f32) + came.astype(f32)).astype(array.dtype), other


def place_rows(whole, rows, rank, behind, group_size):
    source = (rank - behind) % group_size
    return lax.dynamic_update_slice_in_dim(whole, rows, source * rows.shape[0], 0)


def row_parts(rows):
    dp_size = lax.axis_size("dp")
    part = -(-rows // (16 * dp_size)) * 16
    return dp_size, part


def spread_parts(shard):
    dp_size, part = row_parts(shard.shape[0])
    shard = jnp.pad(shard, ((0, part * dp_size - shard.shape[0]), (0, 0)))
    return lax.dynamic_slice_in_dim(shard, lax.axis_index("dp") * part, part, 0)


def spread_gather(shard):
    mine = spread_parts(shard)
    part, dp_size = mine.shape[0], lax.axis_size("dp")
    whole = lax.all_gather(mine, ("tensor", "dp"), axis=0, tiled=True)
    return whole.reshape(lax.axis_size("tensor"), part * dp_size, shard.shape[1])


def body(
    hidden_in,
    lengths,
    labels,
    out_cotangent,
    w_query,
    b_query,
    w_key,
    w_value,
    b_value,
    w_out,
    b_out,
    ln1_gain,
    ln1_bias,
    w_in,
    b_in,
    w_down,
    b_down,
    ln2_gain,
    ln2_bias,
    w_student,
    b_student,
    pool_query,
    w_pool,
    b_pool,
    w_class,
    b_class,
):
    slot_len, model = hidden_in.shape
    group_size = lax.axis_size("tensor")
    own_count = slot_len // group_size
    rank = lax.axis_index("tensor")
    own_start = rank * own_count
    width = w_query.shape[1]
    hidden_width = w_in.shape[1]
    stu_cols = w_student.shape[1]
    length = lengths[0]
    pad_row = lambda row: jnp.pad(row[None, :], ((0, 0), (0, model - row.shape[0])))

    w_kv = jnp.concatenate([w_key, w_value], axis=1)
    w_project_t = jnp.concatenate([w_query.T, w_key.T, w_value.T], axis=0)
    gathered = spread_gather(jnp.concatenate([w_in, w_down, w_out], axis=0))
    w_out_all = gathered[:, model + hidden_width : model + hidden_width + width].reshape(
        group_size * width, model
    )
    tile = jnp.concatenate(
        [
            spread_parts(w_project_t),
            w_student.T,
            b_in[None, :],
            pad_row(b_student),
            jnp.zeros((14, model), bf16),
        ],
        axis=0,
    )
    found = send_tiles(tile, group_size)
    hidden_own = lax.dynamic_slice_in_dim(hidden_in, own_start, own_count, 0)
    cot_own = lax.dynamic_slice_in_dim(out_cotangent, own_start, own_count, 0)
    chunk_at = (rank + jnp.arange(group_size, dtype=jnp.int32)) % group_size
    chunk_valid = jnp.clip(length - chunk_at * own_count, 0, own_count)
    half = group_size // 2
    first_empty = (jnp.sum(chunk_valid[:half]) == 0).astype(jnp.int32)
    second_empty = (jnp.sum(chunk_valid[half:]) == 0).astype(jnp.int32)
    info = jnp.concatenate(
        [
            rank[None],
            chunk_valid,
            first_empty[None],
            (2 - first_empty - second_empty)[None],
        ]
    ).astype(jnp.int32)
    bias_t = jnp.concatenate([b_query, jnp.zeros_like(b_query), b_value])
    hidden_rot, wide_k, wide_v, projected_t, norms = project(
        info, hidden_in, w_kv, w_project_t, bias_t[None, width:], bias_t[:, None], group_size
    )

    order = sorted(range(1, group_size), key=lambda s: -min(s, group_size - s))
    outs = [None] * group_size
    lses = [None] * group_size
    attended = [None] * group_size
    for step, s in enumerate(order + [0]):
        outs[s], lses[s] = attend_forward(info, norms, wide_k, projected_t, s, group_size)
        attended[s] = shift(outs[s], s, group_size)
        if step == 0:
            *found, projected_t = lax.optimization_barrier((*found, projected_t))
            tiles = order_tiles(found, rank)
            part = tile.shape[0] - stu_cols - 16
            w_project_all = lax.all_gather(tiles[:, :part], "dp", axis=1, tiled=True)
            stud_tiles = tiles[:, part:]
        if step == 2:
            attended[order[0]], attended[order[1]], projected_t = lax.optimization_barrier(
                (attended[order[0]], attended[order[1]], projected_t)
            )
    w_stud_t = stud_tiles[:, :stu_cols].reshape(group_size * stu_cols, model)
    b_in_all = stud_tiles[:, stu_cols : stu_cols + 1]
    b_stud_all = stud_tiles[:, stu_cols + 1, :stu_cols].reshape(1, group_size * stu_cols)

    attended_t = jnp.zeros((group_size * width, own_count), bf16)
    for s in range(group_size):
        source = (rank - s) % group_size
        attended_t = lax.dynamic_update_slice_in_dim(attended_t, attended[s], source * width, 0)

    resid1 = across_rows(attended_t, w_out_all) + b_out + hidden_own.astype(f32)
    first, normed1, invstd1 = normalize(resid1, ln1_gain, ln1_bias)
    first_low = first.astype(bf16)
    acts, slopes, ffn = ffn_forward(first_low, gathered, b_in_all)
    resid2 = ffn + b_down + first_low.astype(f32)
    second, normed2, invstd2 = normalize(resid2, ln2_gain, ln2_bias)
    second_low = second.astype(bf16)
    held = shift(second_low, 1, group_size)

    student_low = (against(second_low, w_stud_t) + b_stud_all.astype(f32)).astype(bf16)
    student = student_low.astype(f32)
    student_width = student.shape[1]
    head_width = student_width // POOL_HEADS
    probe_scale = 1.0 / math.sqrt(head_width)
    own_rows = own_start + lax.broadcasted_iota(jnp.int32, (own_count, 1), 0)
    row_valid = own_rows < length
    head_of = lax.broadcasted_iota(jnp.int32, (1, student_width), 1) // head_width

    def per_head(values_wide):
        whole = jnp.zeros_like(values_wide)
        for h in range(POOL_HEADS):
            part = jnp.sum(
                jnp.where(head_of == h, values_wide, 0.0), axis=-1, keepdims=True
            )
            whole = jnp.where(head_of == h, part, whole)
        return whole

    probes = pool_query[None, :]
    energies = jnp.where(row_valid, per_head(student * probes) * probe_scale, mask_fill)
    local_top = jnp.max(energies, axis=0, keepdims=True)
    local_weights = jnp.exp(energies - local_top)
    local_total = jnp.sum(local_weights, axis=0, keepdims=True)
    local_pooled = jnp.sum(local_weights * student, axis=0, keepdims=True)
    stats = jnp.concatenate(
        [local_top, local_total, local_pooled, jnp.zeros((5, student_width), f32)], axis=0
    )
    stats_all = jnp.stack([shift(stats, s, group_size) for s in range(group_size)])
    top = jnp.max(stats_all[:, 0], axis=0, keepdims=True)
    fade = jnp.exp(stats_all[:, 0] - top)
    inv_total = 1.0 / jnp.sum(fade * stats_all[:, 1], axis=0, keepdims=True)
    pooled = jnp.sum(fade * stats_all[:, 2], axis=0, keepdims=True) * inv_total
    squashed = jnp.tanh(jnp.dot(pooled, w_pool, precision=highest) + b_pool)
    logits = jnp.dot(squashed, w_class, precision=highest) + b_class
    classes = lax.broadcasted_iota(jnp.int32, logits.shape, 1)
    g_logits = jax.nn.softmax(logits, axis=-1) - (classes == labels[:, None]).astype(f32)
    grad_w_class_t = g_logits.reshape(-1, 1) * squashed
    grad_b_class = g_logits[0]
    g_u = lax.dot_general(
        g_logits, w_class, (((1,), (1,)), ((), ())), precision=highest
    ) * (1.0 - squashed * squashed)
    grad_w_pool = pooled.reshape(-1, 1) * g_u
    grad_b_pool = g_u[0]
    g_pooled = lax.dot_general(g_u, w_pool, (((1,), (1,)), ((), ())), precision=highest)
    inner = per_head(pooled * g_pooled)
    pool = jnp.exp(energies - top) * inv_total
    g_energy = pool * (per_head(student * g_pooled) - inner)
    g_stud_low = (pool * g_pooled + g_energy * probes * probe_scale).astype(bf16)
    grad_pool_query = jnp.sum(g_energy * student, axis=0) * probe_scale

    grad_second = jnp.where(row_valid, cot_own.astype(f32), 0.0) + matmul(g_stud_low, w_stud_t)
    grad_resid2, grad_ln2_gain, grad_ln2_bias = normalize_back(
        grad_second, normed2, invstd2, ln2_gain
    )
    grad_b_down = jnp.sum(grad_resid2, axis=0)
    grad_ffn_low = grad_resid2.astype(bf16)
    grad_pre, grad_first = ffn_backward(grad_ffn_low, gathered, slopes)
    grad_first, held = lax.optimization_barrier((grad_first, held))
    hidden_out = jnp.zeros((slot_len, model), bf16)
    hidden_out = place_rows(hidden_out, second_low, rank, 0, group_size)
    hidden_out = place_rows(hidden_out, held, rank, 1, group_size)
    held = shift(held, 1, group_size)
    grad_first = grad_first + grad_resid2
    grad_resid1, grad_ln1_gain, grad_ln1_bias = normalize_back(
        grad_first, normed1, invstd1, ln1_gain
    )
    grad_b_out = jnp.sum(grad_resid1, axis=0)
    grad_mix = grad_resid1.astype(bf16)
    grad_att_t = against(w_out_all, grad_mix).astype(bf16)
    grad_outs = []
    for s in range(group_size):
        target = (rank - s) % group_size
        piece = lax.dynamic_slice_in_dim(grad_att_t, target * width, width, 0)
        grad_outs.append(shift(piece, -s, group_size))

    only_once = (rank == 0).astype(f32)
    lanes = student_width
    class_count = grad_b_class.shape[0]
    columns = jnp.stack(
        [grad_b_out, grad_ln1_gain, grad_ln1_bias, grad_b_down, grad_ln2_gain, grad_ln2_bias]
    )
    class_share = -(-class_count // group_size)
    grad_w_class_t = jnp.pad(
        grad_w_class_t * only_once, ((0, class_share * group_size - class_count), (0, 0))
    ).reshape(group_size, class_share, lanes)
    tail = jnp.stack(
        [
            grad_b_pool * only_once,
            jnp.pad(grad_b_class, (0, lanes - class_count)) * only_once,
            grad_pool_query,
        ]
    )
    at = model + hidden_width
    small_at = at + width + stu_cols
    dp_size, part = row_parts(small_at + SMALL_ROWS)
    dense = (first_low, grad_pre, acts, grad_ffn_low, attended_t, grad_mix, g_stud_low, second_low)
    blocks = pack_gradients(
        dp_size, part, group_size, dense, columns, grad_w_pool * only_once, grad_w_class_t, tail
    )
    *grad_outs, blocks, w_project_all = lax.optimization_barrier(
        (*grad_outs, blocks, w_project_all)
    )
    reduced = lax.psum_scatter(
        blocks.reshape(dp_size * group_size, part, model), "dp", scatter_dimension=0, tiled=True
    )

    part_of = functools.partial(attend_backward, info, wide_k, wide_v, projected_t, hidden_rot)
    others = (1, group_size)
    own_side = (grad_outs[0][None], outs[0][None], lses[0][None])
    gq_own, gk_others, gv_others = part_of(*own_side, (0, 1), others)
    gq_own, held, grad_outs[1] = lax.optimization_barrier((gq_own, held, grad_outs[1]))
    hidden_out = place_rows(hidden_out, held, rank, 2, group_size)
    held = shift(held, 1, group_size)
    other_side = tuple(jnp.stack(side[1:]) for side in (grad_outs, outs, lses))
    gq_others = None
    w_kv_sum = None
    kv_arrived = {}
    for step, s in enumerate(order):
        gq_others, low, w_kv_sum = part_of(
            *other_side,
            others,
            (s, s + 1),
            gq=gq_others,
            gkv=(gk_others, gv_others),
            wkv=w_kv_sum,
            gkv_at=s - 1,
            end_k=True,
        )
        kv_arrived[s] = shift(low[0], s, group_size)
        if step == 1:
            earlier = order[0]
            reduced, held, gq_others, kv_arrived[earlier] = lax.optimization_barrier(
                (reduced, held, gq_others, kv_arrived[earlier])
            )
            reduced = lax.psum_scatter(reduced, "tensor", scatter_dimension=0, tiled=True)
            hidden_out = place_rows(hidden_out, held, rank, 3, group_size)
    gkv_own = None
    w_q_sum = None
    q_arrived = {}
    for step, s in enumerate(order):
        low, *gkv_own, w_q_sum = part_of(
            grad_outs[s][None],
            outs[s][None],
            lses[s][None],
            (s, s + 1),
            (0, 1),
            gq=gq_others,
            gkv=gkv_own,
            wq=w_q_sum,
            gq_at=s - 1,
            end_q=True,
        )
        q_arrived[s] = shift(low[0], s, group_size)
        if step < 2:
            earlier = order[step + 1]
            kv_arrived[earlier], w_q_sum = lax.optimization_barrier(
                (kv_arrived[earlier], w_q_sum)
            )
    grad_resid1, w_q_sum = lax.optimization_barrier((grad_resid1, w_q_sum))
    grad_in_own = add_input_gradients(
        info, grad_resid1, w_project_all, kv_arrived, {}, f32
    )
    gq_own, reduced, grad_in_own, *arrivals = lax.optimization_barrier(
        (gq_own, reduced, grad_in_own, *q_arrived.values())
    )
    q_arrived = dict(zip(q_arrived, arrivals))
    reduced = lax.all_gather(reduced[0], "dp", axis=0, tiled=True)
    low_q, low_kv, late = part_of(
        *own_side,
        (0, 1),
        (0, 1),
        gq=gq_own,
        gkv=gkv_own,
        wq=w_q_sum,
        wkv=w_kv_sum,
        end_q=True,
        end_k=True,
    )
    late, grad_in_own = exchange_add(late, grad_in_own, 1)
    q_arrived[0] = low_q[0]
    grad_in_own = add_input_gradients(
        info, grad_in_own, w_project_all, {0: low_kv[0]}, q_arrived, bf16
    )
    small_own = reduced[small_at : small_at + SMALL_ROWS]
    passed = [grad_in_own]
    passed.append(shift(passed[-1], 1, group_size))
    late, passed[-1] = exchange_add(late, passed[-1], 2)
    passed[-1], small_own, hidden_out = lax.optimization_barrier(
        (passed[-1], small_own, hidden_out)
    )
    found = send_tiles(small_own[:, : 4 * UNIT], group_size)
    passed.append(shift(passed[-1], 1, group_size))
    distance = 4
    while distance < dp_size:
        late, passed[-1] = exchange_add(late, passed[-1], distance)
        distance *= 2
    grad_in, found, *passed = lax.optimization_barrier((hidden_rot, found, *passed))
    passed.append(shift(passed[-1], 1, group_size))
    for s in range(group_size):
        grad_in = place_rows(grad_in, passed[s], rank, s, group_size)
    late = late.astype(f32)
    small = order_tiles(found, rank).astype(f32)
    small_own = small_own[:, 4 * UNIT :].astype(f32)
    grad_w_pool = small[:, :, :UNIT].reshape(grad_w_pool.shape)
    column_share = -(-columns.size // (UNIT * group_size))
    columns = small[:, :column_share, UNIT : 2 * UNIT].reshape(-1)[: columns.size].reshape(
        columns.shape
    )
    grad_w_class = (
        small[:, :class_share, 2 * UNIT : 3 * UNIT].reshape(-1, lanes)[:class_count].T
    )
    grad_b_pool = small[0, 0, 3 * UNIT :]
    grad_b_class = small[0, 1, 3 * UNIT : 3 * UNIT + class_count]
    grad_pool_query = small[0, 2, 3 * UNIT :]
    grad_b_in = small_own[: hidden_width // UNIT, :UNIT].reshape(-1)
    grad_b_stud = lax.dynamic_slice_in_dim(small_own[0, UNIT:], rank * stu_cols, stu_cols, 0)

    reduced = reduced.astype(f32)
    return (
        hidden_out,
        logits,
        grad_in,
        late[:width, :model].T,
        late[:width, model],
        late[width : 2 * width, :model].T,
        late[2 * width :, :model].T,
        late[2 * width :, model],
        reduced[at : at + width],
        columns[0],
        columns[1],
        columns[2],
        reduced[:model],
        grad_b_in,
        reduced[model:at],
        columns[3],
        columns[4],
        columns[5],
        reduced[at + width : small_at].T,
        grad_b_stud,
        grad_pool_query,
        grad_w_pool,
        grad_b_pool,
        grad_w_class,
        grad_b_class,
    )


def solution(mesh):
    by_dp = P("dp", None)
    cols = P(None, "tensor")
    rows = P("tensor", None)
    cut = P("tensor")
    in_specs = (
        (by_dp, P("dp"), P("dp"), by_dp, cols, cut, cols, cols, cut, rows, P(), P(), P(), cols)
        + (cut, rows, P(), P(), P(), cols, cut, P(), P(), P(), P(), P())
    )
    out_specs = (
        (by_dp, by_dp, by_dp, cols, cut, cols, cols, cut, rows, P(), P(), P(), cols, cut, rows)
        + (P(), P(), P(), cols, cut, P(), P(), P(), P(), P())
    )
    return jax.shard_map(body, mesh=mesh, in_specs=in_specs, out_specs=out_specs, check_vma=False)
```

```python
import functools
import math

import jax
import jax.numpy as jnp
from jax import lax
from jax.experimental import pallas as pl
from jax.experimental.pallas import tpu as pltpu
from jax.sharding import PartitionSpec as P

HD = 64
POOL_HEADS = 2

epsilon = 1e-06
mask_fill = -1e30
highest = lax.Precision.HIGHEST
bf16 = jnp.bfloat16
f32 = jnp.float32
SCORE_SCALE = 1.0 / math.sqrt(HD)
SCORE_SCALE_2 = math.log2(math.e) * SCORE_SCALE
SAFE_SCORE = 50.0
PLANE = 256
UNIT = 128
SMALL_ROWS = 32
VMEM_LIMIT = 60 * 1024 * 1024


def matmul(left, right):
    return jnp.dot(left, right, preferred_element_type=f32)


def across_rows(left, right):
    return lax.dot_general(left, right, (((0,), (0,)), ((), ())), preferred_element_type=f32)


def against(left, right):
    return lax.dot_general(left, right, (((1,), (1,)), ((), ())), preferred_element_type=f32)


def project_kernel(
    width, info_ref, h_ref, wkv_ref, wt_ref, bkv_ref, bt_ref, rot_ref, k_ref, v_ref, t_ref, n_ref
):
    hidden = h_ref[...]
    rot_ref[...] = hidden
    rows = hidden.shape[0]
    valid = info_ref[1 + pl.program_id(0)]
    key_value = (matmul(hidden, wkv_ref[...]) + bkv_ref[...]).astype(bf16)
    row = lax.broadcasted_iota(jnp.int32, (rows, PLANE - width), 0)
    lane = lax.broadcasted_iota(jnp.int32, (rows, PLANE - width), 1)
    k_ref[:, :width] = key_value[:, :width]
    k_ref[:, width:] = jnp.where((lane == 0) & (row >= valid), mask_fill, 0.0).astype(bf16)
    v_ref[:, :width] = key_value[:, width:]
    v_ref[:, width:] = jnp.zeros((rows, PLANE - width), bf16)
    part = lax.broadcasted_iota(jnp.int32, (3 * width, 1), 0)
    scale = jnp.where(part < width, SCORE_SCALE_2, 1.0)
    turned = ((against(wt_ref[...], hidden) + bt_ref[...]) * scale).astype(bf16)
    t_ref[...] = turned
    n_ref[...] = jnp.zeros_like(n_ref)
    for h in range(2 * width // HD):
        rows_h = turned[HD * h : HD * h + HD].astype(f32)
        norms = jnp.sum(rows_h * rows_h, axis=0, keepdims=True)
        n_ref[0, h : h + 1, :] = jnp.broadcast_to(
            jnp.max(norms, axis=1, keepdims=True), (1, UNIT)
        )


def project(info, hidden_in, w_kv, w_all_t, bias_kv, bias_t, chunks):
    slot_len, model = hidden_in.shape
    width = w_all_t.shape[0] // 3
    rows = slot_len // chunks
    whole = lambda c, info_ref: (0, 0)
    return pl.pallas_call(
        functools.partial(project_kernel, width),
        grid_spec=pltpu.PrefetchScalarGridSpec(
            num_scalar_prefetch=1,
            grid=(chunks,),
            in_specs=[
                pl.BlockSpec((rows, model), lambda c, info_ref: ((info_ref[0] + c) % chunks, 0)),
                pl.BlockSpec((model, 2 * width), whole),
                pl.BlockSpec((3 * width, model), whole),
                pl.BlockSpec((1, 2 * width), whole),
                pl.BlockSpec((3 * width, 1), whole),
            ],
            out_specs=[
                pl.BlockSpec((rows, model), lambda c, info_ref: (c, 0)),
                pl.BlockSpec((rows, PLANE), lambda c, info_ref: (c, 0)),
                pl.BlockSpec((rows, PLANE), lambda c, info_ref: (c, 0)),
                pl.BlockSpec((3 * width, rows), lambda c, info_ref: (0, c)),
                pl.BlockSpec((1, 8, UNIT), lambda c, info_ref: (c, 0, 0)),
            ],
        ),
        out_shape=(
            jax.ShapeDtypeStruct((slot_len, model), bf16),
            jax.ShapeDtypeStruct((slot_len, PLANE), bf16),
            jax.ShapeDtypeStruct((slot_len, PLANE), bf16),
            jax.ShapeDtypeStruct((3 * width, slot_len), bf16),
            jax.ShapeDtypeStruct((chunks, 8, UNIT), f32),
        ),
        compiler_params=pltpu.CompilerParams(vmem_limit_bytes=VMEM_LIMIT),
        cost_estimate=pl.CostEstimate(flops=1, bytes_accessed=1, transcendentals=0),
        name="project",
    )(info, hidden_in, w_kv, w_all_t, bias_kv, bias_t)


def forward_kernel(
    bq, bk, heads, info_ref, n_ref, k_ref, qt_ref, vt_ref, ot_ref, lse_ref, head_q, acc
):
    width = HD * heads
    chunks = info_ref.shape[0] - 3
    first_tile = info_ref[1 + chunks]
    tile_count = info_ref[2 + chunks]
    row = lax.broadcasted_iota(jnp.int32, (PLANE, bq), 0)
    for h in range(heads):
        head_q[h] = jnp.where(row == width, 1.0, 0.0).astype(bf16)
    most = jnp.max(n_ref[...], axis=0)
    small_scores = jnp.max(most[:heads] * most[heads : 2 * heads]) < SAFE_SCORE * SAFE_SCORE

    def head_values(h, k0):
        return vt_ref[HD * h : HD * h + HD, pl.ds(k0, bk)]

    def key_tile(step):
        k0 = pl.multiple_of(((first_tile + step) % 2) * bk, bk)
        return k0, k_ref[pl.ds(k0, bk), :]

    def run(key_step, start, finish, steps):
        def query_step(qb, unused):
            q0 = pl.multiple_of(qb * bq, bq)
            for h in range(heads):
                own = slice(HD * h, HD * h + HD)
                head_q[h, own, :] = qt_ref[own, pl.ds(q0, bq)]
            acc[...] = jnp.zeros_like(acc)
            done = lax.fori_loop(0, steps, key_step, start)
            for h in range(heads):
                total, lse = finish(done[h])
                ot_ref[HD * h : HD * h + HD, pl.ds(q0, bq)] = (acc[h] * (1.0 / total)).astype(
                    bf16
                )
                lse_ref[pl.ds(h, 1), pl.ds(q0, bq)] = lse
            return unused

        lax.fori_loop(0, qt_ref.shape[1] // bq, query_step, 0)

    @pl.when(small_scores)
    def unshifted():
        def key_step(step, totals):
            k0, keys = key_tile(step)
            kept = []
            for h in range(heads):
                weights = jnp.exp2(matmul(keys, head_q[h]))
                kept.append(totals[h] + jnp.sum(weights, axis=0, keepdims=True))
                acc[h] += matmul(head_values(h, k0), weights.astype(bf16))
            return tuple(kept)

        start = tuple(jnp.zeros((1, bq), f32) for _ in range(heads))
        run(key_step, start, lambda total: (total, jnp.log2(total)), tile_count)

    @pl.when(jnp.logical_not(small_scores))
    def shifted():
        small = min(512, bk)
        cuts = bk // small

        def key_step(step, carry):
            tile = (first_tile + step // cuts) % 2
            k0 = pl.multiple_of(tile * bk + (step % cuts) * small, small)
            keys = k_ref[pl.ds(k0, small), :]
            kept = []
            for h in range(heads):
                scores = matmul(keys, head_q[h])
                top, total = carry[h]
                new_top = jnp.maximum(top, jnp.max(scores, axis=0, keepdims=True))
                weights = jnp.exp2(scores - new_top)
                fade = jnp.exp2(top - new_top)
                total = fade * total + jnp.sum(weights, axis=0, keepdims=True)
                values_t = vt_ref[HD * h : HD * h + HD, pl.ds(k0, small)]
                acc[h] = fade * acc[h] + matmul(values_t, weights.astype(bf16))
                kept.append((new_top, total))
            return tuple(kept)

        start = tuple(
            (jnp.full((1, bq), mask_fill, f32), jnp.zeros((1, bq), f32)) for _ in range(heads)
        )
        finish = lambda pair: (pair[1], pair[0] + jnp.log2(pair[1]))
        run(key_step, start, finish, tile_count * cuts)


def attend_forward(info, norms, wide_k, projected_t, chunk, chunks):
    slot_len = wide_k.shape[0]
    width = projected_t.shape[0] // 3
    heads = width // HD
    rows = slot_len // chunks
    bq, bk = min(512, rows), slot_len // 2
    pairs = heads * rows * slot_len
    return pl.pallas_call(
        functools.partial(forward_kernel, bq, bk, heads),
        grid=(1,),
        out_shape=(
            jax.ShapeDtypeStruct((width, rows), bf16),
            jax.ShapeDtypeStruct((8, rows), f32),
        ),
        in_specs=[
            pl.BlockSpec(memory_space=pltpu.SMEM),
            pl.BlockSpec(norms.shape, lambda i: (0, 0, 0)),
            pl.BlockSpec((slot_len, PLANE), lambda i: (0, 0)),
            pl.BlockSpec((width, rows), lambda i: (0, chunk)),
            pl.BlockSpec((width, slot_len), lambda i: (2, 0)),
        ],
        out_specs=[
            pl.BlockSpec((width, rows), lambda i: (0, 0)),
            pl.BlockSpec((8, rows), lambda i: (0, 0)),
        ],
        scratch_shapes=[
            pltpu.VMEM((heads, PLANE, bq), bf16),
            pltpu.VMEM((heads, HD, bq), f32),
        ],
        compiler_params=pltpu.CompilerParams(vmem_limit_bytes=VMEM_LIMIT),
        cost_estimate=pl.CostEstimate(flops=1, bytes_accessed=1, transcendentals=0),
        name="attend_forward",
    )(info, norms, wide_k, projected_t, projected_t)


def backward_kernel(bq, heads, q_span, k_span, rows, has, end_q, end_k, *refs):
    width = HD * heads
    one_key = k_span[1] - k_span[0] == 1
    one_query = q_span[1] - q_span[0] == 1
    refs = list(refs)
    info_ref, k_ref, v_ref, kt_ref, qt_ref, got_ref, ot_ref, lse_ref = refs[:8]
    del refs[:8]
    hidden_ref = refs.pop(0) if end_q or end_k else None
    gq_in = refs.pop(0) if "q" in has else None
    gk_in = refs.pop(0) if "k" in has else None
    gv_in = refs.pop(0) if "k" in has else None
    wq_in = refs.pop(0) if "wq" in has else None
    wkv_in = refs.pop(0) if "wkv" in has else None
    gq_out = refs.pop(0)
    gkv_low = refs.pop(0) if end_k else None
    gk = None if end_k else refs.pop(0)
    gv = None if end_k else refs.pop(0)
    w_out_ref = refs.pop(0) if end_q or end_k else None
    head_q, head_go = refs[:2]
    del refs[:2]
    gq = refs.pop(0) if end_q else gq_out
    if end_k:
        gk, gv = refs.pop(0), refs.pop(0)
    gq[...] = jnp.zeros_like(gq) if gq_in is None else gq_in[...]
    gk[...] = jnp.zeros_like(gk) if gk_in is None else gk_in[...]
    gv[...] = jnp.zeros_like(gv) if gv_in is None else gv_in[...]
    row = lax.broadcasted_iota(jnp.int32, (PLANE, bq), 0)
    for h in range(heads):
        head_q[h] = jnp.where(row == width, 1.0, 0.0).astype(bf16)
        head_go[h] = jnp.zeros((PLANE, bq), bf16)

    def chunk_step(q, unused):
        def query_step(qb, inner):
            q0 = pl.multiple_of(qb * bq, bq)
            span = pl.ds(q0, bq)
            first_row = q0 if one_query else q * rows + q0
            all_span = pl.ds(pl.multiple_of(first_row, bq), bq)
            deltas = []
            tops = []
            for h in range(heads):
                own = slice(HD * h, HD * h + HD)
                head_q[h, own, :] = qt_ref[own, all_span]
                grad_out = got_ref[q - q_span[0], own, span]
                head_go[h, own, :] = grad_out
                outs = ot_ref[q - q_span[0], own, span]
                deltas.append(
                    jnp.sum(grad_out.astype(f32) * outs.astype(f32), axis=0, keepdims=True)
                )
                tops.append(lse_ref[q - q_span[0], pl.ds(h, 1), span])

            def key_step(k, innermost):
                @pl.when(info_ref[1 + k] > 0)
                def one_tile():
                    at = k - k_span[0]
                    k0 = pl.multiple_of((at if one_key else k) * rows, rows)
                    keys = k_ref[pl.ds(k0, rows), :]
                    values = v_ref[pl.ds(k0, rows), :]
                    grad_v = None
                    grad_k = None
                    for h in range(heads):
                        own = slice(HD * h, HD * h + HD)
                        scores = matmul(keys, head_q[h])
                        grad_weights = matmul(values, head_go[h])
                        weights = jnp.exp2(scores - tops[h])
                        grad_scores = (weights * (grad_weights - deltas[h])).astype(bf16)
                        more_v = against(weights.astype(bf16), head_go[h])
                        more_k = against(grad_scores, head_q[h])
                        grad_v = more_v if grad_v is None else grad_v + more_v
                        grad_k = more_k if grad_k is None else grad_k + more_k
                        gq[q - q_span[0], own, span] += matmul(
                            kt_ref[own, pl.ds(k0, rows)], grad_scores
                        )
                    gk[at] += grad_k
                    gv[at] += grad_v

                return innermost

            lax.fori_loop(k_span[0], k_span[1], key_step, 0)
            return inner

        lax.fori_loop(0, (info_ref[1 + q] + bq - 1) // bq, query_step, 0)
        return unused

    lax.fori_loop(q_span[0], q_span[1], chunk_step, 0)
    ones = jnp.ones((rows, UNIT), bf16)

    def add_weights(first_row, product, sum_in):
        lead = slice(first_row, first_row + product(ones).shape[0])
        model = hidden_ref.shape[1]
        for lanes, right in ((slice(0, model), hidden_ref[...]), (slice(model, None), ones)):
            value = product(right)
            if sum_in is not None:
                value = value + sum_in[:, lanes]
            w_out_ref[lead, lanes] = value.astype(w_out_ref.dtype)

    if end_q:
        low = (gq[0] * SCORE_SCALE).astype(bf16)
        gq_out[0] = low
        add_weights(0, lambda right: matmul(low, right), wq_in)
    if end_k:
        gkv_low[0, :, :width] = (gk[0, :, :width] * math.log(2.0)).astype(bf16)
        gkv_low[0, :, width:] = gv[0, :, :width].astype(bf16)
        both = gkv_low[0]
        add_weights(
            width if end_q else 0,
            lambda right: lax.dot_general(
                both, right, (((0,), (0,)), ((), ())), preferred_element_type=f32
            ),
            wkv_in,
        )


def attend_backward(
    info,
    wide_k,
    wide_v,
    projected_t,
    hidden_rot,
    grad_out_t,
    out_t,
    lse,
    q_span,
    k_span,
    gq=None,
    gkv=None,
    wq=None,
    wkv=None,
    gq_at=0,
    gkv_at=0,
    end_q=False,
    end_k=False,
):
    chunks = info.shape[0] - 3
    slot_len = wide_k.shape[0]
    width = projected_t.shape[0] // 3
    model = hidden_rot.shape[1]
    heads = width // HD
    rows = slot_len // chunks
    nq, nk = q_span[1] - q_span[0], k_span[1] - k_span[0]
    bq = min(512, rows)
    k_at = k_span[0]
    if nk == 1:
        key_spec = pl.BlockSpec((rows, PLANE), lambda i: (k_at, 0))
        kt_spec = pl.BlockSpec((width, rows), lambda i: (1, k_at))
    else:
        key_spec = pl.BlockSpec((slot_len, PLANE), lambda i: (0, 0))
        kt_spec = pl.BlockSpec((width, slot_len), lambda i: (1, 0))
    q_at = q_span[0]
    if nq == 1:
        qt_spec = pl.BlockSpec((width, rows), lambda i: (0, q_at))
    else:
        qt_spec = pl.BlockSpec((width, slot_len), lambda i: (0, 0))
    at_zero = lambda i: (0, 0, 0)
    gq_shape, gk_shape = (nq, width, rows), (nk, rows, PLANE)
    gq_spec, gk_spec = pl.BlockSpec(gq_shape, at_zero), pl.BlockSpec(gk_shape, at_zero)
    whole2 = lambda array: pl.BlockSpec(array.shape, lambda i: (0, 0))
    operands = [info, wide_k, wide_v, projected_t, projected_t, grad_out_t, out_t, lse]
    in_specs = [
        pl.BlockSpec(memory_space=pltpu.SMEM),
        key_spec,
        key_spec,
        kt_spec,
        qt_spec,
        gq_spec,
        gq_spec,
        pl.BlockSpec((nq, 8, rows), at_zero),
    ]
    has = []
    if end_q or end_k:
        ended = k_at if end_k else q_span[0]
        operands.append(hidden_rot)
        in_specs.append(pl.BlockSpec((rows, model), lambda i: (ended, 0)))
    if gq is not None:
        has.append("q")
        operands.append(gq)
        in_specs.append(pl.BlockSpec(gq_shape, lambda i: (gq_at, 0, 0)))
    if gkv is not None:
        has.append("k")
        operands.extend(gkv)
        in_specs.extend([pl.BlockSpec(gk_shape, lambda i: (gkv_at, 0, 0))] * 2)
    for name, array in (("wq", wq), ("wkv", wkv)):
        if array is not None:
            has.append(name)
            operands.append(array)
            in_specs.append(whole2(array))
    out_shape = [jax.ShapeDtypeStruct(gq_shape, bf16 if end_q else f32)]
    out_specs = [gq_spec]
    scratch = [
        pltpu.VMEM((heads, PLANE, bq), bf16),
        pltpu.VMEM((heads, PLANE, bq), bf16),
    ]
    if end_q:
        scratch.append(pltpu.VMEM(gq_shape, f32))
    if end_k:
        out_shape.append(jax.ShapeDtypeStruct((nk, rows, 2 * width), bf16))
        out_specs.append(pl.BlockSpec((nk, rows, 2 * width), at_zero))
        scratch.extend([pltpu.VMEM(gk_shape, f32)] * 2)
    else:
        out_shape.extend([jax.ShapeDtypeStruct(gk_shape, f32)] * 2)
        out_specs.extend([gk_spec] * 2)
    if end_q or end_k:
        w_rows = width * ((1 if end_q else 0) + (2 if end_k else 0))
        w_shape = (w_rows, model + UNIT)
        out_shape.append(jax.ShapeDtypeStruct(w_shape, bf16 if end_q and end_k else f32))
        out_specs.append(pl.BlockSpec(w_shape, lambda i: (0, 0)))
    pairs = heads * nq * nk * rows * rows
    return pl.pallas_call(
        functools.partial(
            backward_kernel, bq, heads, q_span, k_span, rows, tuple(has), end_q, end_k
        ),
        grid=(1,),
        out_shape=tuple(out_shape),
        in_specs=in_specs,
        out_specs=out_specs,
        scratch_shapes=scratch,
        compiler_params=pltpu.CompilerParams(vmem_limit_bytes=VMEM_LIMIT),
        cost_estimate=pl.CostEstimate(flops=1, bytes_accessed=1, transcendentals=0),
        name="attend_backward",
    )(*operands)


def input_kernel(width, kv_from, q_from, rank_ref, sum_ref, w_ref, *refs):
    out_ref = refs[-1]
    groups = w_ref.shape[0]
    total = sum_ref[...]
    for at, behind in enumerate(kv_from + q_from):
        source = lax.rem(rank_ref[0] + groups - behind, groups)
        if at < len(kv_from):
            total += matmul(refs[at][...], w_ref[source, width : 3 * width, :])
        else:
            total += across_rows(refs[at][...], w_ref[source, :width, :])
    out_ref[...] = total.astype(out_ref.dtype)


def add_input_gradients(info, so_far, w_project_all, kv_pieces, q_pieces, dtype):
    width = next(iter(kv_pieces.values())).shape[1] // 2
    count, model = so_far.shape
    rows = min(256, count)
    pieces = list(kv_pieces.values()) + list(q_pieces.values())
    by_rows = pl.BlockSpec((rows, model), lambda r: (r, 0))
    return pl.pallas_call(
        functools.partial(input_kernel, width, tuple(kv_pieces), tuple(q_pieces)),
        grid=(count // rows,),
        in_specs=[
            pl.BlockSpec(memory_space=pltpu.SMEM),
            by_rows,
            pl.BlockSpec(w_project_all.shape, lambda r: (0, 0, 0)),
        ]
        + [pl.BlockSpec((rows, 2 * width), lambda r: (r, 0))] * len(kv_pieces)
        + [pl.BlockSpec((width, rows), lambda r: (0, r))] * len(q_pieces),
        out_specs=by_rows,
        out_shape=jax.ShapeDtypeStruct(so_far.shape, dtype),
        compiler_params=pltpu.CompilerParams(vmem_limit_bytes=VMEM_LIMIT),
        cost_estimate=pl.CostEstimate(flops=1, bytes_accessed=1, transcendentals=0),
        name="add_input_gradients",
    )(info, so_far, w_project_all, *pieces)


def ffn_forward_kernel(row_step, x_ref, w_in_ref, b_ref, w_down_ref, act_ref, slope_ref, out_ref):
    @pl.when(pl.program_id(0) == 0)
    def start():
        out_ref[...] = jnp.zeros_like(out_ref)

    for r0 in range(0, x_ref.shape[0], row_step):
        rows = slice(r0, r0 + row_step)
        pre = matmul(x_ref[rows, :], w_in_ref[0]) + b_ref[0].astype(f32)
        below = 0.5 + 0.5 * lax.erf(pre * math.sqrt(0.5))
        density = jnp.exp(-0.5 * pre * pre) * (1.0 / math.sqrt(2.0 * math.pi))
        act = (pre * below).astype(bf16)
        act_ref[0, rows, :] = act
        slope_ref[0, rows, :] = (below + pre * density).astype(bf16)
        more = matmul(act, w_down_ref[0])
        out_ref[rows, :] += more


def ffn_forward(first_low, gathered, b_in_all):
    count, model = first_low.shape
    groups = gathered.shape[0]
    units = b_in_all.shape[-1]
    block = pl.BlockSpec((1, count, units), lambda b: (b, 0, 0))
    return pl.pallas_call(
        functools.partial(ffn_forward_kernel, min(256, count)),
        grid=(groups,),
        in_specs=[
            pl.BlockSpec((count, model), lambda b: (0, 0)),
            pl.BlockSpec((1, model, units), lambda b: (b, 0, 0)),
            pl.BlockSpec((1, 1, units), lambda b: (b, 0, 0)),
            pl.BlockSpec((1, units, model), lambda b: (b, 1, 0)),
        ],
        out_specs=[block, block, pl.BlockSpec((count, model), lambda b: (0, 0))],
        out_shape=(
            jax.ShapeDtypeStruct((groups, count, units), bf16),
            jax.ShapeDtypeStruct((groups, count, units), bf16),
            jax.ShapeDtypeStruct((count, model), f32),
        ),
        compiler_params=pltpu.CompilerParams(vmem_limit_bytes=VMEM_LIMIT),
        cost_estimate=pl.CostEstimate(flops=1, bytes_accessed=1, transcendentals=0),
        name="ffn_forward",
    )(first_low, gathered, b_in_all, gathered)


def ffn_backward_kernel(row_step, g_ref, w_in_ref, w_down_ref, slope_ref, pre_ref, out_ref):
    @pl.when(pl.program_id(0) == 0)
    def start():
        out_ref[...] = jnp.zeros_like(out_ref)

    for r0 in range(0, g_ref.shape[0], row_step):
        rows = slice(r0, r0 + row_step)
        grad_act = against(g_ref[rows, :], w_down_ref[0])
        grad_pre = (grad_act * slope_ref[0, rows, :].astype(f32)).astype(bf16)
        pre_ref[0, rows, :] = grad_pre
        more = against(grad_pre, w_in_ref[0])
        out_ref[rows, :] += more


def ffn_backward(grad_ffn_low, gathered, slopes):
    count, model = grad_ffn_low.shape
    groups, _, units = slopes.shape
    block = pl.BlockSpec((1, count, units), lambda b: (b, 0, 0))
    return pl.pallas_call(
        functools.partial(ffn_backward_kernel, min(256, count)),
        grid=(groups,),
        in_specs=[
            pl.BlockSpec((count, model), lambda b: (0, 0)),
            pl.BlockSpec((1, model, units), lambda b: (b, 0, 0)),
            pl.BlockSpec((1, units, model), lambda b: (b, 1, 0)),
            block,
        ],
        out_specs=[block, pl.BlockSpec((count, model), lambda b: (0, 0))],
        out_shape=(
            jax.ShapeDtypeStruct((groups, count, units), bf16),
            jax.ShapeDtypeStruct((count, model), f32),
        ),
        compiler_params=pltpu.CompilerParams(vmem_limit_bytes=VMEM_LIMIT),
        cost_estimate=pl.CostEstimate(flops=1, bytes_accessed=1, transcendentals=0),
        name="ffn_backward",
    )(grad_ffn_low, gathered, gathered, slopes)


def pack_kernel(
    dp_size,
    part,
    first_ref,
    gpre_ref,
    act_ref,
    gffn_ref,
    att_ref,
    gmix_ref,
    gstud_ref,
    second_ref,
    columns_ref,
    pool_ref,
    class_ref,
    tail_ref,
    out_ref,
    stud_acc,
    small,
):
    b = pl.program_id(0)
    at = 0

    def store(rows_value):
        nonlocal at
        done = 0
        count = rows_value.shape[0]
        while done < count:
            d, offset = divmod(at, part)
            take = min(part - offset, count - done)
            out_ref[d, 0, offset : offset + take, :] = rows_value[done : done + take].astype(bf16)
            done += take
            at += take

    store(across_rows(first_ref[...], gpre_ref[0]))
    store(across_rows(act_ref[0], gffn_ref[...]))
    store(matmul(att_ref[...], gmix_ref[...]))
    groups = pl.num_programs(0)
    stud_cols = stud_acc.shape[1]

    @pl.when(b == 0)
    def student():
        whole = across_rows(gstud_ref[...], second_ref[...])
        for i in range(stud_acc.shape[0]):
            stud_acc[i] = whole[i * stud_cols : (i + 1) * stud_cols]

    store(stud_acc[b])
    small[...] = jnp.zeros_like(small)
    small[:, :UNIT] = pool_ref[...]
    units = columns_ref.shape[1] // UNIT
    count = columns_ref.shape[0] * units
    share = -(-count // stud_acc.shape[0])
    for block in range(stud_acc.shape[0]):

        @pl.when(b == block)
        def own_columns():
            for r in range(share):
                u = block * share + r
                if u < count:
                    lanes = slice((u % units) * UNIT, (u % units + 1) * UNIT)
                    small[r : r + 1, UNIT : 2 * UNIT] = columns_ref[
                        u // units : u // units + 1, lanes
                    ]

    small[: class_ref.shape[1], 2 * UNIT : 3 * UNIT] = class_ref[0]

    @pl.when(b == 0)
    def tail_rows():
        small[: tail_ref.shape[0], 3 * UNIT : 4 * UNIT] = tail_ref[...]

    grad_b_in = jnp.sum(gpre_ref[0].astype(f32), axis=0, keepdims=True)
    for u in range(grad_b_in.shape[1] // UNIT):
        small[u : u + 1, 4 * UNIT : 5 * UNIT] = grad_b_in[:, u * UNIT : (u + 1) * UNIT]
    small[0:1, 5 * UNIT : 6 * UNIT] = jnp.sum(gstud_ref[...].astype(f32), axis=0, keepdims=True)
    store(small[...])
    if at < dp_size * part:
        store(jnp.zeros((dp_size * part - at, small.shape[1]), f32))


def pack_gradients(dp_size, part, groups, dense, columns, pool, classes, tail):
    first_low, grad_pre, acts, grad_ffn, attended_t, grad_mix, grad_stud, second_low = dense
    count, model = first_low.shape
    units = acts.shape[2]
    width = attended_t.shape[0] // groups
    students = grad_stud.shape[1]
    stud_cols = students // groups
    rows = lambda cols: pl.BlockSpec((count, cols), lambda b: (0, 0))
    block = pl.BlockSpec((1, count, units), lambda b: (b, 0, 0))
    whole = lambda array: pl.BlockSpec(array.shape, lambda b: (0,) * array.ndim)
    return pl.pallas_call(
        functools.partial(pack_kernel, dp_size, part),
        grid=(groups,),
        in_specs=[
            rows(model),
            block,
            block,
            rows(model),
            pl.BlockSpec((width, count), lambda b: (b, 0)),
            rows(model),
            rows(students),
            rows(model),
            whole(columns),
            pl.BlockSpec((pool.shape[0] // groups, pool.shape[1]), lambda b: (b, 0)),
            pl.BlockSpec((1,) + classes.shape[1:], lambda b: (b, 0, 0)),
            whole(tail),
        ],
        out_specs=pl.BlockSpec((dp_size, 1, part, model), lambda b: (0, b, 0, 0)),
        out_shape=jax.ShapeDtypeStruct((dp_size, groups, part, model), bf16),
        scratch_shapes=[
            pltpu.VMEM((groups, stud_cols, model), f32),
            pltpu.VMEM((SMALL_ROWS, model), f32),
        ],
        compiler_params=pltpu.CompilerParams(vmem_limit_bytes=VMEM_LIMIT),
        cost_estimate=pl.CostEstimate(flops=1, bytes_accessed=1, transcendentals=0),
        name="pack_gradients",
    )(
        first_low,
        grad_pre,
        acts,
        grad_ffn,
        attended_t,
        grad_mix,
        grad_stud,
        second_low,
        columns,
        pool,
        classes,
        tail,
    )


def normalize(resid, gain, shift):
    center = resid - jnp.mean(resid, axis=-1, keepdims=True)
    invstd = lax.rsqrt(jnp.mean(center * center, axis=-1, keepdims=True) + epsilon)
    normed = center * invstd
    return (normed * gain + shift, normed, invstd)


def normalize_back(grad, normed, invstd, gain):
    scaled = grad * gain
    inner = (
        scaled
        - jnp.mean(scaled, axis=-1, keepdims=True)
        - normed * jnp.mean(scaled * normed, axis=-1, keepdims=True)
    )
    return (invstd * inner, jnp.sum(grad * normed, axis=0), jnp.sum(grad, axis=0))


def shift(array, ahead, group_size):
    if ahead % group_size == 0:
        return array
    moves = [(i, (i + ahead) % group_size) for i in range(group_size)]
    return lax.ppermute(array, "tensor", moves)


def send_tiles(tile, group_size):
    return [shift(tile, s, group_size) for s in range(group_size)]


def order_tiles(found, rank):
    tile, group_size = found[0], len(found)
    tiles = jnp.zeros((group_size,) + tile.shape, tile.dtype)
    for s in range(group_size):
        tiles = lax.dynamic_update_index_in_dim(tiles, found[s], (rank - s) % group_size, 0)
    return tiles


def exchange_add(array, other, distance):
    moves = [(i, i ^ distance) for i in range(lax.axis_size("dp"))]
    came = lax.ppermute(array, "dp", moves)
    came, other = lax.optimization_barrier((came, other))
    return (array.astype(f32) + came.astype(f32)).astype(array.dtype), other


def place_rows(whole, rows, rank, behind, group_size):
    source = (rank - behind) % group_size
    return lax.dynamic_update_slice_in_dim(whole, rows, source * rows.shape[0], 0)


def row_parts(rows):
    dp_size = lax.axis_size("dp")
    part = -(-rows // (16 * dp_size)) * 16
    return dp_size, part


def spread_parts(shard):
    dp_size, part = row_parts(shard.shape[0])
    shard = jnp.pad(shard, ((0, part * dp_size - shard.shape[0]), (0, 0)))
    return lax.dynamic_slice_in_dim(shard, lax.axis_index("dp") * part, part, 0)


def body(
    hidden_in,
    lengths,
    labels,
    out_cotangent,
    w_query,
    b_query,
    w_key,
    w_value,
    b_value,
    w_out,
    b_out,
    ln1_gain,
    ln1_bias,
    w_in,
    b_in,
    w_down,
    b_down,
    ln2_gain,
    ln2_bias,
    w_student,
    b_student,
    pool_query,
    w_pool,
    b_pool,
    w_class,
    b_class,
):
    slot_len, model = hidden_in.shape
    group_size = lax.axis_size("tensor")
    own_count = slot_len // group_size
    rank = lax.axis_index("tensor")
    own_start = rank * own_count
    width = w_query.shape[1]
    hidden_width = w_in.shape[1]
    stu_cols = w_student.shape[1]
    length = lengths[0]
    pad_row = lambda row: jnp.pad(row[None, :], ((0, 0), (0, model - row.shape[0])))

    w_kv = jnp.concatenate([w_key, w_value], axis=1)
    w_project_t = jnp.concatenate([w_query.T, w_key.T, w_value.T], axis=0)
    main = send_tiles(spread_parts(jnp.concatenate([w_in, w_down, w_out], axis=0)), group_size)
    tile = jnp.concatenate(
        [
            spread_parts(w_project_t),
            w_student.T,
            b_in[None, :],
            pad_row(b_student),
            jnp.zeros((14, model), bf16),
        ],
        axis=0,
    )
    found = send_tiles(tile, group_size)
    hidden_own = lax.dynamic_slice_in_dim(hidden_in, own_start, own_count, 0)
    cot_own = lax.dynamic_slice_in_dim(out_cotangent, own_start, own_count, 0)
    chunk_at = (rank + jnp.arange(group_size, dtype=jnp.int32)) % group_size
    chunk_valid = jnp.clip(length - chunk_at * own_count, 0, own_count)
    half = group_size // 2
    first_empty = (jnp.sum(chunk_valid[:half]) == 0).astype(jnp.int32)
    second_empty = (jnp.sum(chunk_valid[half:]) == 0).astype(jnp.int32)
    info = jnp.concatenate(
        [
            rank[None],
            chunk_valid,
            first_empty[None],
            (2 - first_empty - second_empty)[None],
        ]
    ).astype(jnp.int32)
    bias_t = jnp.concatenate([b_query, jnp.zeros_like(b_query), b_value])
    hidden_rot, wide_k, wide_v, projected_t, norms = project(
        info, hidden_in, w_kv, w_project_t, bias_t[None, width:], bias_t[:, None], group_size
    )

    order = sorted(range(1, group_size), key=lambda s: -min(s, group_size - s))
    outs = [None] * group_size
    lses = [None] * group_size
    attended = [None] * group_size
    for step, s in enumerate(order + [0]):
        outs[s], lses[s] = attend_forward(info, norms, wide_k, projected_t, s, group_size)
        attended[s] = shift(outs[s], s, group_size)
        if step == 0:
            *main, projected_t = lax.optimization_barrier((*main, projected_t))
            gathered = lax.all_gather(order_tiles(main, rank), "dp", axis=1, tiled=True)
        if step == 1:
            *found, projected_t = lax.optimization_barrier((*found, projected_t))
            tiles = order_tiles(found, rank)
            part = tile.shape[0] - stu_cols - 16
            w_project_all = lax.all_gather(tiles[:, :part], "dp", axis=1, tiled=True)
            stud_tiles = tiles[:, part:]
        if step == 2:
            attended[order[0]], attended[order[1]], projected_t = lax.optimization_barrier(
                (attended[order[0]], attended[order[1]], projected_t)
            )
    w_out_all = gathered[:, model + hidden_width : model + hidden_width + width].reshape(
        group_size * width, model
    )
    w_stud_t = stud_tiles[:, :stu_cols].reshape(group_size * stu_cols, model)
    b_in_all = stud_tiles[:, stu_cols : stu_cols + 1]
    b_stud_all = stud_tiles[:, stu_cols + 1, :stu_cols].reshape(1, group_size * stu_cols)

    attended_t = jnp.zeros((group_size * width, own_count), bf16)
    for s in range(group_size):
        source = (rank - s) % group_size
        attended_t = lax.dynamic_update_slice_in_dim(attended_t, attended[s], source * width, 0)

    resid1 = across_rows(attended_t, w_out_all) + b_out + hidden_own.astype(f32)
    first, normed1, invstd1 = normalize(resid1, ln1_gain, ln1_bias)
    first_low = first.astype(bf16)
    acts, slopes, ffn = ffn_forward(first_low, gathered, b_in_all)
    resid2 = ffn + b_down + first_low.astype(f32)
    second, normed2, invstd2 = normalize(resid2, ln2_gain, ln2_bias)
    second_low = second.astype(bf16)
    held = shift(second_low, 1, group_size)

    student_low = (against(second_low, w_stud_t) + b_stud_all.astype(f32)).astype(bf16)
    student = student_low.astype(f32)
    student_width = student.shape[1]
    head_width = student_width // POOL_HEADS
    probe_scale = 1.0 / math.sqrt(head_width)
    own_rows = own_start + lax.broadcasted_iota(jnp.int32, (own_count, 1), 0)
    row_valid = own_rows < length
    head_of = lax.broadcasted_iota(jnp.int32, (1, student_width), 1) // head_width

    def per_head(values_wide):
        whole = jnp.zeros_like(values_wide)
        for h in range(POOL_HEADS):
            part = jnp.sum(
                jnp.where(head_of == h, values_wide, 0.0), axis=-1, keepdims=True
            )
            whole = jnp.where(head_of == h, part, whole)
        return whole

    probes = pool_query[None, :]
    energies = jnp.where(row_valid, per_head(student * probes) * probe_scale, mask_fill)
    local_top = jnp.max(energies, axis=0, keepdims=True)
    local_weights = jnp.exp(energies - local_top)
    local_total = jnp.sum(local_weights, axis=0, keepdims=True)
    local_pooled = jnp.sum(local_weights * student, axis=0, keepdims=True)
    stats = jnp.concatenate(
        [local_top, local_total, local_pooled, jnp.zeros((5, student_width), f32)], axis=0
    )
    stats_all = jnp.stack([shift(stats, s, group_size) for s in range(group_size)])
    top = jnp.max(stats_all[:, 0], axis=0, keepdims=True)
    fade = jnp.exp(stats_all[:, 0] - top)
    inv_total = 1.0 / jnp.sum(fade * stats_all[:, 1], axis=0, keepdims=True)
    pooled = jnp.sum(fade * stats_all[:, 2], axis=0, keepdims=True) * inv_total
    squashed = jnp.tanh(jnp.dot(pooled, w_pool, precision=highest) + b_pool)
    logits = jnp.dot(squashed, w_class, precision=highest) + b_class
    classes = lax.broadcasted_iota(jnp.int32, logits.shape, 1)
    g_logits = jax.nn.softmax(logits, axis=-1) - (classes == labels[:, None]).astype(f32)
    grad_w_class_t = g_logits.reshape(-1, 1) * squashed
    grad_b_class = g_logits[0]
    g_u = lax.dot_general(
        g_logits, w_class, (((1,), (1,)), ((), ())), precision=highest
    ) * (1.0 - squashed * squashed)
    grad_w_pool = pooled.reshape(-1, 1) * g_u
    grad_b_pool = g_u[0]
    g_pooled = lax.dot_general(g_u, w_pool, (((1,), (1,)), ((), ())), precision=highest)
    inner = per_head(pooled * g_pooled)
    pool = jnp.exp(energies - top) * inv_total
    g_energy = pool * (per_head(student * g_pooled) - inner)
    g_stud_low = (pool * g_pooled + g_energy * probes * probe_scale).astype(bf16)
    grad_pool_query = jnp.sum(g_energy * student, axis=0) * probe_scale

    grad_second = jnp.where(row_valid, cot_own.astype(f32), 0.0) + matmul(g_stud_low, w_stud_t)
    grad_resid2, grad_ln2_gain, grad_ln2_bias = normalize_back(
        grad_second, normed2, invstd2, ln2_gain
    )
    grad_b_down = jnp.sum(grad_resid2, axis=0)
    grad_ffn_low = grad_resid2.astype(bf16)
    grad_pre, grad_first = ffn_backward(grad_ffn_low, gathered, slopes)
    grad_first, held = lax.optimization_barrier((grad_first, held))
    hidden_out = jnp.zeros((slot_len, model), bf16)
    hidden_out = place_rows(hidden_out, second_low, rank, 0, group_size)
    hidden_out = place_rows(hidden_out, held, rank, 1, group_size)
    held = shift(held, 1, group_size)
    grad_first = grad_first + grad_resid2
    grad_resid1, grad_ln1_gain, grad_ln1_bias = normalize_back(
        grad_first, normed1, invstd1, ln1_gain
    )
    grad_b_out = jnp.sum(grad_resid1, axis=0)
    grad_mix = grad_resid1.astype(bf16)
    grad_att_t = against(w_out_all, grad_mix).astype(bf16)
    grad_outs = []
    for s in range(group_size):
        target = (rank - s) % group_size
        piece = lax.dynamic_slice_in_dim(grad_att_t, target * width, width, 0)
        grad_outs.append(shift(piece, -s, group_size))

    only_once = (rank == 0).astype(f32)
    lanes = student_width
    class_count = grad_b_class.shape[0]
    columns = jnp.stack(
        [grad_b_out, grad_ln1_gain, grad_ln1_bias, grad_b_down, grad_ln2_gain, grad_ln2_bias]
    )
    class_share = -(-class_count // group_size)
    grad_w_class_t = jnp.pad(
        grad_w_class_t * only_once, ((0, class_share * group_size - class_count), (0, 0))
    ).reshape(group_size, class_share, lanes)
    tail = jnp.stack(
        [
            grad_b_pool * only_once,
            jnp.pad(grad_b_class, (0, lanes - class_count)) * only_once,
            grad_pool_query,
        ]
    )
    at = model + hidden_width
    small_at = at + width + stu_cols
    dp_size, part = row_parts(small_at + SMALL_ROWS)
    dense = (first_low, grad_pre, acts, grad_ffn_low, attended_t, grad_mix, g_stud_low, second_low)
    blocks = pack_gradients(
        dp_size, part, group_size, dense, columns, grad_w_pool * only_once, grad_w_class_t, tail
    )
    *grad_outs, blocks, w_project_all = lax.optimization_barrier(
        (*grad_outs, blocks, w_project_all)
    )
    reduced = lax.psum_scatter(
        blocks.reshape(dp_size * group_size, part, model), "dp", scatter_dimension=0, tiled=True
    )

    part_of = functools.partial(attend_backward, info, wide_k, wide_v, projected_t, hidden_rot)
    others = (1, group_size)
    own_side = (grad_outs[0][None], outs[0][None], lses[0][None])
    gq_own, gk_others, gv_others = part_of(*own_side, (0, 1), others)
    gq_own, held, grad_outs[1] = lax.optimization_barrier((gq_own, held, grad_outs[1]))
    hidden_out = place_rows(hidden_out, held, rank, 2, group_size)
    held = shift(held, 1, group_size)
    other_side = tuple(jnp.stack(side[1:]) for side in (grad_outs, outs, lses))
    gq_others = None
    w_kv_sum = None
    kv_arrived = {}
    for step, s in enumerate(order):
        gq_others, low, w_kv_sum = part_of(
            *other_side,
            others,
            (s, s + 1),
            gq=gq_others,
            gkv=(gk_others, gv_others),
            wkv=w_kv_sum,
            gkv_at=s - 1,
            end_k=True,
        )
        kv_arrived[s] = shift(low[0], s, group_size)
        if step == 1:
            earlier = order[0]
            reduced, held, gq_others, kv_arrived[earlier] = lax.optimization_barrier(
                (reduced, held, gq_others, kv_arrived[earlier])
            )
            reduced = lax.psum_scatter(reduced, "tensor", scatter_dimension=0, tiled=True)
            hidden_out = place_rows(hidden_out, held, rank, 3, group_size)
    gkv_own = None
    w_q_sum = None
    q_arrived = {}
    for step, s in enumerate(order):
        low, *gkv_own, w_q_sum = part_of(
            grad_outs[s][None],
            outs[s][None],
            lses[s][None],
            (s, s + 1),
            (0, 1),
            gq=gq_others,
            gkv=gkv_own,
            wq=w_q_sum,
            gq_at=s - 1,
            end_q=True,
        )
        q_arrived[s] = shift(low[0], s, group_size)
        if step < 2:
            earlier = order[step + 1]
            kv_arrived[earlier], w_q_sum = lax.optimization_barrier(
                (kv_arrived[earlier], w_q_sum)
            )
    grad_resid1, w_q_sum = lax.optimization_barrier((grad_resid1, w_q_sum))
    grad_in_own = add_input_gradients(
        info, grad_resid1, w_project_all, kv_arrived, {}, f32
    )
    gq_own, reduced, grad_in_own, *arrivals = lax.optimization_barrier(
        (gq_own, reduced, grad_in_own, *q_arrived.values())
    )
    q_arrived = dict(zip(q_arrived, arrivals))
    reduced = lax.all_gather(reduced[0], "dp", axis=0, tiled=True)
    low_q, low_kv, late = part_of(
        *own_side,
        (0, 1),
        (0, 1),
        gq=gq_own,
        gkv=gkv_own,
        wq=w_q_sum,
        wkv=w_kv_sum,
        end_q=True,
        end_k=True,
    )
    late, grad_in_own = exchange_add(late, grad_in_own, 1)
    q_arrived[0] = low_q[0]
    grad_in_own = add_input_gradients(
        info, grad_in_own, w_project_all, {0: low_kv[0]}, q_arrived, bf16
    )
    small_own = reduced[small_at : small_at + SMALL_ROWS]
    passed = [grad_in_own]
    passed.append(shift(passed[-1], 1, group_size))
    late, passed[-1] = exchange_add(late, passed[-1], 2)
    passed[-1], small_own, hidden_out = lax.optimization_barrier(
        (passed[-1], small_own, hidden_out)
    )
    found = send_tiles(small_own[:, : 4 * UNIT], group_size)
    passed.append(shift(passed[-1], 1, group_size))
    distance = 4
    while distance < dp_size:
        late, passed[-1] = exchange_add(late, passed[-1], distance)
        distance *= 2
    grad_in, found, *passed = lax.optimization_barrier((hidden_rot, found, *passed))
    passed.append(shift(passed[-1], 1, group_size))
    for s in range(group_size):
        grad_in = place_rows(grad_in, passed[s], rank, s, group_size)
    late = late.astype(f32)
    small = order_tiles(found, rank).astype(f32)
    small_own = small_own[:, 4 * UNIT :].astype(f32)
    grad_w_pool = small[:, :, :UNIT].reshape(grad_w_pool.shape)
    column_share = -(-columns.size // (UNIT * group_size))
    columns = small[:, :column_share, UNIT : 2 * UNIT].reshape(-1)[: columns.size].reshape(
        columns.shape
    )
    grad_w_class = (
        small[:, :class_share, 2 * UNIT : 3 * UNIT].reshape(-1, lanes)[:class_count].T
    )
    grad_b_pool = small[0, 0, 3 * UNIT :]
    grad_b_class = small[0, 1, 3 * UNIT : 3 * UNIT + class_count]
    grad_pool_query = small[0, 2, 3 * UNIT :]
    grad_b_in = small_own[: hidden_width // UNIT, :UNIT].reshape(-1)
    grad_b_stud = lax.dynamic_slice_in_dim(small_own[0, UNIT:], rank * stu_cols, stu_cols, 0)

    reduced = reduced.astype(f32)
    return (
        hidden_out,
        logits,
        grad_in,
        late[:width, :model].T,
        late[:width, model],
        late[width : 2 * width, :model].T,
        late[2 * width :, :model].T,
        late[2 * width :, model],
        reduced[at : at + width],
        columns[0],
        columns[1],
        columns[2],
        reduced[:model],
        grad_b_in,
        reduced[model:at],
        columns[3],
        columns[4],
        columns[5],
        reduced[at + width : small_at].T,
        grad_b_stud,
        grad_pool_query,
        grad_w_pool,
        grad_b_pool,
        grad_w_class,
        grad_b_class,
    )


def solution(mesh):
    by_dp = P("dp", None)
    cols = P(None, "tensor")
    rows = P("tensor", None)
    cut = P("tensor")
    in_specs = (
        (by_dp, P("dp"), P("dp"), by_dp, cols, cut, cols, cols, cut, rows, P(), P(), P(), cols)
        + (cut, rows, P(), P(), P(), cols, cut, P(), P(), P(), P(), P())
    )
    out_specs = (
        (by_dp, by_dp, by_dp, cols, cut, cols, cols, cut, rows, P(), P(), P(), cols, cut, rows)
        + (P(), P(), P(), cols, cut, P(), P(), P(), P(), P())
    )
    return jax.shard_map(body, mesh=mesh, in_specs=in_specs, out_specs=out_specs, check_vma=False)
```

```python
import functools
import math

import jax
import jax.numpy as jnp
from jax import lax
from jax.experimental import pallas as pl
from jax.experimental.pallas import tpu as pltpu
from jax.sharding import PartitionSpec as P

HD = 64
POOL_HEADS = 2

epsilon = 1e-06
mask_fill = -1e30
highest = lax.Precision.HIGHEST
bf16 = jnp.bfloat16
f32 = jnp.float32
SCORE_SCALE = 1.0 / math.sqrt(HD)
SCORE_SCALE_2 = math.log2(math.e) * SCORE_SCALE
SAFE_SCORE = 50.0
PLANE = 256
UNIT = 128
SMALL_ROWS = 32
VMEM_LIMIT = 60 * 1024 * 1024


def matmul(left, right):
    return jnp.dot(left, right, preferred_element_type=f32)


def across_rows(left, right):
    return lax.dot_general(left, right, (((0,), (0,)), ((), ())), preferred_element_type=f32)


def against(left, right):
    return lax.dot_general(left, right, (((1,), (1,)), ((), ())), preferred_element_type=f32)


def project_kernel(
    width, info_ref, h_ref, wkv_ref, wt_ref, bkv_ref, bt_ref, rot_ref, k_ref, v_ref, t_ref, n_ref
):
    hidden = h_ref[...]
    rot_ref[...] = hidden
    rows = hidden.shape[0]
    valid = info_ref[1 + pl.program_id(0)]
    key_value = (matmul(hidden, wkv_ref[...]) + bkv_ref[...]).astype(bf16)
    row = lax.broadcasted_iota(jnp.int32, (rows, PLANE - width), 0)
    lane = lax.broadcasted_iota(jnp.int32, (rows, PLANE - width), 1)
    k_ref[:, :width] = key_value[:, :width]
    k_ref[:, width:] = jnp.where((lane == 0) & (row >= valid), mask_fill, 0.0).astype(bf16)
    v_ref[:, :width] = key_value[:, width:]
    v_ref[:, width:] = jnp.zeros((rows, PLANE - width), bf16)
    part = lax.broadcasted_iota(jnp.int32, (3 * width, 1), 0)
    scale = jnp.where(part < width, SCORE_SCALE_2, 1.0)
    turned = ((against(wt_ref[...], hidden) + bt_ref[...]) * scale).astype(bf16)
    t_ref[...] = turned
    n_ref[...] = jnp.zeros_like(n_ref)
    for h in range(2 * width // HD):
        rows_h = turned[HD * h : HD * h + HD].astype(f32)
        norms = jnp.sum(rows_h * rows_h, axis=0, keepdims=True)
        n_ref[0, h : h + 1, :] = jnp.broadcast_to(
            jnp.max(norms, axis=1, keepdims=True), (1, UNIT)
        )


def project(info, hidden_in, w_kv, w_all_t, bias_kv, bias_t, chunks):
    slot_len, model = hidden_in.shape
    width = w_all_t.shape[0] // 3
    rows = slot_len // chunks
    whole = lambda c, info_ref: (0, 0)
    return pl.pallas_call(
        functools.partial(project_kernel, width),
        grid_spec=pltpu.PrefetchScalarGridSpec(
            num_scalar_prefetch=1,
            grid=(chunks,),
            in_specs=[
                pl.BlockSpec((rows, model), lambda c, info_ref: ((info_ref[0] + c) % chunks, 0)),
                pl.BlockSpec((model, 2 * width), whole),
                pl.BlockSpec((3 * width, model), whole),
                pl.BlockSpec((1, 2 * width), whole),
                pl.BlockSpec((3 * width, 1), whole),
            ],
            out_specs=[
                pl.BlockSpec((rows, model), lambda c, info_ref: (c, 0)),
                pl.BlockSpec((rows, PLANE), lambda c, info_ref: (c, 0)),
                pl.BlockSpec((rows, PLANE), lambda c, info_ref: (c, 0)),
                pl.BlockSpec((3 * width, rows), lambda c, info_ref: (0, c)),
                pl.BlockSpec((1, 8, UNIT), lambda c, info_ref: (c, 0, 0)),
            ],
        ),
        out_shape=(
            jax.ShapeDtypeStruct((slot_len, model), bf16),
            jax.ShapeDtypeStruct((slot_len, PLANE), bf16),
            jax.ShapeDtypeStruct((slot_len, PLANE), bf16),
            jax.ShapeDtypeStruct((3 * width, slot_len), bf16),
            jax.ShapeDtypeStruct((chunks, 8, UNIT), f32),
        ),
        compiler_params=pltpu.CompilerParams(vmem_limit_bytes=VMEM_LIMIT),
        cost_estimate=pl.CostEstimate(flops=1, bytes_accessed=1, transcendentals=0),
        name="project",
    )(info, hidden_in, w_kv, w_all_t, bias_kv, bias_t)


def forward_kernel(
    bq, bk, heads, info_ref, n_ref, k_ref, qt_ref, vt_ref, ot_ref, lse_ref, head_q, acc
):
    width = HD * heads
    chunks = info_ref.shape[0] - 3
    first_tile = info_ref[1 + chunks]
    tile_count = info_ref[2 + chunks]
    row = lax.broadcasted_iota(jnp.int32, (PLANE, bq), 0)
    for h in range(heads):
        head_q[h] = jnp.where(row == width, 1.0, 0.0).astype(bf16)
    most = jnp.max(n_ref[...], axis=0)
    small_scores = jnp.max(most[:heads] * most[heads : 2 * heads]) < SAFE_SCORE * SAFE_SCORE

    def head_values(h, k0):
        return vt_ref[HD * h : HD * h + HD, pl.ds(k0, bk)]

    def key_tile(step):
        k0 = pl.multiple_of(((first_tile + step) % 2) * bk, bk)
        return k0, k_ref[pl.ds(k0, bk), :]

    def run(key_step, start, finish, steps):
        def query_step(qb, unused):
            q0 = pl.multiple_of(qb * bq, bq)
            for h in range(heads):
                own = slice(HD * h, HD * h + HD)
                head_q[h, own, :] = qt_ref[own, pl.ds(q0, bq)]
            acc[...] = jnp.zeros_like(acc)
            done = lax.fori_loop(0, steps, key_step, start)
            for h in range(heads):
                total, lse = finish(done[h])
                ot_ref[HD * h : HD * h + HD, pl.ds(q0, bq)] = (acc[h] * (1.0 / total)).astype(
                    bf16
                )
                lse_ref[pl.ds(h, 1), pl.ds(q0, bq)] = lse
            return unused

        lax.fori_loop(0, qt_ref.shape[1] // bq, query_step, 0)

    @pl.when(small_scores)
    def unshifted():
        def key_step(step, totals):
            k0, keys = key_tile(step)
            kept = []
            for h in range(heads):
                weights = jnp.exp2(matmul(keys, head_q[h]))
                kept.append(totals[h] + jnp.sum(weights, axis=0, keepdims=True))
                acc[h] += matmul(head_values(h, k0), weights.astype(bf16))
            return tuple(kept)

        start = tuple(jnp.zeros((1, bq), f32) for _ in range(heads))
        run(key_step, start, lambda total: (total, jnp.log2(total)), tile_count)

    @pl.when(jnp.logical_not(small_scores))
    def shifted():
        small = min(512, bk)
        cuts = bk // small

        def key_step(step, carry):
            tile = (first_tile + step // cuts) % 2
            k0 = pl.multiple_of(tile * bk + (step % cuts) * small, small)
            keys = k_ref[pl.ds(k0, small), :]
            kept = []
            for h in range(heads):
                scores = matmul(keys, head_q[h])
                top, total = carry[h]
                new_top = jnp.maximum(top, jnp.max(scores, axis=0, keepdims=True))
                weights = jnp.exp2(scores - new_top)
                fade = jnp.exp2(top - new_top)
                total = fade * total + jnp.sum(weights, axis=0, keepdims=True)
                values_t = vt_ref[HD * h : HD * h + HD, pl.ds(k0, small)]
                acc[h] = fade * acc[h] + matmul(values_t, weights.astype(bf16))
                kept.append((new_top, total))
            return tuple(kept)

        start = tuple(
            (jnp.full((1, bq), mask_fill, f32), jnp.zeros((1, bq), f32)) for _ in range(heads)
        )
        finish = lambda pair: (pair[1], pair[0] + jnp.log2(pair[1]))
        run(key_step, start, finish, tile_count * cuts)


def attend_forward(info, norms, wide_k, projected_t, chunk, chunks):
    slot_len = wide_k.shape[0]
    width = projected_t.shape[0] // 3
    heads = width // HD
    rows = slot_len // chunks
    bq, bk = min(512, rows), slot_len // 2
    pairs = heads * rows * slot_len
    return pl.pallas_call(
        functools.partial(forward_kernel, bq, bk, heads),
        grid=(1,),
        out_shape=(
            jax.ShapeDtypeStruct((width, rows), bf16),
            jax.ShapeDtypeStruct((8, rows), f32),
        ),
        in_specs=[
            pl.BlockSpec(memory_space=pltpu.SMEM),
            pl.BlockSpec(norms.shape, lambda i: (0, 0, 0)),
            pl.BlockSpec((slot_len, PLANE), lambda i: (0, 0)),
            pl.BlockSpec((width, rows), lambda i: (0, chunk)),
            pl.BlockSpec((width, slot_len), lambda i: (2, 0)),
        ],
        out_specs=[
            pl.BlockSpec((width, rows), lambda i: (0, 0)),
            pl.BlockSpec((8, rows), lambda i: (0, 0)),
        ],
        scratch_shapes=[
            pltpu.VMEM((heads, PLANE, bq), bf16),
            pltpu.VMEM((heads, HD, bq), f32),
        ],
        compiler_params=pltpu.CompilerParams(vmem_limit_bytes=VMEM_LIMIT),
        cost_estimate=pl.CostEstimate(flops=1, bytes_accessed=1, transcendentals=0),
        name="attend_forward",
    )(info, norms, wide_k, projected_t, projected_t)


def backward_kernel(bq, heads, q_span, k_span, rows, has, end_q, end_k, *refs):
    width = HD * heads
    one_key = k_span[1] - k_span[0] == 1
    one_query = q_span[1] - q_span[0] == 1
    refs = list(refs)
    info_ref, k_ref, v_ref, kt_ref, qt_ref, got_ref, ot_ref, lse_ref = refs[:8]
    del refs[:8]
    hidden_ref = refs.pop(0) if end_q or end_k else None
    gq_in = refs.pop(0) if "q" in has else None
    gk_in = refs.pop(0) if "k" in has else None
    gv_in = refs.pop(0) if "k" in has else None
    wq_in = refs.pop(0) if "wq" in has else None
    wkv_in = refs.pop(0) if "wkv" in has else None
    gq_out = refs.pop(0)
    gkv_low = refs.pop(0) if end_k else None
    gk = None if end_k else refs.pop(0)
    gv = None if end_k else refs.pop(0)
    w_out_ref = refs.pop(0) if end_q or end_k else None
    head_q, head_go = refs[:2]
    del refs[:2]
    gq = refs.pop(0) if end_q else gq_out
    if end_k:
        gk, gv = refs.pop(0), refs.pop(0)
    gq[...] = jnp.zeros_like(gq) if gq_in is None else gq_in[...]
    gk[...] = jnp.zeros_like(gk) if gk_in is None else gk_in[...]
    gv[...] = jnp.zeros_like(gv) if gv_in is None else gv_in[...]
    row = lax.broadcasted_iota(jnp.int32, (PLANE, bq), 0)
    for h in range(heads):
        head_q[h] = jnp.where(row == width, 1.0, 0.0).astype(bf16)
        head_go[h] = jnp.zeros((PLANE, bq), bf16)

    def chunk_step(q, unused):
        def query_step(qb, inner):
            q0 = pl.multiple_of(qb * bq, bq)
            span = pl.ds(q0, bq)
            first_row = q0 if one_query else q * rows + q0
            all_span = pl.ds(pl.multiple_of(first_row, bq), bq)
            deltas = []
            tops = []
            for h in range(heads):
                own = slice(HD * h, HD * h + HD)
                head_q[h, own, :] = qt_ref[own, all_span]
                grad_out = got_ref[q - q_span[0], own, span]
                head_go[h, own, :] = grad_out
                outs = ot_ref[q - q_span[0], own, span]
                deltas.append(
                    jnp.sum(grad_out.astype(f32) * outs.astype(f32), axis=0, keepdims=True)
                )
                tops.append(lse_ref[q - q_span[0], pl.ds(h, 1), span])

            def key_step(k, innermost):
                @pl.when(info_ref[1 + k] > 0)
                def one_tile():
                    at = k - k_span[0]
                    k0 = pl.multiple_of((at if one_key else k) * rows, rows)
                    keys = k_ref[pl.ds(k0, rows), :]
                    values = v_ref[pl.ds(k0, rows), :]
                    grad_v = None
                    grad_k = None
                    for h in range(heads):
                        own = slice(HD * h, HD * h + HD)
                        scores = matmul(keys, head_q[h])
                        grad_weights = matmul(values, head_go[h])
                        weights = jnp.exp2(scores - tops[h])
                        grad_scores = (weights * (grad_weights - deltas[h])).astype(bf16)
                        more_v = against(weights.astype(bf16), head_go[h])
                        more_k = against(grad_scores, head_q[h])
                        grad_v = more_v if grad_v is None else grad_v + more_v
                        grad_k = more_k if grad_k is None else grad_k + more_k
                        gq[q - q_span[0], own, span] += matmul(
                            kt_ref[own, pl.ds(k0, rows)], grad_scores
                        )
                    gk[at] += grad_k
                    gv[at] += grad_v

                return innermost

            lax.fori_loop(k_span[0], k_span[1], key_step, 0)
            return inner

        lax.fori_loop(0, (info_ref[1 + q] + bq - 1) // bq, query_step, 0)
        return unused

    lax.fori_loop(q_span[0], q_span[1], chunk_step, 0)
    ones = jnp.ones((rows, UNIT), bf16)

    def add_weights(first_row, product, sum_in):
        lead = slice(first_row, first_row + product(ones).shape[0])
        model = hidden_ref.shape[1]
        for lanes, right in ((slice(0, model), hidden_ref[...]), (slice(model, None), ones)):
            value = product(right)
            if sum_in is not None:
                value = value + sum_in[:, lanes]
            w_out_ref[lead, lanes] = value.astype(w_out_ref.dtype)

    if end_q:
        low = (gq[0] * SCORE_SCALE).astype(bf16)
        gq_out[0] = low
        add_weights(0, lambda right: matmul(low, right), wq_in)
    if end_k:
        gkv_low[0, :, :width] = (gk[0, :, :width] * math.log(2.0)).astype(bf16)
        gkv_low[0, :, width:] = gv[0, :, :width].astype(bf16)
        both = gkv_low[0]
        add_weights(
            width if end_q else 0,
            lambda right: lax.dot_general(
                both, right, (((0,), (0,)), ((), ())), preferred_element_type=f32
            ),
            wkv_in,
        )


def attend_backward(
    info,
    wide_k,
    wide_v,
    projected_t,
    hidden_rot,
    grad_out_t,
    out_t,
    lse,
    q_span,
    k_span,
    gq=None,
    gkv=None,
    wq=None,
    wkv=None,
    gq_at=0,
    gkv_at=0,
    end_q=False,
    end_k=False,
):
    chunks = info.shape[0] - 3
    slot_len = wide_k.shape[0]
    width = projected_t.shape[0] // 3
    model = hidden_rot.shape[1]
    heads = width // HD
    rows = slot_len // chunks
    nq, nk = q_span[1] - q_span[0], k_span[1] - k_span[0]
    bq = min(512, rows)
    k_at = k_span[0]
    if nk == 1:
        key_spec = pl.BlockSpec((rows, PLANE), lambda i: (k_at, 0))
        kt_spec = pl.BlockSpec((width, rows), lambda i: (1, k_at))
    else:
        key_spec = pl.BlockSpec((slot_len, PLANE), lambda i: (0, 0))
        kt_spec = pl.BlockSpec((width, slot_len), lambda i: (1, 0))
    q_at = q_span[0]
    if nq == 1:
        qt_spec = pl.BlockSpec((width, rows), lambda i: (0, q_at))
    else:
        qt_spec = pl.BlockSpec((width, slot_len), lambda i: (0, 0))
    at_zero = lambda i: (0, 0, 0)
    gq_shape, gk_shape = (nq, width, rows), (nk, rows, PLANE)
    gq_spec, gk_spec = pl.BlockSpec(gq_shape, at_zero), pl.BlockSpec(gk_shape, at_zero)
    whole2 = lambda array: pl.BlockSpec(array.shape, lambda i: (0, 0))
    operands = [info, wide_k, wide_v, projected_t, projected_t, grad_out_t, out_t, lse]
    in_specs = [
        pl.BlockSpec(memory_space=pltpu.SMEM),
        key_spec,
        key_spec,
        kt_spec,
        qt_spec,
        gq_spec,
        gq_spec,
        pl.BlockSpec((nq, 8, rows), at_zero),
    ]
    has = []
    if end_q or end_k:
        ended = k_at if end_k else q_span[0]
        operands.append(hidden_rot)
        in_specs.append(pl.BlockSpec((rows, model), lambda i: (ended, 0)))
    if gq is not None:
        has.append("q")
        operands.append(gq)
        in_specs.append(pl.BlockSpec(gq_shape, lambda i: (gq_at, 0, 0)))
    if gkv is not None:
        has.append("k")
        operands.extend(gkv)
        in_specs.extend([pl.BlockSpec(gk_shape, lambda i: (gkv_at, 0, 0))] * 2)
    for name, array in (("wq", wq), ("wkv", wkv)):
        if array is not None:
            has.append(name)
            operands.append(array)
            in_specs.append(whole2(array))
    out_shape = [jax.ShapeDtypeStruct(gq_shape, bf16 if end_q else f32)]
    out_specs = [gq_spec]
    scratch = [
        pltpu.VMEM((heads, PLANE, bq), bf16),
        pltpu.VMEM((heads, PLANE, bq), bf16),
    ]
    if end_q:
        scratch.append(pltpu.VMEM(gq_shape, f32))
    if end_k:
        out_shape.append(jax.ShapeDtypeStruct((nk, rows, 2 * width), bf16))
        out_specs.append(pl.BlockSpec((nk, rows, 2 * width), at_zero))
        scratch.extend([pltpu.VMEM(gk_shape, f32)] * 2)
    else:
        out_shape.extend([jax.ShapeDtypeStruct(gk_shape, f32)] * 2)
        out_specs.extend([gk_spec] * 2)
    if end_q or end_k:
        w_rows = width * ((1 if end_q else 0) + (2 if end_k else 0))
        w_shape = (w_rows, model + UNIT)
        out_shape.append(jax.ShapeDtypeStruct(w_shape, bf16 if end_q and end_k else f32))
        out_specs.append(pl.BlockSpec(w_shape, lambda i: (0, 0)))
    pairs = heads * nq * nk * rows * rows
    return pl.pallas_call(
        functools.partial(
            backward_kernel, bq, heads, q_span, k_span, rows, tuple(has), end_q, end_k
        ),
        grid=(1,),
        out_shape=tuple(out_shape),
        in_specs=in_specs,
        out_specs=out_specs,
        scratch_shapes=scratch,
        compiler_params=pltpu.CompilerParams(vmem_limit_bytes=VMEM_LIMIT),
        cost_estimate=pl.CostEstimate(flops=1, bytes_accessed=1, transcendentals=0),
        name="attend_backward",
    )(*operands)


def input_kernel(width, kv_from, q_from, rank_ref, sum_ref, w_ref, *refs):
    out_ref = refs[-1]
    groups = w_ref.shape[0]
    total = sum_ref[...]
    for at, behind in enumerate(kv_from + q_from):
        source = lax.rem(rank_ref[0] + groups - behind, groups)
        if at < len(kv_from):
            total += matmul(refs[at][...], w_ref[source, width : 3 * width, :])
        else:
            total += across_rows(refs[at][...], w_ref[source, :width, :])
    out_ref[...] = total.astype(out_ref.dtype)


def add_input_gradients(info, so_far, w_project_all, kv_pieces, q_pieces, dtype):
    width = next(iter(kv_pieces.values())).shape[1] // 2
    count, model = so_far.shape
    rows = min(256, count)
    pieces = list(kv_pieces.values()) + list(q_pieces.values())
    by_rows = pl.BlockSpec((rows, model), lambda r: (r, 0))
    return pl.pallas_call(
        functools.partial(input_kernel, width, tuple(kv_pieces), tuple(q_pieces)),
        grid=(count // rows,),
        in_specs=[
            pl.BlockSpec(memory_space=pltpu.SMEM),
            by_rows,
            pl.BlockSpec(w_project_all.shape, lambda r: (0, 0, 0)),
        ]
        + [pl.BlockSpec((rows, 2 * width), lambda r: (r, 0))] * len(kv_pieces)
        + [pl.BlockSpec((width, rows), lambda r: (0, r))] * len(q_pieces),
        out_specs=by_rows,
        out_shape=jax.ShapeDtypeStruct(so_far.shape, dtype),
        compiler_params=pltpu.CompilerParams(vmem_limit_bytes=VMEM_LIMIT),
        cost_estimate=pl.CostEstimate(flops=1, bytes_accessed=1, transcendentals=0),
        name="add_input_gradients",
    )(info, so_far, w_project_all, *pieces)


def ffn_forward_kernel(row_step, x_ref, w_in_ref, b_ref, w_down_ref, act_ref, slope_ref, out_ref):
    @pl.when(pl.program_id(0) == 0)
    def start():
        out_ref[...] = jnp.zeros_like(out_ref)

    for r0 in range(0, x_ref.shape[0], row_step):
        rows = slice(r0, r0 + row_step)
        pre = matmul(x_ref[rows, :], w_in_ref[0]) + b_ref[0].astype(f32)
        below = 0.5 + 0.5 * lax.erf(pre * math.sqrt(0.5))
        density = jnp.exp(-0.5 * pre * pre) * (1.0 / math.sqrt(2.0 * math.pi))
        act = (pre * below).astype(bf16)
        act_ref[0, rows, :] = act
        slope_ref[0, rows, :] = (below + pre * density).astype(bf16)
        more = matmul(act, w_down_ref[0])
        out_ref[rows, :] += more


def ffn_forward(first_low, gathered, b_in_all):
    count, model = first_low.shape
    groups = gathered.shape[0]
    units = b_in_all.shape[-1]
    block = pl.BlockSpec((1, count, units), lambda b: (b, 0, 0))
    return pl.pallas_call(
        functools.partial(ffn_forward_kernel, min(256, count)),
        grid=(groups,),
        in_specs=[
            pl.BlockSpec((count, model), lambda b: (0, 0)),
            pl.BlockSpec((1, model, units), lambda b: (b, 0, 0)),
            pl.BlockSpec((1, 1, units), lambda b: (b, 0, 0)),
            pl.BlockSpec((1, units, model), lambda b: (b, 1, 0)),
        ],
        out_specs=[block, block, pl.BlockSpec((count, model), lambda b: (0, 0))],
        out_shape=(
            jax.ShapeDtypeStruct((groups, count, units), bf16),
            jax.ShapeDtypeStruct((groups, count, units), bf16),
            jax.ShapeDtypeStruct((count, model), f32),
        ),
        compiler_params=pltpu.CompilerParams(vmem_limit_bytes=VMEM_LIMIT),
        cost_estimate=pl.CostEstimate(flops=1, bytes_accessed=1, transcendentals=0),
        name="ffn_forward",
    )(first_low, gathered, b_in_all, gathered)


def ffn_backward_kernel(row_step, g_ref, w_in_ref, w_down_ref, slope_ref, pre_ref, out_ref):
    @pl.when(pl.program_id(0) == 0)
    def start():
        out_ref[...] = jnp.zeros_like(out_ref)

    for r0 in range(0, g_ref.shape[0], row_step):
        rows = slice(r0, r0 + row_step)
        grad_act = against(g_ref[rows, :], w_down_ref[0])
        grad_pre = (grad_act * slope_ref[0, rows, :].astype(f32)).astype(bf16)
        pre_ref[0, rows, :] = grad_pre
        more = against(grad_pre, w_in_ref[0])
        out_ref[rows, :] += more


def ffn_backward(grad_ffn_low, gathered, slopes):
    count, model = grad_ffn_low.shape
    groups, _, units = slopes.shape
    block = pl.BlockSpec((1, count, units), lambda b: (b, 0, 0))
    return pl.pallas_call(
        functools.partial(ffn_backward_kernel, min(256, count)),
        grid=(groups,),
        in_specs=[
            pl.BlockSpec((count, model), lambda b: (0, 0)),
            pl.BlockSpec((1, model, units), lambda b: (b, 0, 0)),
            pl.BlockSpec((1, units, model), lambda b: (b, 1, 0)),
            block,
        ],
        out_specs=[block, pl.BlockSpec((count, model), lambda b: (0, 0))],
        out_shape=(
            jax.ShapeDtypeStruct((groups, count, units), bf16),
            jax.ShapeDtypeStruct((count, model), f32),
        ),
        compiler_params=pltpu.CompilerParams(vmem_limit_bytes=VMEM_LIMIT),
        cost_estimate=pl.CostEstimate(flops=1, bytes_accessed=1, transcendentals=0),
        name="ffn_backward",
    )(grad_ffn_low, gathered, gathered, slopes)


def pack_kernel(
    dp_size,
    part,
    first_ref,
    gpre_ref,
    act_ref,
    gffn_ref,
    att_ref,
    gmix_ref,
    gstud_ref,
    second_ref,
    columns_ref,
    pool_ref,
    class_ref,
    tail_ref,
    out_ref,
    stud_acc,
    small,
):
    b = pl.program_id(0)
    at = 0

    def store(rows_value):
        nonlocal at
        done = 0
        count = rows_value.shape[0]
        while done < count:
            d, offset = divmod(at, part)
            take = min(part - offset, count - done)
            out_ref[d, 0, offset : offset + take, :] = rows_value[done : done + take].astype(bf16)
            done += take
            at += take

    store(across_rows(first_ref[...], gpre_ref[0]))
    store(across_rows(act_ref[0], gffn_ref[...]))
    store(matmul(att_ref[...], gmix_ref[...]))
    groups = pl.num_programs(0)
    stud_cols = stud_acc.shape[1]

    @pl.when(b == 0)
    def student():
        whole = across_rows(gstud_ref[...], second_ref[...])
        for i in range(stud_acc.shape[0]):
            stud_acc[i] = whole[i * stud_cols : (i + 1) * stud_cols]

    store(stud_acc[b])
    small[...] = jnp.zeros_like(small)
    small[:, :UNIT] = pool_ref[...]
    units = columns_ref.shape[1] // UNIT
    count = columns_ref.shape[0] * units
    share = -(-count // stud_acc.shape[0])
    for block in range(stud_acc.shape[0]):

        @pl.when(b == block)
        def own_columns():
            for r in range(share):
                u = block * share + r
                if u < count:
                    lanes = slice((u % units) * UNIT, (u % units + 1) * UNIT)
                    small[r : r + 1, UNIT : 2 * UNIT] = columns_ref[
                        u // units : u // units + 1, lanes
                    ]

    small[: class_ref.shape[1], 2 * UNIT : 3 * UNIT] = class_ref[0]

    @pl.when(b == 0)
    def tail_rows():
        small[: tail_ref.shape[0], 3 * UNIT : 4 * UNIT] = tail_ref[...]

    grad_b_in = jnp.sum(gpre_ref[0].astype(f32), axis=0, keepdims=True)
    for u in range(grad_b_in.shape[1] // UNIT):
        small[u : u + 1, 4 * UNIT : 5 * UNIT] = grad_b_in[:, u * UNIT : (u + 1) * UNIT]
    small[0:1, 5 * UNIT : 6 * UNIT] = jnp.sum(gstud_ref[...].astype(f32), axis=0, keepdims=True)
    store(small[...])
    if at < dp_size * part:
        store(jnp.zeros((dp_size * part - at, small.shape[1]), f32))


def pack_gradients(dp_size, part, groups, dense, columns, pool, classes, tail):
    first_low, grad_pre, acts, grad_ffn, attended_t, grad_mix, grad_stud, second_low = dense
    count, model = first_low.shape
    units = acts.shape[2]
    width = attended_t.shape[0] // groups
    students = grad_stud.shape[1]
    stud_cols = students // groups
    rows = lambda cols: pl.BlockSpec((count, cols), lambda b: (0, 0))
    block = pl.BlockSpec((1, count, units), lambda b: (b, 0, 0))
    whole = lambda array: pl.BlockSpec(array.shape, lambda b: (0,) * array.ndim)
    return pl.pallas_call(
        functools.partial(pack_kernel, dp_size, part),
        grid=(groups,),
        in_specs=[
            rows(model),
            block,
            block,
            rows(model),
            pl.BlockSpec((width, count), lambda b: (b, 0)),
            rows(model),
            rows(students),
            rows(model),
            whole(columns),
            pl.BlockSpec((pool.shape[0] // groups, pool.shape[1]), lambda b: (b, 0)),
            pl.BlockSpec((1,) + classes.shape[1:], lambda b: (b, 0, 0)),
            whole(tail),
        ],
        out_specs=pl.BlockSpec((dp_size, 1, part, model), lambda b: (0, b, 0, 0)),
        out_shape=jax.ShapeDtypeStruct((dp_size, groups, part, model), bf16),
        scratch_shapes=[
            pltpu.VMEM((groups, stud_cols, model), f32),
            pltpu.VMEM((SMALL_ROWS, model), f32),
        ],
        compiler_params=pltpu.CompilerParams(vmem_limit_bytes=VMEM_LIMIT),
        cost_estimate=pl.CostEstimate(flops=1, bytes_accessed=1, transcendentals=0),
        name="pack_gradients",
    )(
        first_low,
        grad_pre,
        acts,
        grad_ffn,
        attended_t,
        grad_mix,
        grad_stud,
        second_low,
        columns,
        pool,
        classes,
        tail,
    )


def normalize(resid, gain, shift):
    center = resid - jnp.mean(resid, axis=-1, keepdims=True)
    invstd = lax.rsqrt(jnp.mean(center * center, axis=-1, keepdims=True) + epsilon)
    normed = center * invstd
    return (normed * gain + shift, normed, invstd)


def normalize_back(grad, normed, invstd, gain):
    scaled = grad * gain
    inner = (
        scaled
        - jnp.mean(scaled, axis=-1, keepdims=True)
        - normed * jnp.mean(scaled * normed, axis=-1, keepdims=True)
    )
    return (invstd * inner, jnp.sum(grad * normed, axis=0), jnp.sum(grad, axis=0))


def shift(array, ahead, group_size):
    if ahead % group_size == 0:
        return array
    moves = [(i, (i + ahead) % group_size) for i in range(group_size)]
    return lax.ppermute(array, "tensor", moves)


def send_tiles(tile, group_size):
    return [shift(tile, s, group_size) for s in range(group_size)]


def order_tiles(found, rank):
    tile, group_size = found[0], len(found)
    tiles = jnp.zeros((group_size,) + tile.shape, tile.dtype)
    for s in range(group_size):
        tiles = lax.dynamic_update_index_in_dim(tiles, found[s], (rank - s) % group_size, 0)
    return tiles


def exchange_add(array, other, distance):
    moves = [(i, i ^ distance) for i in range(lax.axis_size("dp"))]
    came = lax.ppermute(array, "dp", moves)
    came, other = lax.optimization_barrier((came, other))
    return (array.astype(f32) + came.astype(f32)).astype(array.dtype), other


def place_rows(whole, rows, rank, behind, group_size):
    source = (rank - behind) % group_size
    return lax.dynamic_update_slice_in_dim(whole, rows, source * rows.shape[0], 0)


def row_parts(rows):
    dp_size = lax.axis_size("dp")
    part = -(-rows // (16 * dp_size)) * 16
    return dp_size, part


def spread_parts(shard):
    dp_size, part = row_parts(shard.shape[0])
    shard = jnp.pad(shard, ((0, part * dp_size - shard.shape[0]), (0, 0)))
    return lax.dynamic_slice_in_dim(shard, lax.axis_index("dp") * part, part, 0)


def body(
    hidden_in,
    lengths,
    labels,
    out_cotangent,
    w_query,
    b_query,
    w_key,
    w_value,
    b_value,
    w_out,
    b_out,
    ln1_gain,
    ln1_bias,
    w_in,
    b_in,
    w_down,
    b_down,
    ln2_gain,
    ln2_bias,
    w_student,
    b_student,
    pool_query,
    w_pool,
    b_pool,
    w_class,
    b_class,
):
    slot_len, model = hidden_in.shape
    group_size = lax.axis_size("tensor")
    own_count = slot_len // group_size
    rank = lax.axis_index("tensor")
    own_start = rank * own_count
    width = w_query.shape[1]
    hidden_width = w_in.shape[1]
    stu_cols = w_student.shape[1]
    length = lengths[0]
    pad_row = lambda row: jnp.pad(row[None, :], ((0, 0), (0, model - row.shape[0])))

    w_kv = jnp.concatenate([w_key, w_value], axis=1)
    w_project_t = jnp.concatenate([w_query.T, w_key.T, w_value.T], axis=0)
    main = send_tiles(spread_parts(jnp.concatenate([w_in, w_down, w_out], axis=0)), group_size)
    tile = jnp.concatenate(
        [
            spread_parts(w_project_t),
            w_student.T,
            b_in[None, :],
            pad_row(b_student),
            jnp.zeros((14, model), bf16),
        ],
        axis=0,
    )
    found = send_tiles(tile, group_size)
    hidden_own = lax.dynamic_slice_in_dim(hidden_in, own_start, own_count, 0)
    cot_own = lax.dynamic_slice_in_dim(out_cotangent, own_start, own_count, 0)
    chunk_at = (rank + jnp.arange(group_size, dtype=jnp.int32)) % group_size
    chunk_valid = jnp.clip(length - chunk_at * own_count, 0, own_count)
    half = group_size // 2
    first_empty = (jnp.sum(chunk_valid[:half]) == 0).astype(jnp.int32)
    second_empty = (jnp.sum(chunk_valid[half:]) == 0).astype(jnp.int32)
    info = jnp.concatenate(
        [
            rank[None],
            chunk_valid,
            first_empty[None],
            (2 - first_empty - second_empty)[None],
        ]
    ).astype(jnp.int32)
    bias_t = jnp.concatenate([b_query, jnp.zeros_like(b_query), b_value])
    hidden_rot, wide_k, wide_v, projected_t, norms = project(
        info, hidden_in, w_kv, w_project_t, bias_t[None, width:], bias_t[:, None], group_size
    )

    order = sorted(range(1, group_size), key=lambda s: -min(s, group_size - s))
    outs = [None] * group_size
    lses = [None] * group_size
    attended = [None] * group_size
    for step, s in enumerate(order + [0]):
        outs[s], lses[s] = attend_forward(info, norms, wide_k, projected_t, s, group_size)
        attended[s] = shift(outs[s], s, group_size)
        if step == 0:
            *main, projected_t = lax.optimization_barrier((*main, projected_t))
            gathered = lax.all_gather(order_tiles(main, rank), "dp", axis=1, tiled=True)
        if step == 1:
            *found, projected_t = lax.optimization_barrier((*found, projected_t))
            tiles = order_tiles(found, rank)
            part = tile.shape[0] - stu_cols - 16
            w_project_all = lax.all_gather(tiles[:, :part], "dp", axis=1, tiled=True)
            stud_tiles = tiles[:, part:]
        if step == 2:
            attended[order[0]], attended[order[1]], projected_t = lax.optimization_barrier(
                (attended[order[0]], attended[order[1]], projected_t)
            )
    w_out_all = gathered[:, model + hidden_width : model + hidden_width + width].reshape(
        group_size * width, model
    )
    w_stud_t = stud_tiles[:, :stu_cols].reshape(group_size * stu_cols, model)
    b_in_all = stud_tiles[:, stu_cols : stu_cols + 1]
    b_stud_all = stud_tiles[:, stu_cols + 1, :stu_cols].reshape(1, group_size * stu_cols)

    attended_t = jnp.zeros((group_size * width, own_count), bf16)
    for s in range(group_size):
        source = (rank - s) % group_size
        attended_t = lax.dynamic_update_slice_in_dim(attended_t, attended[s], source * width, 0)

    resid1 = across_rows(attended_t, w_out_all) + b_out + hidden_own.astype(f32)
    first, normed1, invstd1 = normalize(resid1, ln1_gain, ln1_bias)
    first_low = first.astype(bf16)
    acts, slopes, ffn = ffn_forward(first_low, gathered, b_in_all)
    resid2 = ffn + b_down + first_low.astype(f32)
    second, normed2, invstd2 = normalize(resid2, ln2_gain, ln2_bias)
    second_low = second.astype(bf16)
    held = shift(second_low, 1, group_size)

    student_low = (against(second_low, w_stud_t) + b_stud_all.astype(f32)).astype(bf16)
    student = student_low.astype(f32)
    student_width = student.shape[1]
    head_width = student_width // POOL_HEADS
    probe_scale = 1.0 / math.sqrt(head_width)
    own_rows = own_start + lax.broadcasted_iota(jnp.int32, (own_count, 1), 0)
    row_valid = own_rows < length
    head_of = lax.broadcasted_iota(jnp.int32, (1, student_width), 1) // head_width

    def per_head(values_wide):
        whole = jnp.zeros_like(values_wide)
        for h in range(POOL_HEADS):
            part = jnp.sum(
                jnp.where(head_of == h, values_wide, 0.0), axis=-1, keepdims=True
            )
            whole = jnp.where(head_of == h, part, whole)
        return whole

    probes = pool_query[None, :]
    energies = jnp.where(row_valid, per_head(student * probes) * probe_scale, mask_fill)
    local_top = jnp.max(energies, axis=0, keepdims=True)
    local_weights = jnp.exp(energies - local_top)
    local_total = jnp.sum(local_weights, axis=0, keepdims=True)
    local_pooled = jnp.sum(local_weights * student, axis=0, keepdims=True)
    stats = jnp.concatenate(
        [local_top, local_total, local_pooled, jnp.zeros((5, student_width), f32)], axis=0
    )
    stats_all = jnp.stack([shift(stats, s, group_size) for s in range(group_size)])
    top = jnp.max(stats_all[:, 0], axis=0, keepdims=True)
    fade = jnp.exp(stats_all[:, 0] - top)
    inv_total = 1.0 / jnp.sum(fade * stats_all[:, 1], axis=0, keepdims=True)
    pooled = jnp.sum(fade * stats_all[:, 2], axis=0, keepdims=True) * inv_total
    squashed = jnp.tanh(jnp.dot(pooled, w_pool, precision=highest) + b_pool)
    logits = jnp.dot(squashed, w_class, precision=highest) + b_class
    classes = lax.broadcasted_iota(jnp.int32, logits.shape, 1)
    g_logits = jax.nn.softmax(logits, axis=-1) - (classes == labels[:, None]).astype(f32)
    grad_w_class_t = g_logits.reshape(-1, 1) * squashed
    grad_b_class = g_logits[0]
    g_u = lax.dot_general(
        g_logits, w_class, (((1,), (1,)), ((), ())), precision=highest
    ) * (1.0 - squashed * squashed)
    grad_w_pool = pooled.reshape(-1, 1) * g_u
    grad_b_pool = g_u[0]
    g_pooled = lax.dot_general(g_u, w_pool, (((1,), (1,)), ((), ())), precision=highest)
    inner = per_head(pooled * g_pooled)
    pool = jnp.exp(energies - top) * inv_total
    g_energy = pool * (per_head(student * g_pooled) - inner)
    g_stud_low = (pool * g_pooled + g_energy * probes * probe_scale).astype(bf16)
    grad_pool_query = jnp.sum(g_energy * student, axis=0) * probe_scale

    grad_second = jnp.where(row_valid, cot_own.astype(f32), 0.0) + matmul(g_stud_low, w_stud_t)
    grad_resid2, grad_ln2_gain, grad_ln2_bias = normalize_back(
        grad_second, normed2, invstd2, ln2_gain
    )
    grad_b_down = jnp.sum(grad_resid2, axis=0)
    grad_ffn_low = grad_resid2.astype(bf16)
    grad_pre, grad_first = ffn_backward(grad_ffn_low, gathered, slopes)
    grad_first, held = lax.optimization_barrier((grad_first, held))
    hidden_out = jnp.zeros((slot_len, model), bf16)
    hidden_out = place_rows(hidden_out, second_low, rank, 0, group_size)
    hidden_out = place_rows(hidden_out, held, rank, 1, group_size)
    held = shift(held, 1, group_size)
    grad_first = grad_first + grad_resid2
    grad_resid1, grad_ln1_gain, grad_ln1_bias = normalize_back(
        grad_first, normed1, invstd1, ln1_gain
    )
    grad_b_out = jnp.sum(grad_resid1, axis=0)
    grad_mix = grad_resid1.astype(bf16)
    grad_att_t = against(w_out_all, grad_mix).astype(bf16)
    grad_outs = []
    for s in range(group_size):
        target = (rank - s) % group_size
        piece = lax.dynamic_slice_in_dim(grad_att_t, target * width, width, 0)
        grad_outs.append(shift(piece, -s, group_size))

    only_once = (rank == 0).astype(f32)
    lanes = student_width
    class_count = grad_b_class.shape[0]
    columns = jnp.stack(
        [grad_b_out, grad_ln1_gain, grad_ln1_bias, grad_b_down, grad_ln2_gain, grad_ln2_bias]
    )
    class_share = -(-class_count // group_size)
    grad_w_class_t = jnp.pad(
        grad_w_class_t * only_once, ((0, class_share * group_size - class_count), (0, 0))
    ).reshape(group_size, class_share, lanes)
    tail = jnp.stack(
        [
            grad_b_pool * only_once,
            jnp.pad(grad_b_class, (0, lanes - class_count)) * only_once,
            grad_pool_query,
        ]
    )
    at = model + hidden_width
    small_at = at + width + stu_cols
    dp_size, part = row_parts(small_at + SMALL_ROWS)
    dense = (first_low, grad_pre, acts, grad_ffn_low, attended_t, grad_mix, g_stud_low, second_low)
    blocks = pack_gradients(
        dp_size, part, group_size, dense, columns, grad_w_pool * only_once, grad_w_class_t, tail
    )
    *grad_outs, blocks, w_project_all = lax.optimization_barrier(
        (*grad_outs, blocks, w_project_all)
    )
    reduced = lax.psum_scatter(
        blocks.reshape(dp_size * group_size, part, model), "dp", scatter_dimension=0, tiled=True
    )

    part_of = functools.partial(attend_backward, info, wide_k, wide_v, projected_t, hidden_rot)
    others = (1, group_size)
    own_side = (grad_outs[0][None], outs[0][None], lses[0][None])
    gq_own, gk_others, gv_others = part_of(*own_side, (0, 1), others)
    gq_own, held, grad_outs[1] = lax.optimization_barrier((gq_own, held, grad_outs[1]))
    hidden_out = place_rows(hidden_out, held, rank, 2, group_size)
    held = shift(held, 1, group_size)
    other_side = tuple(jnp.stack(side[1:]) for side in (grad_outs, outs, lses))
    gq_others = None
    w_kv_sum = None
    kv_arrived = {}
    for step, s in enumerate(order):
        gq_others, low, w_kv_sum = part_of(
            *other_side,
            others,
            (s, s + 1),
            gq=gq_others,
            gkv=(gk_others, gv_others),
            wkv=w_kv_sum,
            gkv_at=s - 1,
            end_k=True,
        )
        kv_arrived[s] = shift(low[0], s, group_size)
        if step == 1:
            earlier = order[0]
            reduced, held, gq_others, kv_arrived[earlier] = lax.optimization_barrier(
                (reduced, held, gq_others, kv_arrived[earlier])
            )
            reduced = lax.psum_scatter(reduced, "tensor", scatter_dimension=0, tiled=True)
            hidden_out = place_rows(hidden_out, held, rank, 3, group_size)
    gkv_own = None
    w_q_sum = None
    q_arrived = {}
    for step, s in enumerate(order):
        low, *gkv_own, w_q_sum = part_of(
            grad_outs[s][None],
            outs[s][None],
            lses[s][None],
            (s, s + 1),
            (0, 1),
            gq=gq_others,
            gkv=gkv_own,
            wq=w_q_sum,
            gq_at=s - 1,
            end_q=True,
        )
        q_arrived[s] = shift(low[0], s, group_size)
        if step < 2:
            earlier = order[step + 1]
            kv_arrived[earlier], w_q_sum = lax.optimization_barrier(
                (kv_arrived[earlier], w_q_sum)
            )
    grad_resid1, w_q_sum = lax.optimization_barrier((grad_resid1, w_q_sum))
    grad_in_own = add_input_gradients(
        info, grad_resid1, w_project_all, kv_arrived, {}, f32
    )
    early = order[:2]
    gq_own, reduced, grad_in_own, *arrivals = lax.optimization_barrier(
        (gq_own, reduced, grad_in_own, *(q_arrived[s] for s in early))
    )
    q_arrived.update(zip(early, arrivals))
    reduced = lax.all_gather(reduced[0], "dp", axis=0, tiled=True)
    low_q, low_kv, late = part_of(
        *own_side,
        (0, 1),
        (0, 1),
        gq=gq_own,
        gkv=gkv_own,
        wq=w_q_sum,
        wkv=w_kv_sum,
        end_q=True,
        end_k=True,
    )
    low_q, q_arrived[order[2]] = lax.optimization_barrier((low_q, q_arrived[order[2]]))
    q_arrived[0] = low_q[0]
    grad_in_own = add_input_gradients(
        info, grad_in_own, w_project_all, {0: low_kv[0]}, q_arrived, bf16
    )
    late, grad_in_own = lax.optimization_barrier((late, grad_in_own))
    small_own = reduced[small_at : small_at + SMALL_ROWS]
    passed = [grad_in_own]
    passed.append(shift(passed[-1], 1, group_size))
    late, passed[-1] = exchange_add(late, passed[-1], 1)
    passed[-1], small_own, hidden_out = lax.optimization_barrier(
        (passed[-1], small_own, hidden_out)
    )
    found = send_tiles(small_own[:, : 4 * UNIT], group_size)
    passed.append(shift(passed[-1], 1, group_size))
    late, passed[-1] = exchange_add(late, passed[-1], 2)
    grad_in, found, *passed = lax.optimization_barrier((hidden_rot, found, *passed))
    passed.append(shift(passed[-1], 1, group_size))
    distance = 4
    while distance < dp_size:
        late, grad_in = exchange_add(late, grad_in, distance)
        distance *= 2
    for s in range(group_size):
        grad_in = place_rows(grad_in, passed[s], rank, s, group_size)
    late = late.astype(f32)
    small = order_tiles(found, rank).astype(f32)
    small_own = small_own[:, 4 * UNIT :].astype(f32)
    grad_w_pool = small[:, :, :UNIT].reshape(grad_w_pool.shape)
    column_share = -(-columns.size // (UNIT * group_size))
    columns = small[:, :column_share, UNIT : 2 * UNIT].reshape(-1)[: columns.size].reshape(
        columns.shape
    )
    grad_w_class = (
        small[:, :class_share, 2 * UNIT : 3 * UNIT].reshape(-1, lanes)[:class_count].T
    )
    grad_b_pool = small[0, 0, 3 * UNIT :]
    grad_b_class = small[0, 1, 3 * UNIT : 3 * UNIT + class_count]
    grad_pool_query = small[0, 2, 3 * UNIT :]
    grad_b_in = small_own[: hidden_width // UNIT, :UNIT].reshape(-1)
    grad_b_stud = lax.dynamic_slice_in_dim(small_own[0, UNIT:], rank * stu_cols, stu_cols, 0)

    reduced = reduced.astype(f32)
    return (
        hidden_out,
        logits,
        grad_in,
        late[:width, :model].T,
        late[:width, model],
        late[width : 2 * width, :model].T,
        late[2 * width :, :model].T,
        late[2 * width :, model],
        reduced[at : at + width],
        columns[0],
        columns[1],
        columns[2],
        reduced[:model],
        grad_b_in,
        reduced[model:at],
        columns[3],
        columns[4],
        columns[5],
        reduced[at + width : small_at].T,
        grad_b_stud,
        grad_pool_query,
        grad_w_pool,
        grad_b_pool,
        grad_w_class,
        grad_b_class,
    )


def solution(mesh):
    by_dp = P("dp", None)
    cols = P(None, "tensor")
    rows = P("tensor", None)
    cut = P("tensor")
    in_specs = (
        (by_dp, P("dp"), P("dp"), by_dp, cols, cut, cols, cols, cut, rows, P(), P(), P(), cols)
        + (cut, rows, P(), P(), P(), cols, cut, P(), P(), P(), P(), P())
    )
    out_specs = (
        (by_dp, by_dp, by_dp, cols, cut, cols, cols, cut, rows, P(), P(), P(), cols, cut, rows)
        + (P(), P(), P(), cols, cut, P(), P(), P(), P(), P())
    )
    return jax.shard_map(body, mesh=mesh, in_specs=in_specs, out_specs=out_specs, check_vma=False)
```
